128 devices in a mesh: sub: 16 (over z, x), grp: 8 (over y, core).
Axes of the slice: x: 4, y: 4, z: 4, core: 2. Of those that a mesh axis runs over, the one named last changes fastest.
Arguments:
- rhs: float32 [8, 64, 256, 256], P('grp', 'sub')
- counts: int32 [8, 64], P('grp', 'sub'), may hold values from 64 to 256, as said below
- solve_panel: bfloat16 [8, 64, 512, 512], P('grp', 'sub'), as said below
- dirichlet_panel: bfloat16 [8, 64, 512, 512], P('grp', 'sub'), as said below
- coupling: float32 [8, 64, 32, 512], P('grp', 'sub'), may hold values from -0.25 to 0.25
- corner_map: int32 [8, 64, 32], P('grp', 'sub'), may hold values from 0 to 2047
- coarse_inverse: float32 [16, 2048, 2048], P('sub', 'grp'), as said below
Outputs:
- multipliers: float32 [8, 64, 256, 256], P('grp', 'sub')
- residual: float32 [8, 64, 256, 256], P('grp', 'sub')
The draws below stay inside these ranges and needn't reach their ends.
Inputs may be any that keep to these rules, and one draw needn't show every extreme that they name: `counts`: some pair has all 256 unknowns constrained. `solve_panel`: each panel is symmetric positive definite. `dirichlet_panel`: each panel is symmetric positive definite. `coarse_inverse`: each slab's matrix is symmetric positive definite.
All inputs are finite; a program needn't handle non-finite values.
Results may differ from the reference program's by a relative error of at most 0.0003.
Values sent between devices are 32-bit elements; how exact they have to be, the bound alone decides.
A program may use at most 128 MiB of HBM per device.

```python
import math
import jax
import jax.numpy as jnp
from jax import lax

P_SIZE = 512
H = 256
NC = 32
R = 256
ITERS = 3
CHAIN = 64
SECTORS = 8
SLABS = 16
NCO = 2048


def gram_block(key, order):
    key_mix, key_scale = jax.random.split(key)
    mixing = jax.random.randint(key_mix, (order, order), -3, 4).astype(jnp.float32)
    gram = jnp.dot(mixing, mixing.T, precision=lax.Precision.HIGHEST) * (0.25 / order)
    scales = jnp.exp(jax.random.uniform(key_scale, (order,), jnp.float32, 0.0, math.log(1.7)))
    outer = scales[:, None] * scales[None, :]
    eye = jnp.eye(order, dtype=jnp.float32)
    return (gram + 0.5 * eye) * outer


def panel_stack(key):

    def one_sector(index):
        keys = jax.random.split(jax.random.fold_in(key, index), CHAIN)
        blocks = jax.vmap(lambda single: gram_block(single, P_SIZE))(keys)
        return blocks.astype(jnp.bfloat16)
    return lax.map(one_sector, jnp.arange(SECTORS))


def draw_solve_panel(key, part):
    return panel_stack(jax.random.fold_in(key, 11))


def draw_dirichlet_panel(key, part):
    return panel_stack(jax.random.fold_in(key, 23))


def draw_coarse_inverse(key, part):
    base = jax.random.fold_in(key, 37)
    return lax.map(lambda index: gram_block(jax.random.fold_in(base, index), NCO), jnp.arange(SLABS))


def draw_counts(key, part):
    values = jax.random.randint(jax.random.fold_in(key, 41), (SECTORS, CHAIN), H // 4, H + 1)
    return values.at[0, 0].set(H).astype(jnp.int32)


def draw_rhs(key, part):
    key_main = jax.random.fold_in(jax.random.fold_in(key, 53), 0)
    rising = 3.0 ** (jnp.arange(CHAIN, dtype=jnp.float32) / max(CHAIN - 1, 1))
    rising = rising[None, :, None, None]
    base = jax.random.normal(key_main, (SECTORS, CHAIN, R, H), jnp.float32)
    return jnp.clip(base, -6.0, 6.0) * rising


def plant(values, stream_key, smallest, largest):
    longest = values.shape.index(max(values.shape))
    spots = []
    for shift in (0, 1):
        where = [jax.random.randint(jax.random.fold_in(stream_key, axis), (), 0, length) for axis, length in enumerate(values.shape)]
        where[longest] = (where[longest] + shift) % values.shape[longest]
        spots.append(tuple(where))
    return values.at[spots[0]].set(smallest).at[spots[1]].set(largest)


def steps_of(own_key, dims, shards, smallest, top_value):
    gain, own = 1.0, jax.random.fold_in(own_key, 6)
    for axis_at, shards_of in shards:
        draws = jnp.exp(jax.random.uniform(jax.random.fold_in(own, axis_at), (shards_of,), jnp.float32, smallest / len(shards), top_value / len(shards)))
        gain = gain * jnp.repeat(draws, dims[axis_at] // shards_of).reshape([-1 if axis == axis_at else 1 for axis in range(len(dims))])
    return gain


def normal_values(rng, extent, deviation, most, shards=(), kind=jnp.bfloat16):
    values = deviation * jax.random.normal(rng, extent, jnp.float32)
    if shards:
        values = values * steps_of(rng, extent, shards, -0.22, 0.18)
    return jnp.clip(values, -most, most).astype(kind)


def setup_inputs(seed: int = 0) -> dict:
    splits = jax.random.split(jax.random.key(seed), 8)
    rhs = draw_rhs(jax.random.fold_in(splits[7], 71), 0)
    counts = draw_counts(jax.random.fold_in(splits[7], 71), 0)
    solve_panel = draw_solve_panel(jax.random.fold_in(splits[7], 71), 0)
    dirichlet_panel = draw_dirichlet_panel(jax.random.fold_in(splits[7], 71), 0)
    coupling = normal_values(splits[4], (SECTORS, CHAIN, NC, P_SIZE), P_SIZE ** -0.5, 0.25, ((0, 8), (1, 16)), jnp.float32)
    corner_map = plant(jax.random.randint(splits[5], (SECTORS, CHAIN, NC), 0, NCO), jax.random.fold_in(splits[5], 1), 0, NCO - 1).astype(jnp.int32)
    coarse_inverse = draw_coarse_inverse(jax.random.fold_in(splits[7], 71), 0)
    return dict(rhs=rhs, counts=counts, solve_panel=solve_panel, dirichlet_panel=dirichlet_panel, coupling=coupling, corner_map=corner_map, coarse_inverse=coarse_inverse)


HIGH = lax.Precision.HIGHEST


def spread_faces(values):
    prior = jnp.concatenate([jnp.zeros_like(values[:, :1]), values[:, :-1]], axis=1)
    return jnp.concatenate([-prior, values], axis=3)


def face_jump(result, live_mask):
    width = result.shape[3] // 2
    following = jnp.concatenate([result[:, 1:, :, :width], jnp.zeros_like(result[:, :1, :, :width])], axis=1)
    return live_mask * (result[..., width:] - following)


def panel_apply(panel, face_vals):
    def one_sector(pair):
        block, vals = pair
        return jnp.einsum("crp,cqp->crq", vals, block.astype(jnp.float32), precision=HIGH)
    return lax.map(one_sector, (panel, face_vals))


def coarse_apply(face_vals, coupling, corner_map, coarse_inverse):
    sectors, chain, corners = corner_map.shape
    slabs, size = coarse_inverse.shape[0], coarse_inverse.shape[1]
    loads = face_vals.shape[2]
    corner_vals = jnp.einsum("gcrp,gckp->gcrk", face_vals, coupling, precision=HIGH)
    onehot = (corner_map[..., None] == jnp.arange(size, dtype=jnp.int32)).astype(jnp.float32)
    onehot = onehot.reshape(sectors, slabs, chain // slabs, corners, size)
    corner_vals = corner_vals.reshape(sectors, slabs, chain // slabs, loads, corners)
    totals = jnp.einsum("gaskn,gasrk->anr", onehot, corner_vals, precision=HIGH)
    solved = jnp.einsum("amn,anr->amr", coarse_inverse, totals, precision=HIGH)
    back = jnp.einsum("gaskn,anr->gasrk", onehot, solved, precision=HIGH)
    back = back.reshape(sectors, chain, loads, corners)
    return jnp.einsum("gcrk,gckp->gcrp", back, coupling, precision=HIGH)


def reference(rhs, counts, solve_panel, dirichlet_panel, coupling, corner_map, coarse_inverse):
    sectors, chain, loads, width = rhs.shape
    positions = jnp.arange(width, dtype=jnp.int32)
    not_last = (jnp.arange(chain, dtype=jnp.int32) != chain - 1)
    live = (positions[None, None, :] < counts[:, :, None]) & not_last[None, :, None]
    live_mask = live.astype(jnp.float32)[:, :, None, :]

    def apply_dual(values):
        face_vals = spread_faces(values)
        result = panel_apply(solve_panel, face_vals) + coarse_apply(face_vals, coupling, corner_map, coarse_inverse)
        return face_jump(result, live_mask)

    def precondition(values):
        return 0.25 * face_jump(panel_apply(dirichlet_panel, spread_faces(values)), live_mask)

    def inner(first, second):
        return jnp.sum(first * second, axis=(0, 1, 3))

    def expand(scalars):
        return scalars[None, None, :, None]

    multipliers = jnp.zeros_like(rhs)
    residual = live_mask * rhs
    precond = precondition(residual)
    direction = precond
    rz_now = inner(residual, precond)
    for step in range(ITERS):
        image = apply_dual(direction)
        alpha = rz_now / inner(direction, image)
        multipliers = multipliers + expand(alpha) * direction
        residual = residual - expand(alpha) * image
        if step + 1 < ITERS:
            precond = precondition(residual)
            rz_next = inner(residual, precond)
            direction = precond + expand(rz_next / rz_now) * direction
            rz_now = rz_next
    return multipliers, residual
```

```python
import jax
import jax.numpy as jnp
from jax import lax
from jax.experimental import pallas as pl
from jax.experimental.pallas import tpu as pltpu
from jax.sharding import PartitionSpec as P

MESH = pl.DeviceIdType.MESH
F32, BF16, I32 = jnp.float32, jnp.bfloat16, jnp.int32
NSUB, NGRP, NY = 16, 8, 4
SUBS, H, PS, NC, NCO = 4, 256, 512, 32, 2048
LANES, CHUNKS, PAIRS = 128, 2, 5
OWN = SUBS * NC
LEFT, RIGHT = 0, 1


def remote(src, dst, send_sem, recv_sem, device):
    return pltpu.make_async_remote_copy(
        src_ref=src,
        dst_ref=dst,
        send_sem=send_sem,
        recv_sem=recv_sem,
        device_id=device,
        device_id_type=MESH,
    )


def split(value):
    high = value.astype(BF16)
    low = (value - high.astype(F32)).astype(BF16)
    return high, low


def colsum(value):
    return jnp.sum(value, axis=0, keepdims=True)


def chunks(body):
    def step(k, carry):
        body(k)
        return carry

    lax.fori_loop(0, CHUNKS, step, 0)


def block(i):
    return pl.ds(H * i, H)


def kernel(
    rhs_h, counts_s, solve_h, dirichlet_h, coupling_h, map_h, coarse_h, x_h, res_h,
    rhs_v, sc, dm, cext, ci, cis, cmt, cnt, onehot, rowhot, a_part, a_split, g_part, ring_a, ring_b,
    gs, ext, mask, r, u, w, m0, n0, m1, p, s, x, vs, wb, from_left, from_right, corners, cown, bext, red_a, red_b,
    load_sem, cm_send, cm_recv, misc_send, misc_recv, halo_send, halo_recv, ex_send, ex_recv,
    bk_send, bk_recv, ag_send, ag_recv, ra_send, ra_recv, rb_send, rb_recv, ring_send, ring_recv,
):
    sub, grp = lax.axis_index("sub"), lax.axis_index("grp")
    right, left = lax.rem(sub + 1, NSUB), lax.rem(sub + NSUB - 1, NSUB)
    y, core = lax.div(grp, 2), lax.rem(grp, 2)
    mate = 2 * y + 1 - core
    to_right, to_left, to_mate = {"sub": right}, {"sub": left}, {"grp": mate}

    def grp_at(step):
        return 2 * lax.rem(y + step, NY) + core

    loads = [
        pltpu.make_async_copy(map_h, cmt.at[grp], load_sem.at[0]),
        pltpu.make_async_copy(coupling_h.at[0], cext.at[pl.ds(1, SUBS)], load_sem.at[1]),
        pltpu.make_async_copy(rhs_h.at[0], rhs_v, load_sem.at[2]),
        pltpu.make_async_copy(coarse_h.at[0], ci, load_sem.at[3]),
        pltpu.make_async_copy(dirichlet_h.at[0], dm, load_sem.at[4]),
        pltpu.make_async_copy(solve_h.at[0], sc.at[:, pl.ds(0, PS)], load_sem.at[5]),
    ]
    for load in loads:
        load.start()

    barrier = pltpu.get_barrier_semaphore()
    for i in range(1, NGRP):
        pl.semaphore_signal(barrier, inc=1, device_id={"grp": lax.rem(grp + i, NGRP)}, device_id_type=MESH)
    for i in range(1, NSUB):
        pl.semaphore_signal(barrier, inc=1, device_id={"sub": lax.rem(sub + i, NSUB)}, device_id_type=MESH)
    pl.semaphore_wait(barrier, NGRP + NSUB - 2)

    def map_copy(i):
        peer = lax.rem(grp + i, NGRP)
        return remote(cmt.at[grp], cmt.at[grp], cm_send.at[i], cm_recv.at[i], {"grp": peer})

    def map_arrival(i):
        slot = lax.rem(grp + NGRP - i, NGRP)
        return remote(cmt.at[slot], cmt.at[slot], cm_send.at[i], cm_recv.at[i], to_mate)

    count_copy = remote(cnt.at[0], cnt.at[1], misc_send.at[0], misc_recv.at[0], to_right)
    cpl_right = remote(
        cext.at[SUBS, :, pl.ds(H, H)], cext.at[0, :, pl.ds(H, H)], misc_send.at[1], misc_recv.at[1], to_right
    )
    cpl_left = remote(
        cext.at[1, :, pl.ds(0, H)], cext.at[SUBS + 1, :, pl.ds(0, H)], misc_send.at[2], misc_recv.at[2], to_left
    )
    mate_copy = remote(a_part.at[core], a_part.at[core], misc_send.at[3], misc_recv.at[3], to_mate)
    mate_arrival = remote(a_part.at[1 - core], a_part.at[1 - core], misc_send.at[3], misc_recv.at[3], to_mate)
    up, down, far = lax.rem(y + 1, NY), lax.rem(y + 3, NY), lax.rem(y + 2, NY)
    to_up, to_down = {"grp": 2 * up + core}, {"grp": 2 * down + core}
    ring_copies = [
        remote(g_part.at[far, pl.ds(0, 2)], ring_a.at[0], ring_send.at[0], ring_recv.at[0], to_up),
        remote(g_part.at[far, pl.ds(2, 2)], ring_a.at[1], ring_send.at[1], ring_recv.at[1], to_down),
        remote(g_part.at[up], ring_b.at[0], ring_send.at[2], ring_recv.at[2], to_up),
        remote(g_part.at[down], ring_b.at[1], ring_send.at[3], ring_recv.at[3], to_down),
    ]

    def halo_copy(k):
        return remote(
            r.at[k, block(SUBS)], r.at[k, block(0)], halo_send.at[k], halo_recv.at[k], to_right
        )

    def face_left(op, k):
        return remote(
            wb.at[op % 2, k, 0, pl.ds(0, H)], from_right.at[op, k],
            ex_send.at[op, LEFT, k], ex_recv.at[op, LEFT, k], to_left,
        )

    def face_right(op, k):
        return remote(
            wb.at[op % 2, k, SUBS - 1, pl.ds(H, H)], from_left.at[op, k],
            ex_send.at[op, RIGHT, k], ex_recv.at[op, RIGHT, k], to_right,
        )

    def back_left(f, k):
        return remote(
            bext.at[f, k, pl.ds(NC, NC)], bext.at[f, k, pl.ds(NC + OWN, NC)],
            bk_send.at[f, LEFT, k], bk_recv.at[f, LEFT, k], to_left,
        )

    def back_right(f, k):
        return remote(
            bext.at[f, k, pl.ds(OWN, NC)], bext.at[f, k, pl.ds(0, NC)],
            bk_send.at[f, RIGHT, k], bk_recv.at[f, RIGHT, k], to_right,
        )

    def corner_copy(f, k, i):
        device = to_mate if i == 0 else {"grp": grp_at(i)}
        mine = corners.at[f, k, grp]
        return remote(mine, mine, ag_send.at[f, k, i], ag_recv.at[f, k, i], device)

    def corner_arrival(f, k, i):
        slot = mate if i == 0 else grp_at(NY - i)
        there = corners.at[f, k, slot]
        return remote(there, there, ag_send.at[f, k, i], ag_recv.at[f, k, i], to_mate)

    def corner_forward(f, k, i):
        there = corners.at[f, k, grp_at(NY - i)]
        return remote(there, there, ag_send.at[f, k, NY - 1 + i], ag_recv.at[f, k, NY - 1 + i], to_mate)

    def corner_forwarded(f, k, i):
        there = corners.at[f, k, 2 * lax.rem(y + NY - i, NY) + 1 - core]
        return remote(there, there, ag_send.at[f, k, NY - 1 + i], ag_recv.at[f, k, NY - 1 + i], to_mate)

    def sum_a(t, i):
        mine = red_a.at[t, grp]
        return remote(mine, mine, ra_send.at[t, i], ra_recv.at[t, i], {"grp": lax.rem(grp + i, NGRP)})

    def sum_a_arrival(t, i):
        there = red_a.at[t, lax.rem(grp + NGRP - i, NGRP)]
        return remote(there, there, ra_send.at[t, i], ra_recv.at[t, i], to_mate)

    def sum_b(t, i):
        mine = red_b.at[t, sub]
        return remote(mine, mine, rb_send.at[t, i], rb_recv.at[t, i], {"sub": lax.rem(sub + i, NSUB)})

    def sum_b_arrival(t, i):
        there = red_b.at[t, lax.rem(sub + NSUB - i, NSUB)]
        return remote(there, there, rb_send.at[t, i], rb_recv.at[t, i], to_right)


    def split_vector(vector, k):
        for i in range(PAIRS):
            high, low = split(vector[k, block(i)])
            vs[k, block(i), pl.ds(0, LANES)] = high
            vs[k, block(i), pl.ds(LANES, LANES)] = low

    def apply_panel(op, k, j, solve):
        faces = vs[k, pl.ds(pl.multiple_of(H * j, H), PS), :]
        both = jnp.dot((sc if solve else dm)[j], faces, preferred_element_type=F32)
        both = both[:, :LANES] + both[:, LANES:]
        wb[op % 2, k, j] = both[:PS]
        if solve:
            f = op // 2
            values = both[PS : PS + NC] + both[PS + NC :]
            rows = pl.ds(pl.multiple_of(NC * j, NC), NC)
            cown[f, k, rows] = values

    def start(op, k, vector, last=False):
        solve = op % 2 == 1
        if op >= 2:
            face_left(op - 2, k).wait_send()
            face_right(op - 2, k).wait_send()
        split_vector(vector, k)

        def outer(t, carry):
            apply_panel(op, k, (SUBS - 1) * t, solve)
            return carry

        lax.fori_loop(0, 2, outer, 0)
        face_left(op, k).start()
        if not last:
            face_right(op, k).start()

        def inner(t, carry):
            apply_panel(op, k, 1 + t, solve)
            return carry

        lax.fori_loop(0, 2, inner, 0)
        if solve:
            f = op // 2
            corners[f, k, grp] = cown[f, k]
            for i in range(NY):
                corner_copy(f, k, i).start()

    def gather(f, k):
        for i in range(1, NY):
            corner_arrival(f, k, i).wait_recv()
            corner_forward(f, k, i).start()

    def coarse(f, k, last=False):
        corner_arrival(f, k, 0).wait_recv()
        for i in range(1, NY):
            corner_forwarded(f, k, i).wait_recv()
        high, low = split(corners[f, k].reshape(NGRP * OWN, LANES))
        both = jnp.dot(gs[...], jnp.concatenate([high, low], axis=1), preferred_element_type=F32)
        both = both[:, :LANES] + both[:, LANES:]
        bext[f, k, pl.ds(NC, OWN)] = both[:OWN] + both[OWN:]
        back_left(f, k).start()
        if not last:
            back_right(f, k).start()

    def image(op, k, i, scale=None):
        before = from_left[op, k] if i == 0 else wb[op % 2, k, i - 1, pl.ds(H, H)]
        after = from_right[op, k] if i == SUBS else wb[op % 2, k, i, pl.ds(0, H)]
        value = before + after
        if op % 2 == 1:
            high, low = split(bext[op // 2, k, pl.ds(NC * i, 2 * NC)])
            faces = jnp.concatenate([high, low, high, low], axis=0)
            value = value + jnp.dot(ext[i], faces, preferred_element_type=F32)
        else:
            value = 0.25 * value
        return jnp.where(mask[i] > 0.0, value, 0.0)

    def arrive(op, k, last=False):
        face_left(op, k).wait_recv()
        if op % 2 == 1:
            back_left(op // 2, k).wait_recv()
        if not last:
            face_right(op, k).wait_recv()
            if op % 2 == 1:
                back_right(op // 2, k).wait_recv()

    def finish(op, k, out):
        arrive(op, k)
        for i in range(PAIRS):
            out[k, block(i)] = image(op, k, i)

    def product(first, second, k):
        return colsum(first[k, pl.ds(H, SUBS * H)] * second[k, pl.ds(H, SUBS * H)])

    def put_sums(t, k, values):
        for i, value in enumerate(values):
            red_a[t, grp, k, pl.ds(i, 1)] = value

    def send_sums(t):
        for i in range(1, NGRP):
            sum_a(t, i).start()

    def pass_sums(t):
        for i in range(1, NGRP):
            sum_a_arrival(t, i).wait_recv()
        red_b[t, sub] = jnp.sum(red_a[t], axis=0)
        for i in range(1, NSUB):
            sum_b(t, i).start()

    def get_sums(t):
        for i in range(1, NSUB):
            sum_b_arrival(t, i).wait_recv()

    def sums(t, k):
        total = jnp.sum(red_b[t, :, k], axis=0)
        return [total[i : i + 1] for i in range(3)]

    load = loads[0]
    load.wait()
    for i in range(1, NGRP):
        map_copy(i).start()
    rows = lax.broadcasted_iota(I32, (H, LANES), 0)
    for c in range(SUBS):
        live = counts_s[0, c]
        if c == SUBS - 1:
            live = jnp.where(sub == NSUB - 1, 0, live)
            cnt[0] = jnp.full((8, LANES), live, I32)
        mask[c + 1] = (rows < live).astype(F32)
    count_copy.start()
    loads[1].wait()
    cpl_right.start()
    cpl_left.start()
    loads[2].wait()
    for c in (3, 0, 1, 2):
        turned = rhs_v[c].T
        for k in range(CHUNKS):
            r[k, block(c + 1)] = jnp.where(
                mask[c + 1] > 0.0, turned[:, LANES * k : LANES * (k + 1)], 0.0
            )
        if c == SUBS - 1:
            for k in range(CHUNKS):
                halo_copy(k).start()

    loads[3].wait()
    for i in range(4):
        high, low = split(ci[pl.ds(64 * i, 64)])
        cis[pl.ds(64 * i, 64)] = high
        cis[pl.ds(256 + 64 * i, 64)] = low
    for i in range(1, NGRP):
        map_arrival(i).wait_recv()

    def columns(q, carry):
        for c in range(2):
            wanted = cmt[2 * q + c, pl.ds(0, 1)]

            def fill(t, inner):
                first = pl.multiple_of(256 * t, 256)
                at = lax.broadcasted_iota(I32, (256, LANES), 0) + first
                onehot[pl.ds(first, 256), pl.ds(LANES * c, LANES)] = (at == wanted).astype(F32).astype(BF16)
                return inner

            lax.fori_loop(0, NCO // 256, fill, 0)
        both = jnp.dot(cis[...], onehot[...], preferred_element_type=F32)
        a_part[core, q] = both[:256] + both[256:]
        return carry

    lax.fori_loop(0, NY, columns, 0)
    mate_copy.start()

    loads[4].wait()
    for j in range(SUBS):
        for a, b in ((0, 1), (1, 0)):
            dm[j, block(a), block(b)] = -dm[j, block(a), block(b)]
    count_copy.wait_recv()
    mask[0] = (rows < cnt[1, pl.ds(0, 1)]).astype(F32)

    def first(k):
        halo_copy(k).wait_recv()
        start(0, k, r)

    chunks(first)

    loads[5].wait()
    cpl_right.wait_recv()
    cpl_left.wait_recv()
    for j in range(SUBS):
        for a, b in ((0, 1), (1, 0)):
            sc[j, block(a), block(b)] = -sc[j, block(a), block(b)]
        for half in range(2):
            part = cext[j + 1, :, block(half)]
            high, low = split(part if half else -part)
            sc[j, pl.ds(PS, NC), block(half)] = high
            sc[j, pl.ds(PS + NC, NC), block(half)] = low
    for i in range(PAIRS):
        both = jnp.concatenate([cext[i, :, block(1)], -cext[i + 1, :, block(0)]], axis=0)
        high = both.astype(BF16).astype(F32)
        low = both - high
        ext[i] = jnp.concatenate([high, high, low, low], axis=0).T.astype(BF16)

    mate_arrival.wait_recv()
    for q in range(NY):
        for c in range(2):
            high, low = split(a_part[c, q])
            a_split[q, block(c), pl.ds(0, 256)] = high
            a_split[q, block(c), pl.ds(256, 256)] = low
    lane = lax.broadcasted_iota(I32, (LANES, LANES), 1).astype(F32)
    base = (2 * NGRP * 32 * y).astype(F32)
    for q in range(NY):
        wanted = jnp.broadcast_to(cmt[2 * q + core, pl.ds(0, 1)], (LANES, LANES)).astype(F32).T
        for t in range(4):
            rowhot[pl.ds(LANES * q, LANES), pl.ds(LANES * t, LANES)] = (
                wanted == lane + (base + 128.0 * t)
            ).astype(F32).astype(BF16)

    def rows_of(q, carry):
        both = jnp.dot(rowhot[...], a_split[q], preferred_element_type=F32)
        both = both[:, :256] + both[:, 256:]
        for chip in range(NY):
            g_part[chip, q] = both[LANES * chip : LANES * (chip + 1)]
        return carry

    lax.fori_loop(0, NY, rows_of, 0)
    ring_copies[0].start()
    ring_copies[1].start()

    def second(k):
        finish(0, k, u)
        start(1, k, u)

    chunks(second)

    ring_copies[0].wait_recv()
    g_part[up, pl.ds(0, 2)] = g_part[up, pl.ds(0, 2)] + ring_a[0]
    ring_copies[2].start()
    ring_copies[1].wait_recv()
    g_part[down, pl.ds(2, 2)] = g_part[down, pl.ds(2, 2)] + ring_a[1]
    ring_copies[3].start()
    chunks(lambda k: gather(0, k))
    ring_copies[2].wait_recv()
    ring_copies[3].wait_recv()
    for q in range(NY):
        high, low = split(g_part[y, q] + ring_b[0, q] + ring_b[1, q])
        gs[pl.ds(0, OWN), pl.ds(256 * q, 256)] = high
        gs[pl.ds(OWN, OWN), pl.ds(256 * q, 256)] = low

    chunks(lambda k: coarse(0, k))

    def third(k):
        finish(1, k, w)
        put_sums(0, k, [product(r, u, k), product(u, w, k), jnp.zeros((1, LANES), F32)])
        start(2, k, w)

    chunks(third)
    send_sums(0)

    def fourth(k):
        finish(2, k, m0)
        start(3, k, m0)

    chunks(fourth)
    pass_sums(0)
    chunks(lambda k: gather(1, k))
    chunks(lambda k: coarse(1, k))
    get_sums(0)

    def scalars(k):
        rz0, den0, _ = sums(0, k)
        return rz0, den0, rz0 / den0

    def fifth(k):
        _, _, alpha = scalars(k)
        halo_copy(k).wait_send()
        arrive(3, k)
        for i in range(PAIRS):
            here = (k, block(i))
            n0[here] = image(3, k, i)
            p[here] = u[here]
            s[here] = w[here]
            x[here] = alpha * u[here]
            r[here] = r[here] - alpha * w[here]
            u[here] = u[here] - alpha * m0[here]
            w[here] = w[here] - alpha * n0[here]
        put_sums(1, k, [product(r, u, k), product(u, w, k), product(u, s, k)])
        start(4, k, w)

    chunks(fifth)
    send_sums(1)

    def sixth(k):
        finish(4, k, m1)
        start(5, k, m1, last=True)

    chunks(sixth)
    pass_sums(1)
    chunks(lambda k: gather(2, k))
    get_sums(1)

    def scalars_one(k):
        rz0, den0, alpha0 = scalars(k)
        rz1, uw, us = sums(1, k)
        beta = rz1 / rz0
        den1 = uw + beta * (us + us) + beta * beta * den0
        return alpha0, rz1, den1, beta, rz1 / den1

    def seventh(k):
        alpha0, _, _, beta, alpha = scalars_one(k)
        for i in range(PAIRS):
            here = (k, block(i))
            p[here] = u[here] + beta * p[here]
            s[here] = w[here] + beta * s[here]
            x[here] = x[here] + alpha * p[here]
            r[here] = r[here] - alpha * s[here]
            u[here] = u[here] - alpha * (m1[here] + beta * m0[here])
            w[here] = w[here] - (alpha * beta) * n0[here]
        coarse(2, k, last=True)
        corner = cown[0, k] - alpha0 * cown[1, k] - alpha * (cown[2, k] + beta * cown[1, k])
        local = colsum(corner * bext[2, k, pl.ds(NC, OWN)])
        for j in range(SUBS):
            local = local + colsum(u[k, pl.ds(H * j, PS)] * wb[1, k, j])
        put_sums(2, k, [product(r, u, k), product(u, w, k) - alpha * local, product(u, s, k)])

    chunks(seventh)
    send_sums(2)
    pass_sums(2)
    chunks(lambda k: arrive(5, k, last=True))
    get_sums(2)

    stores = []
    for c in range(SUBS):
        sides_x, sides_r = [], []
        for k in range(CHUNKS):
            _, rz1, den1, _, alpha1 = scalars_one(k)
            rz2, uw, us = sums(2, k)
            beta = rz2 / rz1
            den2 = uw + beta * (us + us) + beta * beta * den1
            alpha = rz2 / den2
            here = (k, block(c + 1))
            end = w[here] - alpha1 * image(5, k, c + 1)
            sides_x.append(x[here] + alpha * (u[here] + beta * p[here]))
            sides_r.append(r[here] - alpha * (end + beta * s[here]))
        rhs_v[c] = jnp.concatenate(sides_x, axis=1).T
        ci[:, pl.ds(H * c, H)] = jnp.concatenate(sides_r, axis=1).T
        stores.append(pltpu.make_async_copy(rhs_v.at[c], x_h.at[0, c], load_sem.at[6 + 2 * c]))
        stores.append(
            pltpu.make_async_copy(ci.at[:, pl.ds(H * c, H)], res_h.at[0, c], load_sem.at[7 + 2 * c])
        )
        stores[-2].start()
        stores[-1].start()

    for i in range(1, NGRP):
        map_copy(i).wait_send()
    for copy in (count_copy, cpl_right, cpl_left, mate_copy, *ring_copies):
        copy.wait_send()

    def drain(k):
        face_left(4, k).wait_send()
        face_right(4, k).wait_send()
        face_left(5, k).wait_send()
        for f in range(3):
            back_left(f, k).wait_send()
            if f < 2:
                back_right(f, k).wait_send()
            for i in range(NY):
                corner_copy(f, k, i).wait_send()
            for i in range(1, NY):
                corner_forward(f, k, i).wait_send()

    chunks(drain)
    for t in range(3):
        for i in range(1, NGRP):
            sum_a(t, i).wait_send()
        for i in range(1, NSUB):
            sum_b(t, i).wait_send()
    for copy in stores:
        copy.wait()


def local(rhs, counts, solve_panel, dirichlet_panel, coupling, corner_map, coarse_inverse):
    vector = pltpu.VMEM((CHUNKS, PAIRS * H, LANES), F32)
    dma = pltpu.SemaphoreType.DMA
    anywhere = pl.BlockSpec(memory_space=pl.ANY)
    wanted = jnp.broadcast_to(corner_map.reshape(1, OWN), (8, OWN))
    shape = jax.ShapeDtypeStruct(rhs.shape, F32)
    return pl.pallas_call(
        kernel,
        out_shape=(shape, shape),
        in_specs=[anywhere, pl.BlockSpec(memory_space=pltpu.SMEM)] + [anywhere] * 5,
        out_specs=(anywhere, anywhere),
        scratch_shapes=[
            pltpu.VMEM((SUBS, 256, H), F32),
            pltpu.VMEM((SUBS, PS + 2 * NC, PS), BF16),
            pltpu.VMEM((SUBS, PS, PS), BF16),
            pltpu.VMEM((SUBS + 2, NC, PS), F32),
            pltpu.VMEM((256, NCO), F32),
            pltpu.VMEM((512, NCO), BF16),
            pltpu.VMEM((NGRP, 8, LANES), I32),
            pltpu.VMEM((2, 8, LANES), I32),
            pltpu.VMEM((NCO, 256), BF16),
            pltpu.VMEM((512, 512), BF16),
            pltpu.VMEM((2, NY, 256, 256), F32),
            pltpu.VMEM((NY, 512, 512), BF16),
            pltpu.VMEM((NY, NY, OWN, 256), F32),
            pltpu.VMEM((2, 2, OWN, 256), F32),
            pltpu.VMEM((2, NY, OWN, 256), F32),
            pltpu.VMEM((2 * OWN, NGRP * OWN), BF16),
            pltpu.VMEM((PAIRS, H, 8 * NC), BF16),
            pltpu.VMEM((PAIRS, H, LANES), F32),
            vector, vector, vector, vector, vector, vector, vector, vector, vector,
            pltpu.VMEM((CHUNKS, PAIRS * H, 2 * LANES), BF16),
            pltpu.VMEM((2, CHUNKS, SUBS, PS, LANES), F32),
            pltpu.VMEM((6, CHUNKS, H, LANES), F32),
            pltpu.VMEM((6, CHUNKS, H, LANES), F32),
            pltpu.VMEM((3, CHUNKS, NGRP, OWN, LANES), F32),
            pltpu.VMEM((3, CHUNKS, OWN, LANES), F32),
            pltpu.VMEM((3, CHUNKS, OWN + 2 * NC, LANES), F32),
            pltpu.VMEM((3, NGRP, CHUNKS, 8, LANES), F32),
            pltpu.VMEM((3, NSUB, CHUNKS, 8, LANES), F32),
            dma((14,)), dma((NGRP,)), dma((NGRP,)), dma((4,)), dma((4,)), dma((CHUNKS,)), dma((CHUNKS,)),
            dma((6, 2, CHUNKS)), dma((6, 2, CHUNKS)), dma((3, 2, CHUNKS)), dma((3, 2, CHUNKS)),
            dma((3, CHUNKS, 2 * NY - 1)), dma((3, CHUNKS, 2 * NY - 1)),
            dma((3, NGRP)), dma((3, NGRP)), dma((3, NSUB)), dma((3, NSUB)), dma((4,)), dma((4,)),
        ],
        compiler_params=pltpu.CompilerParams(
            collective_id=0, has_side_effects=True, vmem_limit_bytes=66_000_000
        ),
    )(rhs, counts, solve_panel, dirichlet_panel, coupling, wanted, coarse_inverse)


def solution(mesh):
    return jax.shard_map(
        local,
        mesh=mesh,
        in_specs=(
            P("grp", "sub", None, None),
            P("grp", "sub"),
            P("grp", "sub", None, None),
            P("grp", "sub", None, None),
            P("grp", "sub", None, None),
            P("grp", "sub", None),
            P("sub", "grp", None),
        ),
        out_specs=(P("grp", "sub", None, None), P("grp", "sub", None, None)),
        check_vma=False,
    )
```

```python
import jax
import jax.numpy as jnp
from jax import lax
from jax.experimental import pallas as pl
from jax.experimental.pallas import tpu as pltpu
from jax.sharding import PartitionSpec as P

MESH = pl.DeviceIdType.MESH
F32, BF16, I32 = jnp.float32, jnp.bfloat16, jnp.int32
NSUB, NGRP, NY = 16, 8, 4
SUBS, H, PS, NC, NCO = 4, 256, 512, 32, 2048
LANES, CHUNKS, PAIRS = 128, 2, 5
OWN = SUBS * NC
LEFT, RIGHT = 0, 1


def remote(src, dst, send_sem, recv_sem, device):
    return pltpu.make_async_remote_copy(
        src_ref=src,
        dst_ref=dst,
        send_sem=send_sem,
        recv_sem=recv_sem,
        device_id=device,
        device_id_type=MESH,
    )


def split(value):
    high = value.astype(BF16)
    low = (value - high.astype(F32)).astype(BF16)
    return high, low


def colsum(value):
    return jnp.sum(value, axis=0, keepdims=True)


def chunks(body):
    for k in range(CHUNKS):
        body(k)


def block(i):
    return pl.ds(H * i, H)


def kernel(
    rhs_h, counts_s, solve_h, dirichlet_h, coupling_h, map_h, coarse_h, x_h, res_h,
    rhs_v, sc, dm, cext, ci, cis, cmt, cnt, onehot_a, onehot_b, rowhot, a_part, a_split, g_part, ring_a, ring_b,
    gs, ext, mask, r, u, w, m0, n0, m1, p, s, x, vs, wb, from_left, from_right, corners, cown, bext, red_a, red_b,
    load_sem, cm_send, cm_recv, misc_send, misc_recv, halo_send, halo_recv, ex_send, ex_recv,
    bk_send, bk_recv, ag_send, ag_recv, ra_send, ra_recv, rb_send, rb_recv, ring_send, ring_recv,
):
    sub, grp = lax.axis_index("sub"), lax.axis_index("grp")
    right, left = lax.rem(sub + 1, NSUB), lax.rem(sub + NSUB - 1, NSUB)
    y, core = lax.div(grp, 2), lax.rem(grp, 2)
    mate = 2 * y + 1 - core
    up, down, far = lax.rem(y + 1, NY), lax.rem(y + 3, NY), lax.rem(y + 2, NY)
    to_right, to_left, to_mate = {"sub": right}, {"sub": left}, {"grp": mate}
    to_up, to_down = {"grp": 2 * up + core}, {"grp": 2 * down + core}

    barrier = pltpu.get_barrier_semaphore()
    for i in range(1, NGRP):
        pl.semaphore_signal(barrier, inc=1, device_id={"grp": lax.rem(grp + i, NGRP)}, device_id_type=MESH)
    for i in range(1, NSUB):
        pl.semaphore_signal(barrier, inc=1, device_id={"sub": lax.rem(sub + i, NSUB)}, device_id_type=MESH)

    loads = [
        pltpu.make_async_copy(map_h.at[0], cmt.at[grp], load_sem.at[0]),
        pltpu.make_async_copy(rhs_h.at[0], rhs_v.at[pl.ds(1, SUBS)], load_sem.at[1]),
        pltpu.make_async_copy(coarse_h.at[0], ci, load_sem.at[2]),
        pltpu.make_async_copy(dirichlet_h.at[0], dm, load_sem.at[3]),
        pltpu.make_async_copy(coupling_h.at[0], cext.at[pl.ds(1, SUBS)], load_sem.at[4]),
        pltpu.make_async_copy(solve_h.at[0], sc.at[:, pl.ds(0, PS)], load_sem.at[5]),
    ]
    for load in loads:
        load.start()

    def map_copy(i):
        peer = lax.rem(grp + i, NGRP)
        return remote(map_h.at[0], cmt.at[grp], cm_send.at[i], cm_recv.at[i], {"grp": peer})

    def map_arrival(i):
        slot = lax.rem(grp + NGRP - i, NGRP)
        return remote(map_h.at[0], cmt.at[slot], cm_send.at[i], cm_recv.at[i], to_mate)

    count_copy = remote(cnt.at[0], cnt.at[1], misc_send.at[0], misc_recv.at[0], to_right)
    cpl_right = remote(
        coupling_h.at[0, SUBS - 1, :, pl.ds(H, H)], cext.at[0, :, pl.ds(H, H)],
        misc_send.at[1], misc_recv.at[1], to_right,
    )
    cpl_left = remote(
        coupling_h.at[0, 0, :, pl.ds(0, H)], cext.at[SUBS + 1, :, pl.ds(0, H)],
        misc_send.at[2], misc_recv.at[2], to_left,
    )
    mate_copy = remote(a_part.at[core], a_part.at[core], misc_send.at[3], misc_recv.at[3], to_mate)
    mate_arrival = remote(a_part.at[1 - core], a_part.at[1 - core], misc_send.at[3], misc_recv.at[3], to_mate)

    def ring(i, source, target, device):
        return remote(source, target, ring_send.at[i], ring_recv.at[i], device)

    front, rear = pl.ds(0, 2), pl.ds(2, 2)
    ring_copies = [
        ring(0, g_part.at[far, front], ring_a.at[0], to_up),
        ring(1, g_part.at[far, rear], ring_a.at[1], to_down),
        ring(2, g_part.at[up, rear], ring_b.at[0, rear], to_up),
        ring(3, g_part.at[down, front], ring_b.at[1, front], to_down),
        ring(4, g_part.at[up, front], ring_b.at[0, front], to_up),
        ring(5, g_part.at[down, rear], ring_b.at[1, rear], to_down),
    ]

    def halo_copy(k):
        part = pl.ds(LANES * k, LANES)
        return remote(
            rhs_h.at[0, SUBS - 1, part], rhs_v.at[0, part], halo_send.at[k], halo_recv.at[k], to_right
        )

    def face_left(op, k):
        return remote(
            wb.at[op % 2, k, 0, pl.ds(0, H)], from_right.at[op, k],
            ex_send.at[op, LEFT, k], ex_recv.at[op, LEFT, k], to_left,
        )

    def face_right(op, k):
        return remote(
            wb.at[op % 2, k, SUBS - 1, pl.ds(H, H)], from_left.at[op, k],
            ex_send.at[op, RIGHT, k], ex_recv.at[op, RIGHT, k], to_right,
        )

    def back_left(f, k):
        return remote(
            bext.at[f, k, pl.ds(NC, NC)], bext.at[f, k, pl.ds(NC + OWN, NC)],
            bk_send.at[f, LEFT, k], bk_recv.at[f, LEFT, k], to_left,
        )

    def back_right(f, k):
        return remote(
            bext.at[f, k, pl.ds(OWN, NC)], bext.at[f, k, pl.ds(0, NC)],
            bk_send.at[f, RIGHT, k], bk_recv.at[f, RIGHT, k], to_right,
        )

    def corner_link(f, k, i, part, device):
        return remote(part, part, ag_send.at[f, k, i], ag_recv.at[f, k, i], device)

    def corner_slot(f, k, chip, mine=True):
        return corners.at[f, k, 2 * chip + (core if mine else 1 - core)]

    half_a, half_b = pl.ds(0, OWN // 2), pl.ds(OWN // 2, OWN // 2)

    def corner_sends(f, k):
        own = corner_slot(f, k, y)
        return [corner_link(f, k, i, own, to) for i, to in enumerate((to_mate, to_up, to_down))]

    def corner_near(f, k):
        return [
            corner_link(f, k, 1, corner_slot(f, k, down), to_up),
            corner_link(f, k, 2, corner_slot(f, k, up), to_down),
        ]

    def corner_relays(f, k):
        return [
            corner_link(f, k, 3, corner_slot(f, k, down).at[half_a], to_up),
            corner_link(f, k, 4, corner_slot(f, k, up).at[half_b], to_down),
        ]

    def corner_far(f, k):
        return [
            corner_link(f, k, 3, corner_slot(f, k, far).at[half_a], to_up),
            corner_link(f, k, 4, corner_slot(f, k, far).at[half_b], to_down),
        ]

    def corner_forwards(f, k, mine=True):
        return [
            corner_link(f, k, 5, corner_slot(f, k, down, mine), to_mate),
            corner_link(f, k, 6, corner_slot(f, k, up, mine), to_mate),
            corner_link(f, k, 7, corner_slot(f, k, far, mine).at[half_a], to_mate),
            corner_link(f, k, 8, corner_slot(f, k, far, mine).at[half_b], to_mate),
        ]

    def corner_mate(f, k):
        return corner_link(f, k, 0, corner_slot(f, k, y, False), to_mate)

    def sum_a(t, i):
        mine = red_a.at[t, grp]
        return remote(mine, mine, ra_send.at[t, i], ra_recv.at[t, i], {"grp": lax.rem(grp + i, NGRP)})

    def sum_a_arrival(t, i):
        there = red_a.at[t, lax.rem(grp + NGRP - i, NGRP)]
        return remote(there, there, ra_send.at[t, i], ra_recv.at[t, i], to_mate)

    def sum_b(t, i):
        mine = red_b.at[t, sub]
        return remote(mine, mine, rb_send.at[t, i], rb_recv.at[t, i], {"sub": lax.rem(sub + i, NSUB)})

    def sum_b_arrival(t, i):
        there = red_b.at[t, lax.rem(sub + NSUB - i, NSUB)]
        return remote(there, there, rb_send.at[t, i], rb_recv.at[t, i], to_right)


    def split_vector(vector, k, pairs):
        for i in pairs:
            high, low = split(vector[k, block(i)])
            vs[k, block(i), pl.ds(0, LANES)] = high
            vs[k, block(i), pl.ds(LANES, LANES)] = low

    def apply_panel(op, k, j):
        solve = op % 2 == 1
        faces = vs[k, pl.ds(H * j, PS), :]
        both = jnp.dot((sc if solve else dm)[j], faces, preferred_element_type=F32)
        both = both[:, :LANES] + both[:, LANES:]
        wb[op % 2, k, j] = both[:PS]
        if solve:
            f = op // 2
            values = both[PS : PS + NC] + both[PS + NC :]
            cown[f, k, pl.ds(NC * j, NC)] = values
            corners[f, k, grp, pl.ds(NC * j, NC)] = values

    def start(op, k, vector, last=False):
        solve = op % 2 == 1
        if op >= 2:
            face_left(op - 2, k).wait_send()
            face_right(op - 2, k).wait_send()
        split_vector(vector, k, range(PAIRS))
        apply_panel(op, k, 0)
        face_left(op, k).start()
        apply_panel(op, k, SUBS - 1)
        if not last:
            face_right(op, k).start()
        apply_panel(op, k, 1)
        apply_panel(op, k, 2)
        if solve:
            for copy in corner_sends(op // 2, k):
                copy.start()

    def gather_near(f, k):
        near, relays, forwards = corner_near(f, k), corner_relays(f, k), corner_forwards(f, k)
        for i in range(2):
            near[i].wait_recv()
            relays[i].start()
            forwards[i].start()

    def gather_far(f, k):
        arrivals, forwards = corner_far(f, k), corner_forwards(f, k)
        for i in range(2):
            arrivals[i].wait_recv()
            forwards[2 + i].start()

    def coarse(f, k, last=False):
        corner_mate(f, k).wait_recv()
        for copy in corner_forwards(f, k, False):
            copy.wait_recv()
        high, low = split(corners[f, k].reshape(NGRP * OWN, LANES))
        both = jnp.dot(gs[...], jnp.concatenate([high, low], axis=1), preferred_element_type=F32)
        both = both[:, :LANES] + both[:, LANES:]
        bext[f, k, pl.ds(NC, OWN)] = both[:OWN] + both[OWN:]
        back_left(f, k).start()
        if not last:
            back_right(f, k).start()

    def all_coarse(f, last=False):
        chunks(lambda k: gather_near(f, k))
        chunks(lambda k: gather_far(f, k))
        chunks(lambda k: coarse(f, k, last))

    def image(op, k, i):
        before = from_left[op, k] if i == 0 else wb[op % 2, k, i - 1, pl.ds(H, H)]
        after = from_right[op, k] if i == SUBS else wb[op % 2, k, i, pl.ds(0, H)]
        value = before + after
        if op % 2 == 1:
            high, low = split(bext[op // 2, k, pl.ds(NC * i, 2 * NC)])
            faces = jnp.concatenate([high, low, high, low], axis=0)
            value = value + jnp.dot(ext[i], faces, preferred_element_type=F32)
        else:
            value = 0.25 * value
        return jnp.where(mask[i] > 0.0, value, 0.0)

    def arrive(op, k, last=False):
        face_left(op, k).wait_recv()
        if op % 2 == 1:
            back_left(op // 2, k).wait_recv()
        if not last:
            face_right(op, k).wait_recv()
            if op % 2 == 1:
                back_right(op // 2, k).wait_recv()

    def finish(op, k, out):
        for i in range(1, SUBS):
            if op % 2 == 0:
                out[k, block(i)] = image(op, k, i)
        arrive(op, k)
        for i in (0, SUBS) if op % 2 == 0 else range(PAIRS):
            out[k, block(i)] = image(op, k, i)

    def product(first, second, k):
        return colsum(first[k, pl.ds(H, SUBS * H)] * second[k, pl.ds(H, SUBS * H)])

    def put_sums(t, k, values):
        for i, value in enumerate(values):
            red_a[t, grp, pl.ds(3 * k + i, 1)] = value

    def send_sums(t):
        for i in range(1, NGRP):
            sum_a(t, i).start()

    def pass_sums(t):
        for i in range(1, NGRP):
            sum_a_arrival(t, i).wait_recv()
        red_b[t, sub] = jnp.sum(red_a[t], axis=0)
        for i in range(1, NSUB):
            sum_b(t, i).start()

    def get_sums(t):
        for i in range(1, NSUB):
            sum_b_arrival(t, i).wait_recv()
        total = jnp.sum(red_b[t], axis=0)
        return [[total[3 * k + i : 3 * k + i + 1] for i in range(3)] for k in range(CHUNKS)]

    live = [counts_s[0, c] for c in range(SUBS)]
    live[SUBS - 1] = jnp.where(sub == NSUB - 1, 0, live[SUBS - 1])
    cnt[0] = jnp.full((8, LANES), live[SUBS - 1], I32)
    red_a[...] = jnp.zeros_like(red_a)
    pl.semaphore_wait(barrier, NGRP + NSUB - 2)
    for i in range(1, NGRP):
        map_copy(i).start()
    count_copy.start()
    chunks(lambda k: halo_copy(k).start())
    cpl_right.start()
    cpl_left.start()

    loads[2].wait()
    for i in range(4):
        high, low = split(ci[pl.ds(64 * i, 64)])
        cis[pl.ds(64 * i, 64)] = high
        cis[pl.ds(256 + 64 * i, 64)] = low
    rows = lax.broadcasted_iota(I32, (H, LANES), 0)
    for c in range(SUBS):
        mask[c + 1] = (rows < live[c]).astype(F32)
    loads[1].wait()
    for c in range(SUBS):
        turned = rhs_v[c + 1].T
        for k in range(CHUNKS):
            r[k, block(c + 1)] = jnp.where(
                mask[c + 1] > 0.0, turned[:, LANES * k : LANES * (k + 1)], 0.0
            )

    loads[0].wait()
    for i in range(1, NGRP):
        map_arrival(i).wait_recv()

    def map_row(g):
        return jnp.concatenate([cmt[g, pl.ds(c, 1)] for c in range(SUBS)], axis=1)

    def fill(onehot, q):
        for c in range(2):
            wanted = map_row(2 * q + c)
            for t in range(NCO // 256):
                hit = rows + 256 * t == wanted
                onehot[pl.ds(256 * t, 256), pl.ds(LANES * c, LANES)] = hit.astype(F32).astype(BF16)

    slots = (onehot_a, onehot_b)
    fill(onehot_a, 0)
    for q in range(NY):
        if q + 1 < NY:
            fill(slots[(q + 1) % 2], q + 1)
        both = jnp.dot(cis[...], slots[q % 2][...], preferred_element_type=F32)
        a_part[core, q] = both[:256] + both[256:]
    mate_copy.start()

    loads[3].wait()
    for j in range(SUBS):
        for a, b in ((0, 1), (1, 0)):
            dm[j, block(a), block(b)] = -dm[j, block(a), block(b)]
    count_copy.wait_recv()
    mask[0] = (rows < cnt[1, pl.ds(0, 1)]).astype(F32)

    def first(k):
        halo_copy(k).wait_recv()
        r[k, block(0)] = jnp.where(mask[0] > 0.0, rhs_v[0, pl.ds(LANES * k, LANES)].T, 0.0)
        start(0, k, r)

    chunks(first)

    mate_arrival.wait_recv()
    for q in range(NY):
        for c in range(2):
            high, low = split(a_part[c, q])
            a_split[q, block(c), pl.ds(0, 256)] = high
            a_split[q, block(c), pl.ds(256, 256)] = low
    lane = lax.broadcasted_iota(I32, (LANES, LANES), 1).astype(F32)
    base = (2 * 256 * y).astype(F32)
    for q in range(NY):
        wanted = jnp.broadcast_to(map_row(2 * q + core), (LANES, LANES)).astype(F32).T
        for t in range(4):
            rowhot[pl.ds(LANES * q, LANES), pl.ds(LANES * t, LANES)] = (
                wanted == lane + (base + 128.0 * t)
            ).astype(F32).astype(BF16)
    for q in range(NY):
        both = jnp.dot(rowhot[...], a_split[q], preferred_element_type=F32)
        both = both[:, :256] + both[:, 256:]
        for chip in range(NY):
            g_part[chip, q] = both[LANES * chip : LANES * (chip + 1)]
    for i in range(4):
        ring_copies[i].start()

    loads[5].wait()
    loads[4].wait()
    cpl_right.wait_recv()
    cpl_left.wait_recv()
    for j in range(SUBS):
        for a, b in ((0, 1), (1, 0)):
            sc[j, block(a), block(b)] = -sc[j, block(a), block(b)]
        for half in range(2):
            part = cext[j + 1, :, block(half)]
            high, low = split(part if half else -part)
            sc[j, pl.ds(PS, NC), block(half)] = high
            sc[j, pl.ds(PS + NC, NC), block(half)] = low

    def second(k):
        finish(0, k, u)
        start(1, k, u)

    chunks(second)
    ring_copies[0].wait_recv()
    g_part[up, front] = g_part[up, front] + ring_a[0]
    ring_copies[4].start()
    ring_copies[1].wait_recv()
    g_part[down, rear] = g_part[down, rear] + ring_a[1]
    ring_copies[5].start()
    chunks(lambda k: gather_near(0, k))
    for i in range(PAIRS):
        both = jnp.concatenate([cext[i, :, block(1)], -cext[i + 1, :, block(0)]], axis=0)
        high = both.astype(BF16).astype(F32)
        low = both - high
        ext[i] = jnp.concatenate([high, high, low, low], axis=0).T.astype(BF16)
    chunks(lambda k: gather_far(0, k))
    for i in range(2, 6):
        ring_copies[i].wait_recv()
    for q in range(NY):
        high, low = split(g_part[y, q] + ring_b[0, q] + ring_b[1, q])
        gs[pl.ds(0, OWN), pl.ds(256 * q, 256)] = high
        gs[pl.ds(OWN, OWN), pl.ds(256 * q, 256)] = low

    chunks(lambda k: coarse(0, k))

    def third(k):
        finish(1, k, w)
        start(2, k, w)
        put_sums(0, k, [product(r, u, k), product(u, w, k)])

    chunks(third)
    send_sums(0)

    def fourth(k):
        finish(2, k, m0)
        start(3, k, m0)

    chunks(fourth)
    pass_sums(0)
    all_coarse(1)
    rz0, den0, alpha0 = [], [], []
    for rz, uw, _ in get_sums(0):
        rz0.append(rz)
        den0.append(uw)
        alpha0.append(rz / uw)

    def fifth(k):
        arrive(3, k)
        for i in range(PAIRS):
            here = (k, block(i))
            s[here] = w[here]
            n0[here] = image(3, k, i)
            w[here] = w[here] - alpha0[k] * n0[here]
        start(4, k, w)
        for i in range(PAIRS):
            here = (k, block(i))
            p[here] = u[here]
            x[here] = alpha0[k] * u[here]
            r[here] = r[here] - alpha0[k] * s[here]
            u[here] = u[here] - alpha0[k] * m0[here]
        put_sums(1, k, [product(r, u, k), product(u, w, k), product(u, s, k)])

    chunks(fifth)
    send_sums(1)

    def sixth(k):
        finish(4, k, m1)
        start(5, k, m1, last=True)

    chunks(sixth)
    pass_sums(1)
    chunks(lambda k: gather_near(2, k))
    rz1, den1, alpha1 = [], [], []
    beta1 = []
    for k, (rz, uw, us) in enumerate(get_sums(1)):
        beta = rz / rz0[k]
        den = uw + beta * (us + us) + beta * beta * den0[k]
        rz1.append(rz)
        den1.append(den)
        beta1.append(beta)
        alpha1.append(rz / den)
    chunks(lambda k: gather_far(2, k))

    partial = []

    def seventh(k):
        alpha, beta = alpha1[k], beta1[k]
        for i in range(PAIRS):
            here = (k, block(i))
            p[here] = u[here] + beta * p[here]
            s[here] = w[here] + beta * s[here]
            x[here] = x[here] + alpha * p[here]
            r[here] = r[here] - alpha * s[here]
            u[here] = u[here] - alpha * (m1[here] + beta * m0[here])
            w[here] = w[here] - (alpha * beta) * n0[here]
        faces = jnp.zeros((1, LANES), F32)
        for j in range(SUBS):
            faces = faces + colsum(u[k, pl.ds(H * j, PS)] * wb[1, k, j])
        partial.append([product(r, u, k), product(u, w, k), product(u, s, k), faces])

    chunks(seventh)
    chunks(lambda k: coarse(2, k, last=True))
    for k in range(CHUNKS):
        corner = cown[0, k] - alpha0[k] * cown[1, k] - alpha1[k] * (cown[2, k] + beta1[k] * cown[1, k])
        ru, uw, us, faces = partial[k]
        faces = faces + colsum(corner * bext[2, k, pl.ds(NC, OWN)])
        put_sums(2, k, [ru, uw - alpha1[k] * faces, us])
    send_sums(2)

    for i in range(1, NGRP):
        map_copy(i).wait_send()
    for copy in (count_copy, cpl_right, cpl_left, mate_copy, *ring_copies):
        copy.wait_send()
    for t in range(2):
        for i in range(1, NGRP):
            sum_a(t, i).wait_send()
    pass_sums(2)

    def under(k):
        arrive(5, k, last=True)
        for i in range(1, PAIRS):
            here = (k, block(i))
            w[here] = w[here] - alpha1[k] * image(5, k, i)

    chunks(under)

    def drain(k):
        halo_copy(k).wait_send()
        face_left(4, k).wait_send()
        face_right(4, k).wait_send()
        face_left(5, k).wait_send()
        for f in range(3):
            back_left(f, k).wait_send()
            if f < 2:
                back_right(f, k).wait_send()
            for copy in corner_sends(f, k) + corner_relays(f, k) + corner_forwards(f, k):
                copy.wait_send()

    chunks(drain)
    for t in range(2):
        for i in range(1, NSUB):
            sum_b(t, i).wait_send()
    for i in range(1, NGRP):
        sum_a(2, i).wait_send()

    stores = []
    for k, (rz, uw, us) in enumerate(get_sums(2)):
        beta = rz / rz1[k]
        den = uw + beta * (us + us) + beta * beta * den1[k]
        alpha = rz / den
        for i in range(1, PAIRS):
            here = (k, block(i))
            x[here] = x[here] + alpha * (u[here] + beta * p[here])
            r[here] = r[here] - alpha * (w[here] + beta * s[here])
        own = (k, pl.ds(H, SUBS * H))
        stores.append(pltpu.make_async_copy(x.at[own], x_h.at[k], load_sem.at[6 + 2 * k]))
        stores.append(pltpu.make_async_copy(r.at[own], res_h.at[k], load_sem.at[7 + 2 * k]))
        stores[-2].start()
        stores[-1].start()
    for i in range(1, NSUB):
        sum_b(2, i).wait_send()
    for copy in stores:
        copy.wait()


def turn(x_ref, r_ref, x_out, r_out):
    for source, target in ((x_ref, x_out), (r_ref, r_out)):
        for k in range(CHUNKS):
            target[0, 0, pl.ds(LANES * k, LANES)] = source[k].T


def local(rhs, counts, solve_panel, dirichlet_panel, coupling, corner_map, coarse_inverse):
    vector = pltpu.VMEM((CHUNKS, PAIRS * H, LANES), F32)
    dma = pltpu.SemaphoreType.DMA
    anywhere = pl.BlockSpec(memory_space=pl.ANY)
    shape = jax.ShapeDtypeStruct((CHUNKS, SUBS * H, LANES), F32)
    x_turned, r_turned = pl.pallas_call(
        kernel,
        out_shape=(shape, shape),
        in_specs=[anywhere, pl.BlockSpec(memory_space=pltpu.SMEM)] + [anywhere] * 5,
        out_specs=(anywhere, anywhere),
        scratch_shapes=[
            pltpu.VMEM((PAIRS, 256, H), F32),
            pltpu.VMEM((SUBS, PS + 2 * NC, PS), BF16),
            pltpu.VMEM((SUBS, PS, PS), BF16),
            pltpu.VMEM((SUBS + 2, NC, PS), F32),
            pltpu.VMEM((256, NCO), F32),
            pltpu.VMEM((512, NCO), BF16),
            pltpu.VMEM((NGRP, SUBS, NC), I32),
            pltpu.VMEM((2, 8, LANES), I32),
            pltpu.VMEM((NCO, 256), BF16),
            pltpu.VMEM((NCO, 256), BF16),
            pltpu.VMEM((512, 512), BF16),
            pltpu.VMEM((2, NY, 256, 256), F32),
            pltpu.VMEM((NY, 512, 512), BF16),
            pltpu.VMEM((NY, NY, OWN, 256), F32),
            pltpu.VMEM((2, 2, OWN, 256), F32),
            pltpu.VMEM((2, NY, OWN, 256), F32),
            pltpu.VMEM((2 * OWN, NGRP * OWN), BF16),
            pltpu.VMEM((PAIRS, H, 8 * NC), BF16),
            pltpu.VMEM((PAIRS, H, LANES), F32),
            vector, vector, vector, vector, vector, vector, vector, vector, vector,
            pltpu.VMEM((CHUNKS, PAIRS * H, 2 * LANES), BF16),
            pltpu.VMEM((2, CHUNKS, SUBS, PS, LANES), F32),
            pltpu.VMEM((6, CHUNKS, H, LANES), F32),
            pltpu.VMEM((6, CHUNKS, H, LANES), F32),
            pltpu.VMEM((3, CHUNKS, NGRP, OWN, LANES), F32),
            pltpu.VMEM((3, CHUNKS, OWN, LANES), F32),
            pltpu.VMEM((3, CHUNKS, OWN + 2 * NC, LANES), F32),
            pltpu.VMEM((3, NGRP, 8, LANES), F32),
            pltpu.VMEM((3, NSUB, 8, LANES), F32),
            dma((10,)), dma((NGRP,)), dma((NGRP,)), dma((4,)), dma((4,)), dma((CHUNKS,)), dma((CHUNKS,)),
            dma((6, 2, CHUNKS)), dma((6, 2, CHUNKS)), dma((3, 2, CHUNKS)), dma((3, 2, CHUNKS)),
            dma((3, CHUNKS, 9)), dma((3, CHUNKS, 9)),
            dma((3, NGRP)), dma((3, NGRP)), dma((3, NSUB)), dma((3, NSUB)), dma((6,)), dma((6,)),
        ],
        compiler_params=pltpu.CompilerParams(
            collective_id=0, has_side_effects=True, vmem_limit_bytes=66_000_000
        ),
    )(rhs, counts, solve_panel, dirichlet_panel, coupling, corner_map, coarse_inverse)
    out = jax.ShapeDtypeStruct(rhs.shape, F32)
    taken = pl.BlockSpec((CHUNKS, H, LANES), lambda c: (0, c, 0))
    given = pl.BlockSpec((1, 1, CHUNKS * LANES, H), lambda c: (0, c, 0, 0))
    return pl.pallas_call(
        turn,
        out_shape=(out, out),
        grid=(SUBS,),
        in_specs=[taken, taken],
        out_specs=(given, given),
    )(x_turned, r_turned)


def solution(mesh):
    return jax.shard_map(
        local,
        mesh=mesh,
        in_specs=(
            P("grp", "sub", None, None),
            P("grp", "sub"),
            P("grp", "sub", None, None),
            P("grp", "sub", None, None),
            P("grp", "sub", None, None),
            P("grp", "sub", None),
            P("sub", "grp", None),
        ),
        out_specs=(P("grp", "sub", None, None), P("grp", "sub", None, None)),
        check_vma=False,
    )
```

```python
import jax
import jax.numpy as jnp
from jax import lax
from jax.experimental import pallas as pl
from jax.experimental.pallas import tpu as pltpu
from jax.sharding import PartitionSpec as P

MESH = pl.DeviceIdType.MESH
F32, BF16, I32 = jnp.float32, jnp.bfloat16, jnp.int32
NSUB, NGRP, NY = 16, 8, 4
SUBS, H, PS, NC, NCO = 4, 256, 512, 32, 2048
LANES, CHUNKS, PAIRS = 128, 2, 5
OWN = SUBS * NC
LEFT, RIGHT = 0, 1


def remote(src, dst, send_sem, recv_sem, device):
    return pltpu.make_async_remote_copy(
        src_ref=src,
        dst_ref=dst,
        send_sem=send_sem,
        recv_sem=recv_sem,
        device_id=device,
        device_id_type=MESH,
    )


def split(value):
    high = value.astype(BF16)
    low = (value - high.astype(F32)).astype(BF16)
    return high, low


def colsum(value):
    return jnp.sum(value, axis=0, keepdims=True)


def chunks(body):
    for k in range(CHUNKS):
        body(k)


def block(i):
    return pl.ds(H * i, H)


def kernel(
    rhs_h, counts_s, solve_h, dirichlet_h, coupling_h, map_h, coarse_h, x_h, res_h,
    rhs_v, sc, dm, cext, ci, cis, cmt, cnt, onehot_a, onehot_b, rowhot, a_part, a_split, g_part, ring_a, ring_b,
    gs, ext, mask, r, u, w, m0, n0, m1, p, s, x, vs, wb, from_left, from_right, corners, cown, bext, red_a, red_b,
    load_sem, cm_send, cm_recv, misc_send, misc_recv, halo_send, halo_recv, ex_send, ex_recv,
    bk_send, bk_recv, ag_send, ag_recv, ra_send, ra_recv, rb_send, rb_recv, ring_send, ring_recv,
):
    sub, grp = lax.axis_index("sub"), lax.axis_index("grp")
    right, left = lax.rem(sub + 1, NSUB), lax.rem(sub + NSUB - 1, NSUB)
    y, core = lax.div(grp, 2), lax.rem(grp, 2)
    mate = 2 * y + 1 - core
    up, down, far = lax.rem(y + 1, NY), lax.rem(y + 3, NY), lax.rem(y + 2, NY)
    to_right, to_left, to_mate = {"sub": right}, {"sub": left}, {"grp": mate}
    to_up, to_down = {"grp": 2 * up + core}, {"grp": 2 * down + core}

    barrier = pltpu.get_barrier_semaphore()
    for i in range(1, NGRP):
        pl.semaphore_signal(barrier, inc=1, device_id={"grp": lax.rem(grp + i, NGRP)}, device_id_type=MESH)
    for i in range(1, NSUB):
        pl.semaphore_signal(barrier, inc=1, device_id={"sub": lax.rem(sub + i, NSUB)}, device_id_type=MESH)

    loads = [
        pltpu.make_async_copy(map_h.at[0], cmt.at[grp], load_sem.at[0]),
        pltpu.make_async_copy(rhs_h.at[0], rhs_v.at[pl.ds(1, SUBS)], load_sem.at[1]),
        pltpu.make_async_copy(coarse_h.at[0], ci, load_sem.at[2]),
        pltpu.make_async_copy(dirichlet_h.at[0], dm, load_sem.at[3]),
        pltpu.make_async_copy(coupling_h.at[0], cext.at[pl.ds(1, SUBS)], load_sem.at[4]),
        pltpu.make_async_copy(solve_h.at[0], sc.at[:, pl.ds(0, PS)], load_sem.at[5]),
    ]
    for load in loads:
        load.start()

    def map_copy(i):
        peer = lax.rem(grp + i, NGRP)
        return remote(map_h.at[0], cmt.at[grp], cm_send.at[i], cm_recv.at[i], {"grp": peer})

    def map_arrival(i):
        slot = lax.rem(grp + NGRP - i, NGRP)
        return remote(map_h.at[0], cmt.at[slot], cm_send.at[i], cm_recv.at[i], to_mate)

    count_copy = remote(cnt.at[0], cnt.at[1], misc_send.at[0], misc_recv.at[0], to_right)
    cpl_right = remote(
        coupling_h.at[0, SUBS - 1, :, pl.ds(H, H)], cext.at[0, :, pl.ds(H, H)],
        misc_send.at[1], misc_recv.at[1], to_right,
    )
    cpl_left = remote(
        coupling_h.at[0, 0, :, pl.ds(0, H)], cext.at[SUBS + 1, :, pl.ds(0, H)],
        misc_send.at[2], misc_recv.at[2], to_left,
    )

    def mate_copy(q, mine=True):
        part = a_part.at[core if mine else 1 - core, q]
        return remote(part, part, misc_send.at[3 + q], misc_recv.at[3 + q], to_mate)

    def ring(i, source, target, device):
        return remote(source, target, ring_send.at[i], ring_recv.at[i], device)

    front, rear = pl.ds(0, 2), pl.ds(2, 2)
    ring_copies = [
        ring(0, g_part.at[far, front], ring_a.at[0], to_up),
        ring(1, g_part.at[far, rear], ring_a.at[1], to_down),
        ring(2, g_part.at[up, rear], ring_b.at[0, rear], to_up),
        ring(3, g_part.at[down, front], ring_b.at[1, front], to_down),
        ring(4, g_part.at[up, front], ring_b.at[0, front], to_up),
        ring(5, g_part.at[down, rear], ring_b.at[1, rear], to_down),
    ]

    def halo_copy(k):
        part = pl.ds(LANES * k, LANES)
        return remote(
            rhs_h.at[0, SUBS - 1, part], rhs_v.at[0, part], halo_send.at[k], halo_recv.at[k], to_right
        )

    def face_left(op, k):
        return remote(
            wb.at[op % 2, k, 0, pl.ds(0, H)], from_right.at[op, k],
            ex_send.at[op, LEFT, k], ex_recv.at[op, LEFT, k], to_left,
        )

    def face_right(op, k):
        return remote(
            wb.at[op % 2, k, SUBS - 1, pl.ds(H, H)], from_left.at[op, k],
            ex_send.at[op, RIGHT, k], ex_recv.at[op, RIGHT, k], to_right,
        )

    def back_left(f, k):
        return remote(
            bext.at[f, k, pl.ds(NC, NC)], bext.at[f, k, pl.ds(NC + OWN, NC)],
            bk_send.at[f, LEFT, k], bk_recv.at[f, LEFT, k], to_left,
        )

    def back_right(f, k):
        return remote(
            bext.at[f, k, pl.ds(OWN, NC)], bext.at[f, k, pl.ds(0, NC)],
            bk_send.at[f, RIGHT, k], bk_recv.at[f, RIGHT, k], to_right,
        )

    def corner_link(f, k, i, part, device):
        return remote(part, part, ag_send.at[f, k, i], ag_recv.at[f, k, i], device)

    def corner_slot(f, k, chip, mine=True):
        return corners.at[f, k, 2 * chip + (core if mine else 1 - core)]

    def corner_copy(f, k, i):
        device = to_mate if i == 0 else {"grp": 2 * lax.rem(y + i, NY) + core}
        return corner_link(f, k, i, corner_slot(f, k, y), device)

    def corner_arrival(f, k, i):
        return corner_link(f, k, i, corner_slot(f, k, lax.rem(y + NY - i, NY), i > 0), to_mate)

    def corner_forward(f, k, i, mine=True):
        return corner_link(f, k, NY - 1 + i, corner_slot(f, k, lax.rem(y + NY - i, NY), mine), to_mate)

    def sum_a(t, i):
        mine = red_a.at[t, grp]
        return remote(mine, mine, ra_send.at[t, i], ra_recv.at[t, i], {"grp": lax.rem(grp + i, NGRP)})

    def sum_a_arrival(t, i):
        there = red_a.at[t, lax.rem(grp + NGRP - i, NGRP)]
        return remote(there, there, ra_send.at[t, i], ra_recv.at[t, i], to_mate)

    def sum_b(t, i):
        mine = red_b.at[t, sub]
        return remote(mine, mine, rb_send.at[t, i], rb_recv.at[t, i], {"sub": lax.rem(sub + i, NSUB)})

    def sum_b_arrival(t, i):
        there = red_b.at[t, lax.rem(sub + NSUB - i, NSUB)]
        return remote(there, there, rb_send.at[t, i], rb_recv.at[t, i], to_right)


    def apply_panel(op, k, j):
        solve = op % 2 == 1
        faces = vs[k, pl.ds(H * j, PS), :]
        both = jnp.dot((sc if solve else dm)[j], faces, preferred_element_type=F32)
        both = both[:, :LANES] + both[:, LANES:]
        wb[op % 2, k, j] = both[:PS]
        if solve:
            f = op // 2
            values = both[PS : PS + NC] + both[PS + NC :]
            cown[f, k, pl.ds(NC * j, NC)] = values
            corners[f, k, grp, pl.ds(NC * j, NC)] = values

    def put_faces(k, pairs, value):
        for i in pairs:
            high, low = split(value(k, i))
            vs[k, block(i), pl.ds(0, LANES)] = high
            vs[k, block(i), pl.ds(LANES, LANES)] = low

    def inner(op, value):
        for k in range(CHUNKS):
            put_faces(k, range(1, SUBS), value)
            apply_panel(op, k, 1)
            apply_panel(op, k, 2)

    def outer(op, value, last=False):
        for k in range(CHUNKS):
            if op > 0:
                arrive(op - 1, k)
            if op >= 2:
                face_left(op - 2, k).wait_send()
                face_right(op - 2, k).wait_send()
            put_faces(k, (0, SUBS), value)
            apply_panel(op, k, 0)
            face_left(op, k).start()
            apply_panel(op, k, SUBS - 1)
            if op % 2 == 1:
                for i in (2, 1, 3, 0):
                    corner_copy(op // 2, k, i).start()
            if not last:
                face_right(op, k).start()

    def gather(f, k):
        for i in (1, 3, 2):
            corner_arrival(f, k, i).wait_recv()
            corner_forward(f, k, i).start()

    def coarse(f, k, last=False):
        corner_arrival(f, k, 0).wait_recv()
        for i in range(1, NY):
            corner_forward(f, k, i, False).wait_recv()
        high, low = split(corners[f, k].reshape(NGRP * OWN, LANES))
        both = jnp.dot(gs[...], jnp.concatenate([high, low], axis=1), preferred_element_type=F32)
        both = both[:, :LANES] + both[:, LANES:]
        bext[f, k, pl.ds(NC, OWN)] = both[:OWN] + both[OWN:]
        back_left(f, k).start()
        if not last:
            back_right(f, k).start()

    def all_coarse(f, last=False):
        for k in range(CHUNKS):
            gather(f, k)
        for k in range(CHUNKS):
            coarse(f, k, last)

    def image(op, k, i):
        before = from_left[op, k] if i == 0 else wb[op % 2, k, i - 1, pl.ds(H, H)]
        after = from_right[op, k] if i == SUBS else wb[op % 2, k, i, pl.ds(0, H)]
        value = before + after
        if op % 2 == 1:
            high, low = split(bext[op // 2, k, pl.ds(NC * i, 2 * NC)])
            faces = jnp.concatenate([high, low, high, low], axis=0)
            value = value + jnp.dot(ext[i], faces, preferred_element_type=F32)
        else:
            value = 0.25 * value
        return jnp.where(mask[i] > 0.0, value, 0.0)

    def arrive(op, k, last=False):
        face_left(op, k).wait_recv()
        if op % 2 == 1:
            back_left(op // 2, k).wait_recv()
        if not last:
            face_right(op, k).wait_recv()
            if op % 2 == 1:
                back_right(op // 2, k).wait_recv()

    def image_in(op, out):
        def value(k, i):
            result = image(op, k, i)
            out[k, block(i)] = result
            return result

        return value

    def product(first, second, k):
        return colsum(first[k, pl.ds(H, SUBS * H)] * second[k, pl.ds(H, SUBS * H)])

    def put_sums(t, k, values):
        for i, value in enumerate(values):
            red_a[t, grp, pl.ds(3 * k + i, 1)] = value

    def send_sums(t):
        for i in range(1, NGRP):
            sum_a(t, i).start()

    def pass_sums(t):
        for i in range(1, NGRP):
            sum_a_arrival(t, i).wait_recv()
        red_b[t, sub] = jnp.sum(red_a[t], axis=0)
        for i in range(1, NSUB):
            sum_b(t, i).start()

    def get_sums(t):
        for i in range(1, NSUB):
            sum_b_arrival(t, i).wait_recv()
        total = jnp.sum(red_b[t], axis=0)
        return [[total[3 * k + i : 3 * k + i + 1] for i in range(3)] for k in range(CHUNKS)]

    live = [counts_s[0, c] for c in range(SUBS)]
    live[SUBS - 1] = jnp.where(sub == NSUB - 1, 0, live[SUBS - 1])
    cnt[0] = jnp.full((8, LANES), live[SUBS - 1], I32)
    red_a[...] = jnp.zeros_like(red_a)
    pl.semaphore_wait(barrier, NGRP + NSUB - 2)
    for i in range(1, NGRP):
        map_copy(i).start()
    count_copy.start()
    chunks(lambda k: halo_copy(k).start())
    cpl_right.start()
    cpl_left.start()

    loads[2].wait()
    for i in range(4):
        high, low = split(ci[pl.ds(64 * i, 64)])
        cis[pl.ds(64 * i, 64)] = high
        cis[pl.ds(256 + 64 * i, 64)] = low
    rows = lax.broadcasted_iota(I32, (H, LANES), 0)
    for c in range(SUBS):
        mask[c + 1] = (rows < live[c]).astype(F32)
    loads[1].wait()
    for c in range(SUBS):
        turned = rhs_v[c + 1].T
        for k in range(CHUNKS):
            r[k, block(c + 1)] = jnp.where(
                mask[c + 1] > 0.0, turned[:, LANES * k : LANES * (k + 1)], 0.0
            )

    loads[3].wait()
    for j in range(SUBS):
        for a, b in ((0, 1), (1, 0)):
            dm[j, block(a), block(b)] = -dm[j, block(a), block(b)]

    def residual(k, i):
        if i == 0:
            halo_copy(k).wait_recv()
            turned = rhs_v[0, pl.ds(LANES * k, LANES)].T
            r[k, block(0)] = jnp.where(mask[0] > 0.0, turned, 0.0)
        return r[k, block(i)]

    inner(0, residual)

    loads[0].wait()
    for i in range(1, NGRP):
        map_arrival(i).wait_recv()

    def map_row(g):
        return jnp.concatenate([cmt[g, pl.ds(c, 1)] for c in range(SUBS)], axis=1)

    def fill(onehot, q):
        for c in range(2):
            wanted = map_row(2 * q + c)
            for t in range(NCO // 256):
                hit = rows + 256 * t == wanted
                onehot[pl.ds(256 * t, 256), pl.ds(LANES * c, LANES)] = hit.astype(F32).astype(BF16)

    slots = (onehot_a, onehot_b)
    fill(onehot_a, 0)
    for q in range(NY):
        if q + 1 < NY:
            fill(slots[(q + 1) % 2], q + 1)
        both = jnp.dot(cis[...], slots[q % 2][...], preferred_element_type=F32)
        a_part[core, q] = both[:256] + both[256:]
        mate_copy(q).start()

    count_copy.wait_recv()
    mask[0] = (rows < cnt[1, pl.ds(0, 1)]).astype(F32)
    outer(0, residual)

    for q in range(NY):
        mate_copy(q, False).wait_recv()
        for c in range(2):
            high, low = split(a_part[c, q])
            a_split[q, block(c), pl.ds(0, 256)] = high
            a_split[q, block(c), pl.ds(256, 256)] = low
    lane = lax.broadcasted_iota(I32, (LANES, LANES), 1).astype(F32)
    base = (2 * 256 * y).astype(F32)
    for q in range(NY):
        wanted = jnp.broadcast_to(map_row(2 * q + core), (LANES, LANES)).astype(F32).T
        for t in range(4):
            rowhot[pl.ds(LANES * q, LANES), pl.ds(LANES * t, LANES)] = (
                wanted == lane + (base + 128.0 * t)
            ).astype(F32).astype(BF16)
    for q in range(NY):
        both = jnp.dot(rowhot[...], a_split[q], preferred_element_type=F32)
        both = both[:, :256] + both[:, 256:]
        for chip in range(NY):
            g_part[chip, q] = both[LANES * chip : LANES * (chip + 1)]
    for i in range(4):
        ring_copies[i].start()

    loads[5].wait()
    loads[4].wait()
    cpl_right.wait_recv()
    cpl_left.wait_recv()
    for j in range(SUBS):
        for a, b in ((0, 1), (1, 0)):
            sc[j, block(a), block(b)] = -sc[j, block(a), block(b)]
        for half in range(2):
            part = cext[j + 1, :, block(half)]
            high, low = split(part if half else -part)
            sc[j, pl.ds(PS, NC), block(half)] = high
            sc[j, pl.ds(PS + NC, NC), block(half)] = low

    inner(1, image_in(0, u))
    outer(1, image_in(0, u))
    ring_copies[0].wait_recv()
    g_part[up, front] = g_part[up, front] + ring_a[0]
    ring_copies[4].start()
    ring_copies[1].wait_recv()
    g_part[down, rear] = g_part[down, rear] + ring_a[1]
    ring_copies[5].start()
    for i in range(PAIRS):
        both = jnp.concatenate([cext[i, :, block(1)], -cext[i + 1, :, block(0)]], axis=0)
        high = both.astype(BF16).astype(F32)
        low = both - high
        ext[i] = jnp.concatenate([high, high, low, low], axis=0).T.astype(BF16)
    chunks(lambda k: gather(0, k))
    for i in range(2, 6):
        ring_copies[i].wait_recv()
    for q in range(NY):
        high, low = split(g_part[y, q] + ring_b[0, q] + ring_b[1, q])
        gs[pl.ds(0, OWN), pl.ds(256 * q, 256)] = high
        gs[pl.ds(OWN, OWN), pl.ds(256 * q, 256)] = low

    chunks(lambda k: coarse(0, k))

    inner(2, image_in(1, w))
    outer(2, image_in(1, w))
    chunks(lambda k: put_sums(0, k, [product(r, u, k), product(u, w, k)]))
    send_sums(0)
    inner(3, image_in(2, m0))
    pass_sums(0)
    outer(3, image_in(2, m0))
    all_coarse(1)
    rz0, den0, alpha0 = [], [], []
    for rz, uw, _ in get_sums(0):
        rz0.append(rz)
        den0.append(uw)
        alpha0.append(rz / uw)

    def lowered(k, i):
        here = (k, block(i))
        s[here] = w[here]
        n0[here] = image(3, k, i)
        w[here] = w[here] - alpha0[k] * n0[here]
        return w[here]

    inner(4, lowered)
    outer(4, lowered)

    def fifth(k):
        for i in range(PAIRS):
            here = (k, block(i))
            p[here] = u[here]
            x[here] = alpha0[k] * u[here]
            r[here] = r[here] - alpha0[k] * s[here]
            u[here] = u[here] - alpha0[k] * m0[here]
        put_sums(1, k, [product(r, u, k), product(u, w, k), product(u, s, k)])

    chunks(fifth)
    send_sums(1)
    inner(5, image_in(4, m1))
    pass_sums(1)
    outer(5, image_in(4, m1), last=True)
    rz1, den1, alpha1 = [], [], []
    beta1 = []
    for k, (rz, uw, us) in enumerate(get_sums(1)):
        beta = rz / rz0[k]
        den = uw + beta * (us + us) + beta * beta * den0[k]
        rz1.append(rz)
        den1.append(den)
        beta1.append(beta)
        alpha1.append(rz / den)

    partial = []

    def seventh(k):
        alpha, beta = alpha1[k], beta1[k]
        for i in range(PAIRS):
            here = (k, block(i))
            p[here] = u[here] + beta * p[here]
            s[here] = w[here] + beta * s[here]
            x[here] = x[here] + alpha * p[here]
            r[here] = r[here] - alpha * s[here]
            u[here] = u[here] - alpha * (m1[here] + beta * m0[here])
            w[here] = w[here] - (alpha * beta) * n0[here]
        faces = jnp.zeros((1, LANES), F32)
        for j in range(SUBS):
            faces = faces + colsum(u[k, pl.ds(H * j, PS)] * wb[1, k, j])
        partial.append([product(r, u, k), product(u, w, k), product(u, s, k), faces])

    chunks(seventh)
    all_coarse(2, last=True)
    for k in range(CHUNKS):
        corner = cown[0, k] - alpha0[k] * cown[1, k] - alpha1[k] * (cown[2, k] + beta1[k] * cown[1, k])
        ru, uw, us, faces = partial[k]
        faces = faces + colsum(corner * bext[2, k, pl.ds(NC, OWN)])
        put_sums(2, k, [ru, uw - alpha1[k] * faces, us])
    send_sums(2)

    for i in range(1, NGRP):
        map_copy(i).wait_send()
    for copy in (count_copy, cpl_right, cpl_left, *ring_copies):
        copy.wait_send()
    for q in range(NY):
        mate_copy(q).wait_send()
    for t in range(2):
        for i in range(1, NGRP):
            sum_a(t, i).wait_send()
    pass_sums(2)

    def under(k):
        arrive(5, k, last=True)
        for i in range(1, PAIRS):
            here = (k, block(i))
            w[here] = w[here] - alpha1[k] * image(5, k, i)

    chunks(under)

    def drain(k):
        halo_copy(k).wait_send()
        face_left(4, k).wait_send()
        face_right(4, k).wait_send()
        face_left(5, k).wait_send()
        for f in range(3):
            back_left(f, k).wait_send()
            if f < 2:
                back_right(f, k).wait_send()
            for i in range(NY):
                corner_copy(f, k, i).wait_send()
            for i in range(1, NY):
                corner_forward(f, k, i).wait_send()

    chunks(drain)
    for t in range(2):
        for i in range(1, NSUB):
            sum_b(t, i).wait_send()
    for i in range(1, NGRP):
        sum_a(2, i).wait_send()

    stores = []
    for k, (rz, uw, us) in enumerate(get_sums(2)):
        beta = rz / rz1[k]
        den = uw + beta * (us + us) + beta * beta * den1[k]
        alpha = rz / den
        for i in range(1, PAIRS):
            here = (k, block(i))
            x[here] = x[here] + alpha * (u[here] + beta * p[here])
            r[here] = r[here] - alpha * (w[here] + beta * s[here])
        own = (k, pl.ds(H, SUBS * H))
        stores.append(pltpu.make_async_copy(x.at[own], x_h.at[k], load_sem.at[6 + 2 * k]))
        stores.append(pltpu.make_async_copy(r.at[own], res_h.at[k], load_sem.at[7 + 2 * k]))
        stores[-2].start()
        stores[-1].start()
    for i in range(1, NSUB):
        sum_b(2, i).wait_send()
    for copy in stores:
        copy.wait()


def turn(x_h, r_h, x_out, r_out, taken, given, load_sem, store_sem):
    def load(side, c):
        source = (x_h, r_h)[side].at[:, block(c)]
        return pltpu.make_async_copy(source, taken.at[side, c], load_sem.at[side, c])

    def store(side, c):
        target = (x_out, r_out)[side].at[0, c]
        return pltpu.make_async_copy(given.at[side, c], target, store_sem.at[side, c])

    parts = [(side, c) for c in range(SUBS) for side in range(2)]
    for part in parts:
        load(*part).start()
    for side, c in parts:
        load(side, c).wait()
        for k in range(CHUNKS):
            given[side, c, pl.ds(LANES * k, LANES)] = taken[side, c, k].T
        store(side, c).start()
    for part in parts:
        store(*part).wait()


def local(rhs, counts, solve_panel, dirichlet_panel, coupling, corner_map, coarse_inverse):
    vector = pltpu.VMEM((CHUNKS, PAIRS * H, LANES), F32)
    dma = pltpu.SemaphoreType.DMA
    anywhere = pl.BlockSpec(memory_space=pl.ANY)
    shape = jax.ShapeDtypeStruct((CHUNKS, SUBS * H, LANES), F32)
    x_turned, r_turned = pl.pallas_call(
        kernel,
        out_shape=(shape, shape),
        in_specs=[anywhere, pl.BlockSpec(memory_space=pltpu.SMEM)] + [anywhere] * 5,
        out_specs=(anywhere, anywhere),
        scratch_shapes=[
            pltpu.VMEM((PAIRS, 256, H), F32),
            pltpu.VMEM((SUBS, PS + 2 * NC, PS), BF16),
            pltpu.VMEM((SUBS, PS, PS), BF16),
            pltpu.VMEM((SUBS + 2, NC, PS), F32),
            pltpu.VMEM((256, NCO), F32),
            pltpu.VMEM((512, NCO), BF16),
            pltpu.VMEM((NGRP, SUBS, NC), I32),
            pltpu.VMEM((2, 8, LANES), I32),
            pltpu.VMEM((NCO, 256), BF16),
            pltpu.VMEM((NCO, 256), BF16),
            pltpu.VMEM((512, 512), BF16),
            pltpu.VMEM((2, NY, 256, 256), F32),
            pltpu.VMEM((NY, 512, 512), BF16),
            pltpu.VMEM((NY, NY, OWN, 256), F32),
            pltpu.VMEM((2, 2, OWN, 256), F32),
            pltpu.VMEM((2, NY, OWN, 256), F32),
            pltpu.VMEM((2 * OWN, NGRP * OWN), BF16),
            pltpu.VMEM((PAIRS, H, 8 * NC), BF16),
            pltpu.VMEM((PAIRS, H, LANES), F32),
            vector, vector, vector, vector, vector, vector, vector, vector, vector,
            pltpu.VMEM((CHUNKS, PAIRS * H, 2 * LANES), BF16),
            pltpu.VMEM((2, CHUNKS, SUBS, PS, LANES), F32),
            pltpu.VMEM((6, CHUNKS, H, LANES), F32),
            pltpu.VMEM((6, CHUNKS, H, LANES), F32),
            pltpu.VMEM((3, CHUNKS, NGRP, OWN, LANES), F32),
            pltpu.VMEM((3, CHUNKS, OWN, LANES), F32),
            pltpu.VMEM((3, CHUNKS, OWN + 2 * NC, LANES), F32),
            pltpu.VMEM((3, NGRP, 8, LANES), F32),
            pltpu.VMEM((3, NSUB, 8, LANES), F32),
            dma((10,)), dma((NGRP,)), dma((NGRP,)), dma((7,)), dma((7,)), dma((CHUNKS,)), dma((CHUNKS,)),
            dma((6, 2, CHUNKS)), dma((6, 2, CHUNKS)), dma((3, 2, CHUNKS)), dma((3, 2, CHUNKS)),
            dma((3, CHUNKS, 7)), dma((3, CHUNKS, 7)),
            dma((3, NGRP)), dma((3, NGRP)), dma((3, NSUB)), dma((3, NSUB)), dma((6,)), dma((6,)),
        ],
        compiler_params=pltpu.CompilerParams(
            collective_id=0, has_side_effects=True, vmem_limit_bytes=66_000_000
        ),
    )(rhs, counts, solve_panel, dirichlet_panel, coupling, corner_map, coarse_inverse)
    out = jax.ShapeDtypeStruct(rhs.shape, F32)
    return pl.pallas_call(
        turn,
        out_shape=(out, out),
        in_specs=[anywhere, anywhere],
        out_specs=(anywhere, anywhere),
        scratch_shapes=[
            pltpu.VMEM((2, SUBS, CHUNKS, H, LANES), F32),
            pltpu.VMEM((2, SUBS, CHUNKS * LANES, H), F32),
            dma((2, SUBS)), dma((2, SUBS)),
        ],
    )(x_turned, r_turned)


def solution(mesh):
    return jax.shard_map(
        local,
        mesh=mesh,
        in_specs=(
            P("grp", "sub", None, None),
            P("grp", "sub"),
            P("grp", "sub", None, None),
            P("grp", "sub", None, None),
            P("grp", "sub", None, None),
            P("grp", "sub", None),
            P("sub", "grp", None),
        ),
        out_specs=(P("grp", "sub", None, None), P("grp", "sub", None, None)),
        check_vma=False,
    )
```

```python
import jax
import jax.numpy as jnp
from jax import lax
from jax.experimental import pallas as pl
from jax.experimental.pallas import tpu as pltpu
from jax.sharding import PartitionSpec as P

MESH = pl.DeviceIdType.MESH
F32, BF16, I32 = jnp.float32, jnp.bfloat16, jnp.int32
NSUB, NGRP, NY = 16, 8, 4
SUBS, H, PS, NC, NCO = 4, 256, 512, 32, 2048
LANES, CHUNKS, PAIRS = 128, 2, 5
OWN = SUBS * NC
LEFT, RIGHT = 0, 1


def remote(src, dst, send_sem, recv_sem, device):
    return pltpu.make_async_remote_copy(
        src_ref=src,
        dst_ref=dst,
        send_sem=send_sem,
        recv_sem=recv_sem,
        device_id=device,
        device_id_type=MESH,
    )


def split(value):
    high = value.astype(BF16)
    low = (value - high.astype(F32)).astype(BF16)
    return high, low


def colsum(value):
    return jnp.sum(value, axis=0, keepdims=True)


def chunks(body):
    for k in range(CHUNKS):
        body(k)


def block(i):
    return pl.ds(H * i, H)


def kernel(
    rhs_h, counts_s, solve_h, dirichlet_h, coupling_h, map_h, coarse_h, x_h, res_h,
    rhs_v, sc, dm, cext, ci, cis, cmt, cnt, onehot_a, onehot_b, rowhot, a_part, a_split, g_part, ring_a, ring_b,
    gs, ext, mask, r, u, w, m0, n0, m1, p, s, x, vs, wb, from_left, from_right, corners, cown, bext, red_a, red_b,
    load_sem, cm_send, cm_recv, misc_send, misc_recv, halo_send, halo_recv, ex_send, ex_recv,
    bk_send, bk_recv, ag_send, ag_recv, ra_send, ra_recv, rb_send, rb_recv, ring_send, ring_recv,
):
    sub, grp = lax.axis_index("sub"), lax.axis_index("grp")
    right, left = lax.rem(sub + 1, NSUB), lax.rem(sub + NSUB - 1, NSUB)
    y, core = lax.div(grp, 2), lax.rem(grp, 2)
    mate = 2 * y + 1 - core
    up, down, far = lax.rem(y + 1, NY), lax.rem(y + 3, NY), lax.rem(y + 2, NY)
    to_right, to_left, to_mate = {"sub": right}, {"sub": left}, {"grp": mate}
    to_up, to_down = {"grp": 2 * up + core}, {"grp": 2 * down + core}

    barrier = pltpu.get_barrier_semaphore()
    for i in range(1, NGRP):
        pl.semaphore_signal(barrier, inc=1, device_id={"grp": lax.rem(grp + i, NGRP)}, device_id_type=MESH)
    for i in range(1, NSUB):
        pl.semaphore_signal(barrier, inc=1, device_id={"sub": lax.rem(sub + i, NSUB)}, device_id_type=MESH)

    loads = [
        pltpu.make_async_copy(map_h.at[0], cmt.at[grp], load_sem.at[0]),
        pltpu.make_async_copy(rhs_h.at[0], rhs_v.at[pl.ds(1, SUBS)], load_sem.at[1]),
        pltpu.make_async_copy(coarse_h.at[0], ci, load_sem.at[2]),
        pltpu.make_async_copy(dirichlet_h.at[0], dm, load_sem.at[3]),
        pltpu.make_async_copy(coupling_h.at[0], cext.at[pl.ds(1, SUBS)], load_sem.at[4]),
        pltpu.make_async_copy(solve_h.at[0], sc.at[:, pl.ds(0, PS)], load_sem.at[5]),
    ]
    for load in loads:
        load.start()

    def map_copy(i):
        peer = lax.rem(grp + i, NGRP)
        return remote(map_h.at[0], cmt.at[grp], cm_send.at[i], cm_recv.at[i], {"grp": peer})

    def map_arrival(i):
        slot = lax.rem(grp + NGRP - i, NGRP)
        return remote(map_h.at[0], cmt.at[slot], cm_send.at[i], cm_recv.at[i], to_mate)

    count_copy = remote(cnt.at[0], cnt.at[1], misc_send.at[0], misc_recv.at[0], to_right)
    cpl_right = remote(
        coupling_h.at[0, SUBS - 1, :, pl.ds(H, H)], cext.at[0, :, pl.ds(H, H)],
        misc_send.at[1], misc_recv.at[1], to_right,
    )
    cpl_left = remote(
        coupling_h.at[0, 0, :, pl.ds(0, H)], cext.at[SUBS + 1, :, pl.ds(0, H)],
        misc_send.at[2], misc_recv.at[2], to_left,
    )

    def mate_copy(q, mine=True):
        part = a_part.at[core if mine else 1 - core, q]
        return remote(part, part, misc_send.at[3 + q], misc_recv.at[3 + q], to_mate)

    def ring(stage, q):
        upward = (q < 2) == (stage != 1)
        if stage == 0:
            source, target = g_part.at[far, q], ring_a.at[q]
        else:
            source, target = g_part.at[up if upward else down, q], ring_b.at[0 if upward else 1, q]
        return remote(
            source, target, ring_send.at[stage, q], ring_recv.at[stage, q], to_up if upward else to_down
        )

    def halo_copy(k):
        part = pl.ds(LANES * k, LANES)
        return remote(
            rhs_h.at[0, SUBS - 1, part], rhs_v.at[0, part], halo_send.at[k], halo_recv.at[k], to_right
        )

    def face_left(op, k):
        return remote(
            wb.at[op % 2, k, 0, pl.ds(0, H)], from_right.at[op, k],
            ex_send.at[op, LEFT, k], ex_recv.at[op, LEFT, k], to_left,
        )

    def face_right(op, k):
        return remote(
            wb.at[op % 2, k, SUBS - 1, pl.ds(H, H)], from_left.at[op, k],
            ex_send.at[op, RIGHT, k], ex_recv.at[op, RIGHT, k], to_right,
        )

    def back_left(f, k):
        return remote(
            bext.at[f, k, pl.ds(NC, NC)], bext.at[f, k, pl.ds(NC + OWN, NC)],
            bk_send.at[f, LEFT, k], bk_recv.at[f, LEFT, k], to_left,
        )

    def back_right(f, k):
        return remote(
            bext.at[f, k, pl.ds(OWN, NC)], bext.at[f, k, pl.ds(0, NC)],
            bk_send.at[f, RIGHT, k], bk_recv.at[f, RIGHT, k], to_right,
        )

    def corner_link(f, k, i, part, device):
        return remote(part, part, ag_send.at[f, k, i], ag_recv.at[f, k, i], device)

    def corner_slot(f, k, chip, mine=True):
        return corners.at[f, k, 2 * chip + (core if mine else 1 - core)]

    def corner_copy(f, k, i):
        device = to_mate if i == 0 else {"grp": 2 * lax.rem(y + i, NY) + core}
        return corner_link(f, k, i, corner_slot(f, k, y), device)

    def corner_arrival(f, k, i):
        return corner_link(f, k, i, corner_slot(f, k, lax.rem(y + NY - i, NY), i > 0), to_mate)

    def corner_forward(f, k, i, mine=True):
        return corner_link(f, k, NY - 1 + i, corner_slot(f, k, lax.rem(y + NY - i, NY), mine), to_mate)

    def sum_a(t, i):
        mine = red_a.at[t, grp]
        return remote(mine, mine, ra_send.at[t, i], ra_recv.at[t, i], {"grp": lax.rem(grp + i, NGRP)})

    def sum_a_arrival(t, i):
        there = red_a.at[t, lax.rem(grp + NGRP - i, NGRP)]
        return remote(there, there, ra_send.at[t, i], ra_recv.at[t, i], to_mate)

    def sum_b(t, i):
        mine = red_b.at[t, sub]
        return remote(mine, mine, rb_send.at[t, i], rb_recv.at[t, i], {"sub": lax.rem(sub + i, NSUB)})

    def sum_b_arrival(t, i):
        there = red_b.at[t, lax.rem(sub + NSUB - i, NSUB)]
        return remote(there, there, rb_send.at[t, i], rb_recv.at[t, i], to_right)


    def apply_panel(op, k, j):
        solve = op % 2 == 1
        faces = vs[k, pl.ds(H * j, PS), :]
        both = jnp.dot((sc if solve else dm)[j], faces, preferred_element_type=F32)
        both = both[:, :LANES] + both[:, LANES:]
        wb[op % 2, k, j] = both[:PS]
        if solve:
            f = op // 2
            values = both[PS : PS + NC] + both[PS + NC :]
            cown[f, k, pl.ds(NC * j, NC)] = values
            corners[f, k, grp, pl.ds(NC * j, NC)] = values

    def put_faces(k, pairs, value):
        for i in pairs:
            high, low = split(value(k, i))
            vs[k, block(i), pl.ds(0, LANES)] = high
            vs[k, block(i), pl.ds(LANES, LANES)] = low

    def inner(op, value):
        for k in range(CHUNKS):
            put_faces(k, range(1, SUBS), value)
            apply_panel(op, k, 1)
            apply_panel(op, k, 2)

    def outer(op, value, last=False, parts=range(CHUNKS)):
        for k in parts:
            if op > 0:
                arrive(op - 1, k)
            if op >= 2:
                face_left(op - 2, k).wait_send()
                face_right(op - 2, k).wait_send()
            put_faces(k, (0, SUBS), value)
            apply_panel(op, k, 0)
            face_left(op, k).start()
            apply_panel(op, k, SUBS - 1)
            if op % 2 == 1:
                for i in (2, 1, 3, 0):
                    corner_copy(op // 2, k, i).start()
            if not last:
                face_right(op, k).start()

    def gather(f, k):
        for i in (1, 3, 2):
            corner_arrival(f, k, i).wait_recv()
            corner_forward(f, k, i).start()

    def coarse(f, k, last=False):
        corner_arrival(f, k, 0).wait_recv()
        for i in range(1, NY):
            corner_forward(f, k, i, False).wait_recv()
        high, low = split(corners[f, k].reshape(NGRP * OWN, LANES))
        both = jnp.dot(gs[...], jnp.concatenate([high, low], axis=1), preferred_element_type=F32)
        both = both[:, :LANES] + both[:, LANES:]
        bext[f, k, pl.ds(NC, OWN)] = both[:OWN] + both[OWN:]
        back_left(f, k).start()
        if not last:
            back_right(f, k).start()

    def all_coarse(f, last=False):
        for k in range(CHUNKS):
            gather(f, k)
        for k in range(CHUNKS):
            coarse(f, k, last)

    def image(op, k, i):
        before = from_left[op, k] if i == 0 else wb[op % 2, k, i - 1, pl.ds(H, H)]
        after = from_right[op, k] if i == SUBS else wb[op % 2, k, i, pl.ds(0, H)]
        value = before + after
        if op % 2 == 1:
            high, low = split(bext[op // 2, k, pl.ds(NC * i, 2 * NC)])
            faces = jnp.concatenate([high, low, high, low], axis=0)
            value = value + jnp.dot(ext[i], faces, preferred_element_type=F32)
        else:
            value = 0.25 * value
        return jnp.where(mask[i] > 0.0, value, 0.0)

    def arrive(op, k, last=False):
        face_left(op, k).wait_recv()
        if op % 2 == 1:
            back_left(op // 2, k).wait_recv()
        if not last:
            face_right(op, k).wait_recv()
            if op % 2 == 1:
                back_right(op // 2, k).wait_recv()

    def image_in(op, out):
        def value(k, i):
            result = image(op, k, i)
            out[k, block(i)] = result
            return result

        return value

    def product(first, second, k):
        return colsum(first[k, pl.ds(H, SUBS * H)] * second[k, pl.ds(H, SUBS * H)])

    def put_sums(t, k, values):
        for i, value in enumerate(values):
            red_a[t, grp, pl.ds(3 * k + i, 1)] = value

    def send_sums(t):
        for i in range(1, NGRP):
            sum_a(t, i).start()

    def pass_sums(t):
        for i in range(1, NGRP):
            sum_a_arrival(t, i).wait_recv()
        red_b[t, sub] = jnp.sum(red_a[t], axis=0)
        for i in range(1, NSUB):
            sum_b(t, i).start()

    def get_sums(t):
        for i in range(1, NSUB):
            sum_b_arrival(t, i).wait_recv()
        total = jnp.sum(red_b[t], axis=0)
        return [[total[3 * k + i : 3 * k + i + 1] for i in range(3)] for k in range(CHUNKS)]

    live = [counts_s[0, c] for c in range(SUBS)]
    live[SUBS - 1] = jnp.where(sub == NSUB - 1, 0, live[SUBS - 1])
    cnt[0] = jnp.full((8, LANES), live[SUBS - 1], I32)
    red_a[...] = jnp.zeros_like(red_a)
    pl.semaphore_wait(barrier, NGRP + NSUB - 2)
    for i in range(1, NGRP):
        map_copy(i).start()
    count_copy.start()
    chunks(lambda k: halo_copy(k).start())
    cpl_right.start()
    cpl_left.start()

    loads[2].wait()
    for i in range(4):
        high, low = split(ci[pl.ds(64 * i, 64)])
        cis[pl.ds(64 * i, 64)] = high
        cis[pl.ds(256 + 64 * i, 64)] = low
    rows = lax.broadcasted_iota(I32, (H, LANES), 0)
    for c in range(SUBS):
        mask[c + 1] = (rows < live[c]).astype(F32)
    loads[1].wait()
    for c in range(SUBS):
        turned = rhs_v[c + 1].T
        for k in range(CHUNKS):
            r[k, block(c + 1)] = jnp.where(
                mask[c + 1] > 0.0, turned[:, LANES * k : LANES * (k + 1)], 0.0
            )

    loads[3].wait()
    for j in range(SUBS):
        for a, b in ((0, 1), (1, 0)):
            dm[j, block(a), block(b)] = -dm[j, block(a), block(b)]

    def residual(k, i):
        if i == 0:
            halo_copy(k).wait_recv()
            turned = rhs_v[0, pl.ds(LANES * k, LANES)].T
            r[k, block(0)] = jnp.where(mask[0] > 0.0, turned, 0.0)
        return r[k, block(i)]

    inner(0, residual)

    loads[0].wait()
    for i in range(1, NGRP):
        map_arrival(i).wait_recv()

    def map_row(g):
        return jnp.concatenate([cmt[g, pl.ds(c, 1)] for c in range(SUBS)], axis=1)

    def fill(onehot, q):
        for c in range(2):
            wanted = map_row(2 * q + c)
            for t in range(NCO // 256):
                hit = rows + 256 * t == wanted
                onehot[pl.ds(256 * t, 256), pl.ds(LANES * c, LANES)] = hit.astype(F32).astype(BF16)

    slots = (onehot_a, onehot_b)
    order = (0, 2, 1, 3)

    def columns(n):
        q, onehot = order[n], slots[n % 2]
        both = jnp.dot(cis[...], onehot[...], preferred_element_type=F32)
        a_part[core, q] = both[:256] + both[256:]
        mate_copy(q).start()

    def rows_of(n):
        q = order[n]
        mate_copy(q, False).wait_recv()
        for c in range(2):
            high, low = split(a_part[c, q])
            a_split[q, block(c), pl.ds(0, 256)] = high
            a_split[q, block(c), pl.ds(256, 256)] = low
        both = jnp.dot(rowhot[...], a_split[q], preferred_element_type=F32)
        both = both[:, :256] + both[:, 256:]
        for chip in range(NY):
            g_part[chip, q] = both[LANES * chip : LANES * (chip + 1)]
        ring(0, q).start()
        ring(1, q).start()

    def add_row(q):
        ring(0, q).wait_recv()
        there = (up if q < 2 else down, q)
        g_part[there] = g_part[there] + ring_a[q]
        ring(2, q).start()

    fill(onehot_a, order[0])
    fill(onehot_b, order[1])
    columns(0)
    lane = lax.broadcasted_iota(I32, (LANES, LANES), 1).astype(F32)
    base = (2 * 256 * y).astype(F32)
    for q in range(NY):
        wanted = jnp.broadcast_to(map_row(2 * q + core), (LANES, LANES)).astype(F32).T
        for t in range(4):
            rowhot[pl.ds(LANES * q, LANES), pl.ds(LANES * t, LANES)] = (
                wanted == lane + (base + 128.0 * t)
            ).astype(F32).astype(BF16)
    fill(onehot_a, order[2])
    columns(1)
    rows_of(0)
    fill(onehot_b, order[3])
    columns(2)
    count_copy.wait_recv()
    mask[0] = (rows < cnt[1, pl.ds(0, 1)]).astype(F32)
    outer(0, residual, parts=(0,))
    rows_of(1)
    columns(3)
    outer(0, residual, parts=(1,))
    rows_of(2)
    rows_of(3)

    loads[5].wait()
    loads[4].wait()
    cpl_right.wait_recv()
    cpl_left.wait_recv()
    for j in range(SUBS):
        for a, b in ((0, 1), (1, 0)):
            sc[j, block(a), block(b)] = -sc[j, block(a), block(b)]
        for half in range(2):
            part = cext[j + 1, :, block(half)]
            high, low = split(part if half else -part)
            sc[j, pl.ds(PS, NC), block(half)] = high
            sc[j, pl.ds(PS + NC, NC), block(half)] = low

    inner(1, image_in(0, u))
    add_row(0)
    add_row(2)
    outer(1, image_in(0, u), parts=(0,))
    add_row(1)
    add_row(3)
    outer(1, image_in(0, u), parts=(1,))
    for i in range(PAIRS):
        both = jnp.concatenate([cext[i, :, block(1)], -cext[i + 1, :, block(0)]], axis=0)
        high = both.astype(BF16).astype(F32)
        low = both - high
        ext[i] = jnp.concatenate([high, high, low, low], axis=0).T.astype(BF16)
    chunks(lambda k: gather(0, k))
    for q in range(NY):
        ring(1, q).wait_recv()
        ring(2, q).wait_recv()
        high, low = split(g_part[y, q] + ring_b[0, q] + ring_b[1, q])
        gs[pl.ds(0, OWN), pl.ds(256 * q, 256)] = high
        gs[pl.ds(OWN, OWN), pl.ds(256 * q, 256)] = low

    chunks(lambda k: coarse(0, k))

    inner(2, image_in(1, w))
    outer(2, image_in(1, w))
    chunks(lambda k: put_sums(0, k, [product(r, u, k), product(u, w, k)]))
    send_sums(0)
    inner(3, image_in(2, m0))
    pass_sums(0)
    outer(3, image_in(2, m0))
    all_coarse(1)
    rz0, den0, alpha0 = [], [], []
    for rz, uw, _ in get_sums(0):
        rz0.append(rz)
        den0.append(uw)
        alpha0.append(rz / uw)

    def lowered(k, i):
        here = (k, block(i))
        s[here] = w[here]
        n0[here] = image(3, k, i)
        w[here] = w[here] - alpha0[k] * n0[here]
        return w[here]

    inner(4, lowered)
    outer(4, lowered)

    def fifth(k):
        for i in range(PAIRS):
            here = (k, block(i))
            p[here] = u[here]
            x[here] = alpha0[k] * u[here]
            r[here] = r[here] - alpha0[k] * s[here]
            u[here] = u[here] - alpha0[k] * m0[here]
        put_sums(1, k, [product(r, u, k), product(u, w, k), product(u, s, k)])

    chunks(fifth)
    send_sums(1)
    inner(5, image_in(4, m1))
    pass_sums(1)
    outer(5, image_in(4, m1), last=True)
    rz1, den1, alpha1 = [], [], []
    beta1 = []
    for k, (rz, uw, us) in enumerate(get_sums(1)):
        beta = rz / rz0[k]
        den = uw + beta * (us + us) + beta * beta * den0[k]
        rz1.append(rz)
        den1.append(den)
        beta1.append(beta)
        alpha1.append(rz / den)

    partial = []

    def seventh(k):
        alpha, beta = alpha1[k], beta1[k]
        for i in range(PAIRS):
            here = (k, block(i))
            p[here] = u[here] + beta * p[here]
            s[here] = w[here] + beta * s[here]
            x[here] = x[here] + alpha * p[here]
            r[here] = r[here] - alpha * s[here]
            u[here] = u[here] - alpha * (m1[here] + beta * m0[here])
            w[here] = w[here] - (alpha * beta) * n0[here]
        faces = jnp.zeros((1, LANES), F32)
        for j in range(SUBS):
            faces = faces + colsum(u[k, pl.ds(H * j, PS)] * wb[1, k, j])
        partial.append([product(r, u, k), product(u, w, k), product(u, s, k), faces])

    chunks(seventh)
    all_coarse(2, last=True)
    for k in range(CHUNKS):
        corner = cown[0, k] - alpha0[k] * cown[1, k] - alpha1[k] * (cown[2, k] + beta1[k] * cown[1, k])
        ru, uw, us, faces = partial[k]
        faces = faces + colsum(corner * bext[2, k, pl.ds(NC, OWN)])
        put_sums(2, k, [ru, uw - alpha1[k] * faces, us])
    send_sums(2)

    for i in range(1, NGRP):
        map_copy(i).wait_send()
    for copy in (count_copy, cpl_right, cpl_left):
        copy.wait_send()
    for q in range(NY):
        mate_copy(q).wait_send()
        for stage in range(3):
            ring(stage, q).wait_send()
    for t in range(2):
        for i in range(1, NGRP):
            sum_a(t, i).wait_send()
    pass_sums(2)

    def under(k):
        arrive(5, k, last=True)
        for i in range(1, PAIRS):
            here = (k, block(i))
            w[here] = w[here] - alpha1[k] * image(5, k, i)

    chunks(under)

    def drain(k):
        halo_copy(k).wait_send()
        face_left(4, k).wait_send()
        face_right(4, k).wait_send()
        face_left(5, k).wait_send()
        for f in range(3):
            back_left(f, k).wait_send()
            if f < 2:
                back_right(f, k).wait_send()
            for i in range(NY):
                corner_copy(f, k, i).wait_send()
            for i in range(1, NY):
                corner_forward(f, k, i).wait_send()

    chunks(drain)
    for t in range(2):
        for i in range(1, NSUB):
            sum_b(t, i).wait_send()
    for i in range(1, NGRP):
        sum_a(2, i).wait_send()

    stores = []
    for k, (rz, uw, us) in enumerate(get_sums(2)):
        beta = rz / rz1[k]
        den = uw + beta * (us + us) + beta * beta * den1[k]
        alpha = rz / den
        for i in range(1, PAIRS):
            here = (k, block(i))
            x[here] = x[here] + alpha * (u[here] + beta * p[here])
            r[here] = r[here] - alpha * (w[here] + beta * s[here])
        own = (k, pl.ds(H, SUBS * H))
        stores.append(pltpu.make_async_copy(x.at[own], x_h.at[k], load_sem.at[6 + 2 * k]))
        stores.append(pltpu.make_async_copy(r.at[own], res_h.at[k], load_sem.at[7 + 2 * k]))
        stores[-2].start()
        stores[-1].start()
    for i in range(1, NSUB):
        sum_b(2, i).wait_send()
    for copy in stores:
        copy.wait()


def turn(x_h, r_h, x_out, r_out, taken, given, load_sem, store_sem):
    def load(side, c):
        source = (x_h, r_h)[side].at[:, block(c)]
        return pltpu.make_async_copy(source, taken.at[side, c], load_sem.at[side, c])

    def store(side, c):
        target = (x_out, r_out)[side].at[0, c]
        return pltpu.make_async_copy(given.at[side, c], target, store_sem.at[side, c])

    parts = [(side, c) for c in range(SUBS) for side in range(2)]
    for part in parts:
        load(*part).start()
    for side, c in parts:
        load(side, c).wait()
        for k in range(CHUNKS):
            given[side, c, pl.ds(LANES * k, LANES)] = taken[side, c, k].T
        store(side, c).start()
    for part in parts:
        store(*part).wait()


def local(rhs, counts, solve_panel, dirichlet_panel, coupling, corner_map, coarse_inverse):
    vector = pltpu.VMEM((CHUNKS, PAIRS * H, LANES), F32)
    dma = pltpu.SemaphoreType.DMA
    anywhere = pl.BlockSpec(memory_space=pl.ANY)
    shape = jax.ShapeDtypeStruct((CHUNKS, SUBS * H, LANES), F32)
    x_turned, r_turned = pl.pallas_call(
        kernel,
        out_shape=(shape, shape),
        in_specs=[anywhere, pl.BlockSpec(memory_space=pltpu.SMEM)] + [anywhere] * 5,
        out_specs=(anywhere, anywhere),
        scratch_shapes=[
            pltpu.VMEM((PAIRS, 256, H), F32),
            pltpu.VMEM((SUBS, PS + 2 * NC, PS), BF16),
            pltpu.VMEM((SUBS, PS, PS), BF16),
            pltpu.VMEM((SUBS + 2, NC, PS), F32),
            pltpu.VMEM((256, NCO), F32),
            pltpu.VMEM((512, NCO), BF16),
            pltpu.VMEM((NGRP, SUBS, NC), I32),
            pltpu.VMEM((2, 8, LANES), I32),
            pltpu.VMEM((NCO, 256), BF16),
            pltpu.VMEM((NCO, 256), BF16),
            pltpu.VMEM((512, 512), BF16),
            pltpu.VMEM((2, NY, 256, 256), F32),
            pltpu.VMEM((NY, 512, 512), BF16),
            pltpu.VMEM((NY, NY, OWN, 256), F32),
            pltpu.VMEM((NY, OWN, 256), F32),
            pltpu.VMEM((2, NY, OWN, 256), F32),
            pltpu.VMEM((2 * OWN, NGRP * OWN), BF16),
            pltpu.VMEM((PAIRS, H, 8 * NC), BF16),
            pltpu.VMEM((PAIRS, H, LANES), F32),
            vector, vector, vector, vector, vector, vector, vector, vector, vector,
            pltpu.VMEM((CHUNKS, PAIRS * H, 2 * LANES), BF16),
            pltpu.VMEM((2, CHUNKS, SUBS, PS, LANES), F32),
            pltpu.VMEM((6, CHUNKS, H, LANES), F32),
            pltpu.VMEM((6, CHUNKS, H, LANES), F32),
            pltpu.VMEM((3, CHUNKS, NGRP, OWN, LANES), F32),
            pltpu.VMEM((3, CHUNKS, OWN, LANES), F32),
            pltpu.VMEM((3, CHUNKS, OWN + 2 * NC, LANES), F32),
            pltpu.VMEM((3, NGRP, 8, LANES), F32),
            pltpu.VMEM((3, NSUB, 8, LANES), F32),
            dma((10,)), dma((NGRP,)), dma((NGRP,)), dma((7,)), dma((7,)), dma((CHUNKS,)), dma((CHUNKS,)),
            dma((6, 2, CHUNKS)), dma((6, 2, CHUNKS)), dma((3, 2, CHUNKS)), dma((3, 2, CHUNKS)),
            dma((3, CHUNKS, 7)), dma((3, CHUNKS, 7)),
            dma((3, NGRP)), dma((3, NGRP)), dma((3, NSUB)), dma((3, NSUB)), dma((3, NY)), dma((3, NY)),
        ],
        compiler_params=pltpu.CompilerParams(
            collective_id=0, has_side_effects=True, vmem_limit_bytes=66_000_000
        ),
    )(rhs, counts, solve_panel, dirichlet_panel, coupling, corner_map, coarse_inverse)
    out = jax.ShapeDtypeStruct(rhs.shape, F32)
    return pl.pallas_call(
        turn,
        out_shape=(out, out),
        in_specs=[anywhere, anywhere],
        out_specs=(anywhere, anywhere),
        scratch_shapes=[
            pltpu.VMEM((2, SUBS, CHUNKS, H, LANES), F32),
            pltpu.VMEM((2, SUBS, CHUNKS * LANES, H), F32),
            dma((2, SUBS)), dma((2, SUBS)),
        ],
    )(x_turned, r_turned)


def solution(mesh):
    return jax.shard_map(
        local,
        mesh=mesh,
        in_specs=(
            P("grp", "sub", None, None),
            P("grp", "sub"),
            P("grp", "sub", None, None),
            P("grp", "sub", None, None),
            P("grp", "sub", None, None),
            P("grp", "sub", None),
            P("sub", "grp", None),
        ),
        out_specs=(P("grp", "sub", None, None), P("grp", "sub", None, None)),
        check_vma=False,
    )
```

```python
import jax
import jax.numpy as jnp
from jax import lax
from jax.experimental import pallas as pl
from jax.experimental.pallas import tpu as pltpu
from jax.sharding import PartitionSpec as P

MESH = pl.DeviceIdType.MESH
F32, BF16, I32 = jnp.float32, jnp.bfloat16, jnp.int32
NSUB, NGRP, NY = 16, 8, 4
SUBS, H, PS, NC, NCO = 4, 256, 512, 32, 2048
LANES, CHUNKS, PAIRS = 128, 2, 5
OWN = SUBS * NC
LEFT, RIGHT = 0, 1


def remote(src, dst, send_sem, recv_sem, device):
    return pltpu.make_async_remote_copy(
        src_ref=src,
        dst_ref=dst,
        send_sem=send_sem,
        recv_sem=recv_sem,
        device_id=device,
        device_id_type=MESH,
    )


def split(value):
    high = value.astype(BF16)
    low = (value - high.astype(F32)).astype(BF16)
    return high, low


def colsum(value):
    return jnp.sum(value, axis=0, keepdims=True)


def chunks(body):
    for k in range(CHUNKS):
        body(k)


def block(i):
    return pl.ds(H * i, H)


def kernel(
    rhs_h, counts_s, solve_h, dirichlet_h, coupling_h, map_h, coarse_h, x_h, res_h,
    rhs_v, sc, dm, cext, ci, cis, cmt, cnt, onehot_a, onehot_b, rowhot, a_part, a_split, g_part, ring_a, ring_b,
    gs, ext, mask, r, u, w, m0, n0, m1, p, s, x, vs, wb, from_left, from_right, corners, cown, bext, red_a, red_b,
    load_sem, cm_send, cm_recv, misc_send, misc_recv, halo_send, halo_recv, ex_send, ex_recv,
    bk_send, bk_recv, ag_send, ag_recv, ra_send, ra_recv, rb_send, rb_recv, ring_send, ring_recv,
):
    sub, grp = lax.axis_index("sub"), lax.axis_index("grp")
    right, left = lax.rem(sub + 1, NSUB), lax.rem(sub + NSUB - 1, NSUB)
    y, core = lax.div(grp, 2), lax.rem(grp, 2)
    mate = 2 * y + 1 - core
    up, down, far = lax.rem(y + 1, NY), lax.rem(y + 3, NY), lax.rem(y + 2, NY)
    to_right, to_left, to_mate = {"sub": right}, {"sub": left}, {"grp": mate}
    to_up, to_down = {"grp": 2 * up + core}, {"grp": 2 * down + core}

    barrier = pltpu.get_barrier_semaphore()
    for i in range(1, NGRP):
        pl.semaphore_signal(barrier, inc=1, device_id={"grp": lax.rem(grp + i, NGRP)}, device_id_type=MESH)
    for i in range(1, NSUB):
        pl.semaphore_signal(barrier, inc=1, device_id={"sub": lax.rem(sub + i, NSUB)}, device_id_type=MESH)

    loads = [
        pltpu.make_async_copy(map_h.at[0], cmt.at[grp], load_sem.at[0]),
        pltpu.make_async_copy(rhs_h.at[0], rhs_v.at[pl.ds(1, SUBS)], load_sem.at[1]),
        pltpu.make_async_copy(coarse_h.at[0], ci, load_sem.at[2]),
        pltpu.make_async_copy(dirichlet_h.at[0], dm, load_sem.at[3]),
        pltpu.make_async_copy(coupling_h.at[0], cext.at[pl.ds(1, SUBS)], load_sem.at[4]),
        pltpu.make_async_copy(solve_h.at[0], sc.at[:, pl.ds(0, PS)], load_sem.at[5]),
    ]
    for load in loads:
        load.start()

    def map_copy(i):
        peer = lax.rem(grp + i, NGRP)
        return remote(map_h.at[0], cmt.at[grp], cm_send.at[i], cm_recv.at[i], {"grp": peer})

    def map_arrival(i):
        slot = lax.rem(grp + NGRP - i, NGRP)
        return remote(map_h.at[0], cmt.at[slot], cm_send.at[i], cm_recv.at[i], to_mate)

    count_copy = remote(cnt.at[0], cnt.at[1], misc_send.at[0], misc_recv.at[0], to_right)
    cpl_right = remote(
        coupling_h.at[0, SUBS - 1, :, pl.ds(H, H)], cext.at[0, :, pl.ds(H, H)],
        misc_send.at[1], misc_recv.at[1], to_right,
    )
    cpl_left = remote(
        coupling_h.at[0, 0, :, pl.ds(0, H)], cext.at[SUBS + 1, :, pl.ds(0, H)],
        misc_send.at[2], misc_recv.at[2], to_left,
    )

    def mate_copy(q, mine=True):
        part = a_part.at[core if mine else 1 - core, q]
        return remote(part, part, misc_send.at[3 + q], misc_recv.at[3 + q], to_mate)

    def ring(stage, q):
        upward = (q < 2) == (stage != 1)
        if stage == 0:
            source, target = g_part.at[far, q], ring_a.at[q]
        else:
            source, target = g_part.at[up if upward else down, q], ring_b.at[0 if upward else 1, q]
        return remote(
            source, target, ring_send.at[stage, q], ring_recv.at[stage, q], to_up if upward else to_down
        )

    def halo_copy(k):
        part = pl.ds(LANES * k, LANES)
        return remote(
            rhs_h.at[0, SUBS - 1, part], rhs_v.at[0, part], halo_send.at[k], halo_recv.at[k], to_right
        )

    def face_left(op, k):
        return remote(
            wb.at[op % 2, k, 0, pl.ds(0, H)], from_right.at[op, k],
            ex_send.at[op, LEFT, k], ex_recv.at[op, LEFT, k], to_left,
        )

    def face_right(op, k):
        return remote(
            wb.at[op % 2, k, SUBS - 1, pl.ds(H, H)], from_left.at[op, k],
            ex_send.at[op, RIGHT, k], ex_recv.at[op, RIGHT, k], to_right,
        )

    def back_left(f, k):
        return remote(
            bext.at[f, k, pl.ds(NC, NC)], bext.at[f, k, pl.ds(NC + OWN, NC)],
            bk_send.at[f, LEFT, k], bk_recv.at[f, LEFT, k], to_left,
        )

    def back_right(f, k):
        return remote(
            bext.at[f, k, pl.ds(OWN, NC)], bext.at[f, k, pl.ds(0, NC)],
            bk_send.at[f, RIGHT, k], bk_recv.at[f, RIGHT, k], to_right,
        )

    def corner_link(f, k, i, part, device):
        return remote(part, part, ag_send.at[f, k, i], ag_recv.at[f, k, i], device)

    def corner_slot(f, k, chip, mine=True):
        return corners.at[f, k, 2 * chip + (core if mine else 1 - core)]

    def corner_copy(f, k, i):
        device = to_mate if i == 0 else {"grp": 2 * lax.rem(y + i, NY) + core}
        return corner_link(f, k, i, corner_slot(f, k, y), device)

    def corner_arrival(f, k, i):
        return corner_link(f, k, i, corner_slot(f, k, lax.rem(y + NY - i, NY), i > 0), to_mate)

    def corner_forward(f, k, i, mine=True):
        return corner_link(f, k, NY - 1 + i, corner_slot(f, k, lax.rem(y + NY - i, NY), mine), to_mate)

    def sum_a(t, i):
        mine = red_a.at[t, grp]
        return remote(mine, mine, ra_send.at[t, i], ra_recv.at[t, i], {"grp": lax.rem(grp + i, NGRP)})

    def sum_a_arrival(t, i):
        there = red_a.at[t, lax.rem(grp + NGRP - i, NGRP)]
        return remote(there, there, ra_send.at[t, i], ra_recv.at[t, i], to_mate)

    def sum_b(t, i):
        mine = red_b.at[t, sub]
        return remote(mine, mine, rb_send.at[t, i], rb_recv.at[t, i], {"sub": lax.rem(sub + i, NSUB)})

    def sum_b_arrival(t, i):
        there = red_b.at[t, lax.rem(sub + NSUB - i, NSUB)]
        return remote(there, there, rb_send.at[t, i], rb_recv.at[t, i], to_right)


    def panel_rows(op, k, j, first, count):
        panel = (sc if op % 2 == 1 else dm)[j, pl.ds(first, count)]
        both = jnp.dot(panel, vs[k, pl.ds(H * j, PS), :], preferred_element_type=F32)
        return both[:, :LANES] + both[:, LANES:]

    def put_corner(op, k, j, both):
        f = op // 2
        values = both[:NC] + both[NC:]
        cown[f, k, pl.ds(NC * j, NC)] = values
        corners[f, k, grp, pl.ds(NC * j, NC)] = values

    def apply_panel(op, k, j):
        both = panel_rows(op, k, j, 0, PS + (2 * NC if op % 2 == 1 else 0))
        wb[op % 2, k, j] = both[:PS]
        if op % 2 == 1:
            put_corner(op, k, j, both[PS:])

    def apply_half(op, k, j, half):
        wb[op % 2, k, j, block(half)] = panel_rows(op, k, j, H * half, H)

    def put_faces(k, pairs, value):
        for i in pairs:
            high, low = split(value(k, i))
            vs[k, block(i), pl.ds(0, LANES)] = high
            vs[k, block(i), pl.ds(LANES, LANES)] = low

    def inner(op, value):
        for k in range(CHUNKS):
            put_faces(k, range(1, SUBS), value)
            apply_panel(op, k, 1)
            apply_panel(op, k, 2)

    def outer(op, value, last=False, parts=range(CHUNKS)):
        for k in parts:
            if op > 0:
                arrive(op - 1, k)
            if op >= 2:
                face_left(op - 2, k).wait_send()
                face_right(op - 2, k).wait_send()
            put_faces(k, (0, SUBS), value)
            if op % 2 == 1:
                for j in (0, SUBS - 1):
                    put_corner(op, k, j, panel_rows(op, k, j, PS, 2 * NC))
                for i in (2, 1, 3, 0):
                    corner_copy(op // 2, k, i).start()
            apply_half(op, k, 0, 0)
            face_left(op, k).start()
            apply_half(op, k, SUBS - 1, 1)
            if not last:
                face_right(op, k).start()
            apply_half(op, k, 0, 1)
            apply_half(op, k, SUBS - 1, 0)

    def gather(f, k):
        for i in (1, 3, 2):
            corner_arrival(f, k, i).wait_recv()
            corner_forward(f, k, i).start()

    def coarse(f, k, last=False):
        corner_arrival(f, k, 0).wait_recv()
        for i in range(1, NY):
            corner_forward(f, k, i, False).wait_recv()
        high, low = split(corners[f, k].reshape(NGRP * OWN, LANES))
        both = jnp.dot(gs[...], jnp.concatenate([high, low], axis=1), preferred_element_type=F32)
        both = both[:, :LANES] + both[:, LANES:]
        bext[f, k, pl.ds(NC, OWN)] = both[:OWN] + both[OWN:]
        back_left(f, k).start()
        if not last:
            back_right(f, k).start()

    def all_coarse(f, last=False):
        for k in range(CHUNKS):
            gather(f, k)
        for k in range(CHUNKS):
            coarse(f, k, last)

    def image(op, k, i):
        before = from_left[op, k] if i == 0 else wb[op % 2, k, i - 1, pl.ds(H, H)]
        after = from_right[op, k] if i == SUBS else wb[op % 2, k, i, pl.ds(0, H)]
        value = before + after
        if op % 2 == 1:
            high, low = split(bext[op // 2, k, pl.ds(NC * i, 2 * NC)])
            faces = jnp.concatenate([high, low, high, low], axis=0)
            value = value + jnp.dot(ext[i], faces, preferred_element_type=F32)
        else:
            value = 0.25 * value
        return jnp.where(mask[i] > 0.0, value, 0.0)

    def arrive(op, k, last=False):
        face_left(op, k).wait_recv()
        if op % 2 == 1:
            back_left(op // 2, k).wait_recv()
        if not last:
            face_right(op, k).wait_recv()
            if op % 2 == 1:
                back_right(op // 2, k).wait_recv()

    def image_in(op, out):
        def value(k, i):
            result = image(op, k, i)
            out[k, block(i)] = result
            return result

        return value

    def product(first, second, k):
        return colsum(first[k, pl.ds(H, SUBS * H)] * second[k, pl.ds(H, SUBS * H)])

    def put_sums(t, k, values):
        for i, value in enumerate(values):
            red_a[t, grp, pl.ds(3 * k + i, 1)] = value

    def send_sums(t):
        for i in range(1, NGRP):
            sum_a(t, i).start()

    def pass_sums(t):
        for i in range(1, NGRP):
            sum_a_arrival(t, i).wait_recv()
        red_b[t, sub] = jnp.sum(red_a[t], axis=0)
        for i in range(1, NSUB):
            sum_b(t, i).start()

    def get_sums(t):
        for i in range(1, NSUB):
            sum_b_arrival(t, i).wait_recv()
        total = jnp.sum(red_b[t], axis=0)
        return [[total[3 * k + i : 3 * k + i + 1] for i in range(3)] for k in range(CHUNKS)]

    live = [counts_s[0, c] for c in range(SUBS)]
    live[SUBS - 1] = jnp.where(sub == NSUB - 1, 0, live[SUBS - 1])
    cnt[0] = jnp.full((8, LANES), live[SUBS - 1], I32)
    red_a[...] = jnp.zeros_like(red_a)
    pl.semaphore_wait(barrier, NGRP + NSUB - 2)
    for i in range(1, NGRP):
        map_copy(i).start()
    count_copy.start()
    chunks(lambda k: halo_copy(k).start())
    cpl_right.start()
    cpl_left.start()

    loads[2].wait()
    for i in range(4):
        high, low = split(ci[pl.ds(64 * i, 64)])
        cis[pl.ds(64 * i, 64)] = high
        cis[pl.ds(256 + 64 * i, 64)] = low
    rows = lax.broadcasted_iota(I32, (H, LANES), 0)
    for c in range(SUBS):
        mask[c + 1] = (rows < live[c]).astype(F32)
    loads[1].wait()
    for c in range(SUBS):
        turned = rhs_v[c + 1].T
        for k in range(CHUNKS):
            r[k, block(c + 1)] = jnp.where(
                mask[c + 1] > 0.0, turned[:, LANES * k : LANES * (k + 1)], 0.0
            )

    loads[3].wait()
    for j in range(SUBS):
        for a, b in ((0, 1), (1, 0)):
            dm[j, block(a), block(b)] = -dm[j, block(a), block(b)]

    def residual(k, i):
        if i == 0:
            halo_copy(k).wait_recv()
            turned = rhs_v[0, pl.ds(LANES * k, LANES)].T
            r[k, block(0)] = jnp.where(mask[0] > 0.0, turned, 0.0)
        return r[k, block(i)]

    inner(0, residual)

    loads[0].wait()
    for i in range(1, NGRP):
        map_arrival(i).wait_recv()

    def map_row(g):
        return jnp.concatenate([cmt[g, pl.ds(c, 1)] for c in range(SUBS)], axis=1)

    def fill(onehot, q):
        for c in range(2):
            wanted = map_row(2 * q + c)
            for t in range(NCO // 256):
                hit = rows + 256 * t == wanted
                onehot[pl.ds(256 * t, 256), pl.ds(LANES * c, LANES)] = hit.astype(F32).astype(BF16)

    slots = (onehot_a, onehot_b)
    order = (0, 2, 1, 3)

    def columns(n):
        q, onehot = order[n], slots[n % 2]
        both = jnp.dot(cis[...], onehot[...], preferred_element_type=F32)
        a_part[core, q] = both[:256] + both[256:]
        mate_copy(q).start()

    def rows_of(n):
        q = order[n]
        mate_copy(q, False).wait_recv()
        for c in range(2):
            high, low = split(a_part[c, q])
            a_split[q, block(c), pl.ds(0, 256)] = high
            a_split[q, block(c), pl.ds(256, 256)] = low
        both = jnp.dot(rowhot[...], a_split[q], preferred_element_type=F32)
        both = both[:, :256] + both[:, 256:]
        for chip in range(NY):
            g_part[chip, q] = both[LANES * chip : LANES * (chip + 1)]
        ring(0, q).start()
        ring(1, q).start()

    def add_row(q):
        ring(0, q).wait_recv()
        there = (up if q < 2 else down, q)
        g_part[there] = g_part[there] + ring_a[q]
        ring(2, q).start()

    fill(onehot_a, order[0])
    fill(onehot_b, order[1])
    columns(0)
    lane = lax.broadcasted_iota(I32, (LANES, LANES), 1).astype(F32)
    base = (2 * 256 * y).astype(F32)
    for q in range(NY):
        wanted = jnp.broadcast_to(map_row(2 * q + core), (LANES, LANES)).astype(F32).T
        for t in range(4):
            rowhot[pl.ds(LANES * q, LANES), pl.ds(LANES * t, LANES)] = (
                wanted == lane + (base + 128.0 * t)
            ).astype(F32).astype(BF16)
    fill(onehot_a, order[2])
    columns(1)
    rows_of(0)
    fill(onehot_b, order[3])
    columns(2)
    count_copy.wait_recv()
    mask[0] = (rows < cnt[1, pl.ds(0, 1)]).astype(F32)
    outer(0, residual, parts=(0,))
    rows_of(1)
    columns(3)
    outer(0, residual, parts=(1,))
    rows_of(2)
    rows_of(3)

    loads[5].wait()
    loads[4].wait()
    cpl_right.wait_recv()
    cpl_left.wait_recv()
    for j in range(SUBS):
        for a, b in ((0, 1), (1, 0)):
            sc[j, block(a), block(b)] = -sc[j, block(a), block(b)]
        for half in range(2):
            part = cext[j + 1, :, block(half)]
            high, low = split(part if half else -part)
            sc[j, pl.ds(PS, NC), block(half)] = high
            sc[j, pl.ds(PS + NC, NC), block(half)] = low

    inner(1, image_in(0, u))
    add_row(0)
    add_row(2)
    outer(1, image_in(0, u), parts=(0,))
    add_row(1)
    add_row(3)
    outer(1, image_in(0, u), parts=(1,))
    for i in range(PAIRS):
        both = jnp.concatenate([cext[i, :, block(1)], -cext[i + 1, :, block(0)]], axis=0)
        high = both.astype(BF16).astype(F32)
        low = both - high
        ext[i] = jnp.concatenate([high, high, low, low], axis=0).T.astype(BF16)
    chunks(lambda k: gather(0, k))
    for q in range(NY):
        ring(1, q).wait_recv()
        ring(2, q).wait_recv()
        high, low = split(g_part[y, q] + ring_b[0, q] + ring_b[1, q])
        gs[pl.ds(0, OWN), pl.ds(256 * q, 256)] = high
        gs[pl.ds(OWN, OWN), pl.ds(256 * q, 256)] = low

    chunks(lambda k: coarse(0, k))

    inner(2, image_in(1, w))
    outer(2, image_in(1, w))
    chunks(lambda k: put_sums(0, k, [product(r, u, k), product(u, w, k)]))
    send_sums(0)
    inner(3, image_in(2, m0))
    pass_sums(0)
    outer(3, image_in(2, m0))
    all_coarse(1)
    rz0, den0, alpha0 = [], [], []
    for rz, uw, _ in get_sums(0):
        rz0.append(rz)
        den0.append(uw)
        alpha0.append(rz / uw)

    def lowered(k, i):
        here = (k, block(i))
        s[here] = w[here]
        n0[here] = image(3, k, i)
        w[here] = w[here] - alpha0[k] * n0[here]
        return w[here]

    inner(4, lowered)
    outer(4, lowered)

    def fifth(k):
        for i in range(PAIRS):
            here = (k, block(i))
            p[here] = u[here]
            x[here] = alpha0[k] * u[here]
            r[here] = r[here] - alpha0[k] * s[here]
            u[here] = u[here] - alpha0[k] * m0[here]
        put_sums(1, k, [product(r, u, k), product(u, w, k), product(u, s, k)])

    chunks(fifth)
    send_sums(1)
    inner(5, image_in(4, m1))
    pass_sums(1)
    outer(5, image_in(4, m1), last=True)
    rz1, den1, alpha1 = [], [], []
    beta1 = []
    for k, (rz, uw, us) in enumerate(get_sums(1)):
        beta = rz / rz0[k]
        den = uw + beta * (us + us) + beta * beta * den0[k]
        rz1.append(rz)
        den1.append(den)
        beta1.append(beta)
        alpha1.append(rz / den)

    partial = []

    def seventh(k):
        alpha, beta = alpha1[k], beta1[k]
        for i in range(PAIRS):
            here = (k, block(i))
            p[here] = u[here] + beta * p[here]
            s[here] = w[here] + beta * s[here]
            x[here] = x[here] + alpha * p[here]
            r[here] = r[here] - alpha * s[here]
            u[here] = u[here] - alpha * (m1[here] + beta * m0[here])
            w[here] = w[here] - (alpha * beta) * n0[here]
        faces = jnp.zeros((1, LANES), F32)
        for j in range(SUBS):
            faces = faces + colsum(u[k, pl.ds(H * j, PS)] * wb[1, k, j])
        partial.append([product(r, u, k), product(u, w, k), product(u, s, k), faces])

    chunks(seventh)
    all_coarse(2, last=True)
    for k in range(CHUNKS):
        corner = cown[0, k] - alpha0[k] * cown[1, k] - alpha1[k] * (cown[2, k] + beta1[k] * cown[1, k])
        ru, uw, us, faces = partial[k]
        faces = faces + colsum(corner * bext[2, k, pl.ds(NC, OWN)])
        put_sums(2, k, [ru, uw - alpha1[k] * faces, us])
    send_sums(2)

    for i in range(1, NGRP):
        map_copy(i).wait_send()
    for copy in (count_copy, cpl_right, cpl_left):
        copy.wait_send()
    for q in range(NY):
        mate_copy(q).wait_send()
        for stage in range(3):
            ring(stage, q).wait_send()
    for t in range(2):
        for i in range(1, NGRP):
            sum_a(t, i).wait_send()
    pass_sums(2)

    def under(k):
        arrive(5, k, last=True)
        for i in range(1, PAIRS):
            here = (k, block(i))
            w[here] = w[here] - alpha1[k] * image(5, k, i)

    chunks(under)

    def drain(k):
        halo_copy(k).wait_send()
        face_left(4, k).wait_send()
        face_right(4, k).wait_send()
        face_left(5, k).wait_send()
        for f in range(3):
            back_left(f, k).wait_send()
            if f < 2:
                back_right(f, k).wait_send()
            for i in range(NY):
                corner_copy(f, k, i).wait_send()
            for i in range(1, NY):
                corner_forward(f, k, i).wait_send()

    chunks(drain)
    for t in range(2):
        for i in range(1, NSUB):
            sum_b(t, i).wait_send()
    for i in range(1, NGRP):
        sum_a(2, i).wait_send()

    stores = []
    for k, (rz, uw, us) in enumerate(get_sums(2)):
        beta = rz / rz1[k]
        den = uw + beta * (us + us) + beta * beta * den1[k]
        alpha = rz / den
        for i in range(1, PAIRS):
            here = (k, block(i))
            x[here] = x[here] + alpha * (u[here] + beta * p[here])
            r[here] = r[here] - alpha * (w[here] + beta * s[here])
        own = (k, pl.ds(H, SUBS * H))
        stores.append(pltpu.make_async_copy(x.at[own], x_h.at[k], load_sem.at[6 + 2 * k]))
        stores.append(pltpu.make_async_copy(r.at[own], res_h.at[k], load_sem.at[7 + 2 * k]))
        stores[-2].start()
        stores[-1].start()
    for i in range(1, NSUB):
        sum_b(2, i).wait_send()
    for copy in stores:
        copy.wait()


def turn(x_h, r_h, x_out, r_out, taken, given, load_sem, store_sem):
    def load(side, c):
        source = (x_h, r_h)[side].at[:, block(c)]
        return pltpu.make_async_copy(source, taken.at[side, c], load_sem.at[side, c])

    def store(side, c):
        target = (x_out, r_out)[side].at[0, c]
        return pltpu.make_async_copy(given.at[side, c], target, store_sem.at[side, c])

    parts = [(side, c) for c in range(SUBS) for side in range(2)]
    for part in parts:
        load(*part).start()
    for side, c in parts:
        load(side, c).wait()
        for k in range(CHUNKS):
            given[side, c, pl.ds(LANES * k, LANES)] = taken[side, c, k].T
        store(side, c).start()
    for part in parts:
        store(*part).wait()


def local(rhs, counts, solve_panel, dirichlet_panel, coupling, corner_map, coarse_inverse):
    vector = pltpu.VMEM((CHUNKS, PAIRS * H, LANES), F32)
    dma = pltpu.SemaphoreType.DMA
    anywhere = pl.BlockSpec(memory_space=pl.ANY)
    shape = jax.ShapeDtypeStruct((CHUNKS, SUBS * H, LANES), F32)
    x_turned, r_turned = pl.pallas_call(
        kernel,
        out_shape=(shape, shape),
        in_specs=[anywhere, pl.BlockSpec(memory_space=pltpu.SMEM)] + [anywhere] * 5,
        out_specs=(anywhere, anywhere),
        scratch_shapes=[
            pltpu.VMEM((PAIRS, 256, H), F32),
            pltpu.VMEM((SUBS, PS + 2 * NC, PS), BF16),
            pltpu.VMEM((SUBS, PS, PS), BF16),
            pltpu.VMEM((SUBS + 2, NC, PS), F32),
            pltpu.VMEM((256, NCO), F32),
            pltpu.VMEM((512, NCO), BF16),
            pltpu.VMEM((NGRP, SUBS, NC), I32),
            pltpu.VMEM((2, 8, LANES), I32),
            pltpu.VMEM((NCO, 256), BF16),
            pltpu.VMEM((NCO, 256), BF16),
            pltpu.VMEM((512, 512), BF16),
            pltpu.VMEM((2, NY, 256, 256), F32),
            pltpu.VMEM((NY, 512, 512), BF16),
            pltpu.VMEM((NY, NY, OWN, 256), F32),
            pltpu.VMEM((NY, OWN, 256), F32),
            pltpu.VMEM((2, NY, OWN, 256), F32),
            pltpu.VMEM((2 * OWN, NGRP * OWN), BF16),
            pltpu.VMEM((PAIRS, H, 8 * NC), BF16),
            pltpu.VMEM((PAIRS, H, LANES), F32),
            vector, vector, vector, vector, vector, vector, vector, vector, vector,
            pltpu.VMEM((CHUNKS, PAIRS * H, 2 * LANES), BF16),
            pltpu.VMEM((2, CHUNKS, SUBS, PS, LANES), F32),
            pltpu.VMEM((6, CHUNKS, H, LANES), F32),
            pltpu.VMEM((6, CHUNKS, H, LANES), F32),
            pltpu.VMEM((3, CHUNKS, NGRP, OWN, LANES), F32),
            pltpu.VMEM((3, CHUNKS, OWN, LANES), F32),
            pltpu.VMEM((3, CHUNKS, OWN + 2 * NC, LANES), F32),
            pltpu.VMEM((3, NGRP, 8, LANES), F32),
            pltpu.VMEM((3, NSUB, 8, LANES), F32),
            dma((10,)), dma((NGRP,)), dma((NGRP,)), dma((7,)), dma((7,)), dma((CHUNKS,)), dma((CHUNKS,)),
            dma((6, 2, CHUNKS)), dma((6, 2, CHUNKS)), dma((3, 2, CHUNKS)), dma((3, 2, CHUNKS)),
            dma((3, CHUNKS, 7)), dma((3, CHUNKS, 7)),
            dma((3, NGRP)), dma((3, NGRP)), dma((3, NSUB)), dma((3, NSUB)), dma((3, NY)), dma((3, NY)),
        ],
        compiler_params=pltpu.CompilerParams(
            collective_id=0, has_side_effects=True, vmem_limit_bytes=66_000_000
        ),
    )(rhs, counts, solve_panel, dirichlet_panel, coupling, corner_map, coarse_inverse)
    out = jax.ShapeDtypeStruct(rhs.shape, F32)
    return pl.pallas_call(
        turn,
        out_shape=(out, out),
        in_specs=[anywhere, anywhere],
        out_specs=(anywhere, anywhere),
        scratch_shapes=[
            pltpu.VMEM((2, SUBS, CHUNKS, H, LANES), F32),
            pltpu.VMEM((2, SUBS, CHUNKS * LANES, H), F32),
            dma((2, SUBS)), dma((2, SUBS)),
        ],
    )(x_turned, r_turned)


def solution(mesh):
    return jax.shard_map(
        local,
        mesh=mesh,
        in_specs=(
            P("grp", "sub", None, None),
            P("grp", "sub"),
            P("grp", "sub", None, None),
            P("grp", "sub", None, None),
            P("grp", "sub", None, None),
            P("grp", "sub", None),
            P("sub", "grp", None),
        ),
        out_specs=(P("grp", "sub", None, None), P("grp", "sub", None, None)),
        check_vma=False,
    )
```

```python
import jax
import jax.numpy as jnp
from jax import lax
from jax.experimental import pallas as pl
from jax.experimental.pallas import tpu as pltpu
from jax.sharding import PartitionSpec as P

MESH = pl.DeviceIdType.MESH
F32, BF16, I32 = jnp.float32, jnp.bfloat16, jnp.int32
NSUB, NGRP, NY = 16, 8, 4
SUBS, H, PS, NC, NCO = 4, 256, 512, 32, 2048
LANES, CHUNKS, PAIRS = 128, 2, 5
OWN = SUBS * NC
LEFT, RIGHT = 0, 1


def remote(src, dst, send_sem, recv_sem, device):
    return pltpu.make_async_remote_copy(
        src_ref=src,
        dst_ref=dst,
        send_sem=send_sem,
        recv_sem=recv_sem,
        device_id=device,
        device_id_type=MESH,
    )


def split(value):
    high = value.astype(BF16)
    low = (value - high.astype(F32)).astype(BF16)
    return high, low


def colsum(value):
    return jnp.sum(value, axis=0, keepdims=True)


def chunks(body):
    for k in range(CHUNKS):
        body(k)


def block(i):
    return pl.ds(H * i, H)


def kernel(
    rhs_h, counts_s, solve_h, dirichlet_h, coupling_h, map_h, coarse_h, x_h, res_h,
    rhs_v, sc, dm, cext, ci, cis, cmt, cnt, onehot_a, onehot_b, rowhot, a_part, a_split, g_part, ring_a, ring_b,
    gs, ps, shared, shares, ext, mask, r, u, w, m0, n0, m1, p, s, x, vs, wb, from_left, from_right, corners, cown, bext, red_a, red_b,
    load_sem, cm_send, cm_recv, misc_send, misc_recv, halo_send, halo_recv, ex_send, ex_recv,
    bk_send, bk_recv, ag_send, ag_recv, ra_send, ra_recv, rb_send, rb_recv, ring_send, ring_recv,
    share_send, share_recv,
):
    sub, grp = lax.axis_index("sub"), lax.axis_index("grp")
    right, left = lax.rem(sub + 1, NSUB), lax.rem(sub + NSUB - 1, NSUB)
    y, core = lax.div(grp, 2), lax.rem(grp, 2)
    mate = 2 * y + 1 - core
    up, down, far = lax.rem(y + 1, NY), lax.rem(y + 3, NY), lax.rem(y + 2, NY)
    to_right, to_left, to_mate = {"sub": right}, {"sub": left}, {"grp": mate}
    to_up, to_down = {"grp": 2 * up + core}, {"grp": 2 * down + core}

    barrier = pltpu.get_barrier_semaphore()
    for i in range(1, NGRP):
        pl.semaphore_signal(barrier, inc=1, device_id={"grp": lax.rem(grp + i, NGRP)}, device_id_type=MESH)
    for i in range(1, NSUB):
        pl.semaphore_signal(barrier, inc=1, device_id={"sub": lax.rem(sub + i, NSUB)}, device_id_type=MESH)

    loads = [
        pltpu.make_async_copy(map_h.at[0], cmt.at[grp], load_sem.at[0]),
        pltpu.make_async_copy(rhs_h.at[0], rhs_v.at[pl.ds(1, SUBS)], load_sem.at[1]),
        pltpu.make_async_copy(coarse_h.at[0], ci, load_sem.at[2]),
        pltpu.make_async_copy(dirichlet_h.at[0], dm, load_sem.at[3]),
        pltpu.make_async_copy(coupling_h.at[0], cext.at[pl.ds(1, SUBS)], load_sem.at[4]),
        pltpu.make_async_copy(solve_h.at[0], sc.at[:, pl.ds(0, PS)], load_sem.at[5]),
    ]
    for load in loads:
        load.start()

    def map_copy(i):
        peer = lax.rem(grp + i, NGRP)
        return remote(map_h.at[0], cmt.at[grp], cm_send.at[i], cm_recv.at[i], {"grp": peer})

    def map_arrival(i):
        slot = lax.rem(grp + NGRP - i, NGRP)
        return remote(map_h.at[0], cmt.at[slot], cm_send.at[i], cm_recv.at[i], to_mate)

    count_copy = remote(cnt.at[0], cnt.at[1], misc_send.at[0], misc_recv.at[0], to_right)
    cpl_right = remote(
        coupling_h.at[0, SUBS - 1, :, pl.ds(H, H)], cext.at[0, :, pl.ds(H, H)],
        misc_send.at[1], misc_recv.at[1], to_right,
    )
    cpl_left = remote(
        coupling_h.at[0, 0, :, pl.ds(0, H)], cext.at[SUBS + 1, :, pl.ds(0, H)],
        misc_send.at[2], misc_recv.at[2], to_left,
    )

    def mate_copy(q, mine=True):
        part = a_part.at[core if mine else 1 - core, q]
        return remote(part, part, misc_send.at[3 + q], misc_recv.at[3 + q], to_mate)

    def ring(stage, q):
        upward = (q < 2) == (stage != 1)
        if stage == 0:
            source, target = g_part.at[far, q], ring_a.at[q]
        else:
            source, target = g_part.at[up if upward else down, q], ring_b.at[0 if upward else 1, q]
        return remote(
            source, target, ring_send.at[stage, q], ring_recv.at[stage, q], to_up if upward else to_down
        )

    def halo_copy(k):
        part = pl.ds(LANES * k, LANES)
        return remote(
            rhs_h.at[0, SUBS - 1, part], rhs_v.at[0, part], halo_send.at[k], halo_recv.at[k], to_right
        )

    def face_left(op, k):
        return remote(
            wb.at[op % 2, k, 0, pl.ds(0, H)], from_right.at[op, k],
            ex_send.at[op, LEFT, k], ex_recv.at[op, LEFT, k], to_left,
        )

    def face_right(op, k):
        return remote(
            wb.at[op % 2, k, SUBS - 1, pl.ds(H, H)], from_left.at[op, k],
            ex_send.at[op, RIGHT, k], ex_recv.at[op, RIGHT, k], to_right,
        )

    def back_left(f, k):
        return remote(
            bext.at[f, k, pl.ds(NC, NC)], bext.at[f, k, pl.ds(NC + OWN, NC)],
            bk_send.at[f, LEFT, k], bk_recv.at[f, LEFT, k], to_left,
        )

    def back_right(f, k):
        return remote(
            bext.at[f, k, pl.ds(OWN, NC)], bext.at[f, k, pl.ds(0, NC)],
            bk_send.at[f, RIGHT, k], bk_recv.at[f, RIGHT, k], to_right,
        )

    def corner_link(f, k, i, part, device):
        return remote(part, part, ag_send.at[f, k, i], ag_recv.at[f, k, i], device)

    def corner_slot(f, k, chip, mine=True):
        return corners.at[f, k, 2 * chip + (core if mine else 1 - core)]

    def corner_copy(f, k, i):
        device = to_mate if i == 0 else {"grp": 2 * lax.rem(y + i, NY) + core}
        return corner_link(f, k, i, corner_slot(f, k, y), device)

    def corner_arrival(f, k, i):
        return corner_link(f, k, i, corner_slot(f, k, lax.rem(y + NY - i, NY), i > 0), to_mate)

    def corner_forward(f, k, i, mine=True):
        return corner_link(f, k, NY - 1 + i, corner_slot(f, k, lax.rem(y + NY - i, NY), mine), to_mate)

    def sum_a(t, i):
        mine = red_a.at[t, grp]
        return remote(mine, mine, ra_send.at[t, i], ra_recv.at[t, i], {"grp": lax.rem(grp + i, NGRP)})

    def sum_a_arrival(t, i):
        there = red_a.at[t, lax.rem(grp + NGRP - i, NGRP)]
        return remote(there, there, ra_send.at[t, i], ra_recv.at[t, i], to_mate)

    def sum_b(t, i):
        mine = red_b.at[t, sub]
        return remote(mine, mine, rb_send.at[t, i], rb_recv.at[t, i], {"sub": lax.rem(sub + i, NSUB)})

    def sum_b_arrival(t, i):
        there = red_b.at[t, lax.rem(sub + NSUB - i, NSUB)]
        return remote(there, there, rb_send.at[t, i], rb_recv.at[t, i], to_right)


    def panel_rows(op, k, j, first, count):
        panel = (sc if op % 2 == 1 else dm)[j, pl.ds(first, count)]
        both = jnp.dot(panel, vs[k, pl.ds(H * j, PS), :], preferred_element_type=F32)
        return both[:, :LANES] + both[:, LANES:]

    def put_corner(op, k, j, both):
        f = op // 2
        values = both[:NC] + both[NC:]
        cown[f, k, pl.ds(NC * j, NC)] = values
        corners[f, k, grp, pl.ds(NC * j, NC)] = values

    def apply_panel(op, k, j):
        both = panel_rows(op, k, j, 0, PS + (2 * NC if op % 2 == 1 else 0))
        wb[op % 2, k, j] = both[:PS]
        if op % 2 == 1:
            put_corner(op, k, j, both[PS:])

    def apply_half(op, k, j, half):
        wb[op % 2, k, j, block(half)] = panel_rows(op, k, j, H * half, H)

    def put_faces(k, pairs, value):
        for i in pairs:
            high, low = split(value(k, i))
            vs[k, block(i), pl.ds(0, LANES)] = high
            vs[k, block(i), pl.ds(LANES, LANES)] = low

    def inner(op, value):
        for k in range(CHUNKS):
            put_faces(k, range(1, SUBS), value)
            apply_panel(op, k, 1)
            apply_panel(op, k, 2)

    def outer(op, value, last=False, parts=range(CHUNKS)):
        for k in parts:
            if op > 0:
                arrive(op - 1, k)
            if op >= 2:
                face_left(op - 2, k).wait_send()
                face_right(op - 2, k).wait_send()
            put_faces(k, (0, SUBS), value)
            if op % 2 == 1:
                for j in (0, SUBS - 1):
                    put_corner(op, k, j, panel_rows(op, k, j, PS, 2 * NC))
                for i in (2, 1, 3, 0):
                    corner_copy(op // 2, k, i).start()
            apply_half(op, k, 0, 0)
            face_left(op, k).start()
            apply_half(op, k, SUBS - 1, 1)
            if not last:
                face_right(op, k).start()
            apply_half(op, k, 0, 1)
            apply_half(op, k, SUBS - 1, 0)

    def gather(f, k):
        for i in (1, 3, 2):
            corner_arrival(f, k, i).wait_recv()
            corner_forward(f, k, i).start()

    def gathered(f, k):
        corner_arrival(f, k, 0).wait_recv()
        for i in range(1, NY):
            corner_forward(f, k, i, False).wait_recv()
        high, low = split(corners[f, k].reshape(NGRP * OWN, LANES))
        return jnp.concatenate([high, low], axis=1)

    def quadrants(rows, values):
        both = jnp.dot(rows, values, preferred_element_type=F32)
        both = both[:, :LANES] + both[:, LANES:]
        return both[:OWN] + both[OWN:]

    def share_copy(k, step):
        chip = lax.rem(y + step, NY)
        return remote(
            shared.at[k, chip], shares.at[k, y], share_send.at[k, step], share_recv.at[k, step],
            {"grp": 2 * chip + core},
        )

    def share_arrival(k, step):
        there = shares.at[k, lax.rem(y + NY - step, NY)]
        return remote(there, there, share_send.at[k, step], share_recv.at[k, step], to_mate)

    def scatter(k):
        values = gathered(0, k)
        for step in (2, 1, 3, 0):
            chip = lax.rem(y + step, NY)
            shared[k, chip] = quadrants(ps[chip], values)
            if step:
                share_copy(k, step).start()

    def collect(k):
        total = shared[k, y]
        for step in range(1, NY):
            share_arrival(k, step).wait_recv()
            total = total + shares[k, lax.rem(y + NY - step, NY)]
        bext[0, k, pl.ds(NC, OWN)] = total
        back_left(0, k).start()
        back_right(0, k).start()

    def coarse(f, k, last=False):
        bext[f, k, pl.ds(NC, OWN)] = quadrants(gs[...], gathered(f, k))
        back_left(f, k).start()
        if not last:
            back_right(f, k).start()

    def all_coarse(f, last=False):
        for k in range(CHUNKS):
            gather(f, k)
        for k in range(CHUNKS):
            coarse(f, k, last)

    def image(op, k, i):
        before = from_left[op, k] if i == 0 else wb[op % 2, k, i - 1, pl.ds(H, H)]
        after = from_right[op, k] if i == SUBS else wb[op % 2, k, i, pl.ds(0, H)]
        value = before + after
        if op % 2 == 1:
            high, low = split(bext[op // 2, k, pl.ds(NC * i, 2 * NC)])
            faces = jnp.concatenate([high, low, high, low], axis=0)
            value = value + jnp.dot(ext[i], faces, preferred_element_type=F32)
        else:
            value = 0.25 * value
        return jnp.where(mask[i] > 0.0, value, 0.0)

    def arrive(op, k, last=False):
        face_left(op, k).wait_recv()
        if op % 2 == 1:
            back_left(op // 2, k).wait_recv()
        if not last:
            face_right(op, k).wait_recv()
            if op % 2 == 1:
                back_right(op // 2, k).wait_recv()

    def image_in(op, out):
        def value(k, i):
            result = image(op, k, i)
            out[k, block(i)] = result
            return result

        return value

    def product(first, second, k):
        return colsum(first[k, pl.ds(H, SUBS * H)] * second[k, pl.ds(H, SUBS * H)])

    def put_sums(t, k, values):
        for i, value in enumerate(values):
            red_a[t, grp, pl.ds(3 * k + i, 1)] = value

    def send_sums(t):
        for i in range(1, NGRP):
            sum_a(t, i).start()

    def pass_sums(t):
        for i in range(1, NGRP):
            sum_a_arrival(t, i).wait_recv()
        red_b[t, sub] = jnp.sum(red_a[t], axis=0)
        for i in range(1, NSUB):
            sum_b(t, i).start()

    def get_sums(t):
        for i in range(1, NSUB):
            sum_b_arrival(t, i).wait_recv()
        total = jnp.sum(red_b[t], axis=0)
        return [[total[3 * k + i : 3 * k + i + 1] for i in range(3)] for k in range(CHUNKS)]

    live = [counts_s[0, c] for c in range(SUBS)]
    live[SUBS - 1] = jnp.where(sub == NSUB - 1, 0, live[SUBS - 1])
    cnt[0] = jnp.full((8, LANES), live[SUBS - 1], I32)
    red_a[...] = jnp.zeros_like(red_a)
    pl.semaphore_wait(barrier, NGRP + NSUB - 2)
    for i in range(1, NGRP):
        map_copy(i).start()
    count_copy.start()
    chunks(lambda k: halo_copy(k).start())
    cpl_right.start()
    cpl_left.start()

    loads[2].wait()
    for i in range(4):
        high, low = split(ci[pl.ds(64 * i, 64)])
        cis[pl.ds(64 * i, 64)] = high
        cis[pl.ds(256 + 64 * i, 64)] = low
    rows = lax.broadcasted_iota(I32, (H, LANES), 0)
    for c in range(SUBS):
        mask[c + 1] = (rows < live[c]).astype(F32)
    loads[1].wait()
    for c in range(SUBS):
        turned = rhs_v[c + 1].T
        for k in range(CHUNKS):
            r[k, block(c + 1)] = jnp.where(
                mask[c + 1] > 0.0, turned[:, LANES * k : LANES * (k + 1)], 0.0
            )

    loads[3].wait()
    for j in range(SUBS):
        for a, b in ((0, 1), (1, 0)):
            dm[j, block(a), block(b)] = -dm[j, block(a), block(b)]

    def residual(k, i):
        if i == 0:
            halo_copy(k).wait_recv()
            turned = rhs_v[0, pl.ds(LANES * k, LANES)].T
            r[k, block(0)] = jnp.where(mask[0] > 0.0, turned, 0.0)
        return r[k, block(i)]

    inner(0, residual)

    loads[0].wait()
    for i in range(1, NGRP):
        map_arrival(i).wait_recv()

    def map_row(g):
        return jnp.concatenate([cmt[g, pl.ds(c, 1)] for c in range(SUBS)], axis=1)

    def fill(onehot, q):
        for c in range(2):
            wanted = map_row(2 * q + c)
            for t in range(NCO // 256):
                hit = rows + 256 * t == wanted
                onehot[pl.ds(256 * t, 256), pl.ds(LANES * c, LANES)] = hit.astype(F32).astype(BF16)

    slots = (onehot_a, onehot_b)
    order = (0, 2, 1, 3)

    def columns(n):
        q, onehot = order[n], slots[n % 2]
        both = jnp.dot(cis[...], onehot[...], preferred_element_type=F32)
        a_part[core, q] = both[:256] + both[256:]
        mate_copy(q).start()

    def rows_of(n):
        q = order[n]
        mate_copy(q, False).wait_recv()
        for c in range(2):
            high, low = split(a_part[c, q])
            a_split[q, block(c), pl.ds(0, 256)] = high
            a_split[q, block(c), pl.ds(256, 256)] = low
        both = jnp.dot(rowhot[...], a_split[q], preferred_element_type=F32)
        both = both[:, :256] + both[:, 256:]
        for chip in range(NY):
            part = both[LANES * chip : LANES * (chip + 1)]
            g_part[chip, q] = part
            high, low = split(part)
            ps[chip, pl.ds(0, OWN), pl.ds(256 * q, 256)] = high
            ps[chip, pl.ds(OWN, OWN), pl.ds(256 * q, 256)] = low

    def add_row(q):
        ring(0, q).wait_recv()
        there = (up if q < 2 else down, q)
        g_part[there] = g_part[there] + ring_a[q]
        ring(2, q).start()

    fill(onehot_a, order[0])
    fill(onehot_b, order[1])
    columns(0)
    lane = lax.broadcasted_iota(I32, (LANES, LANES), 1).astype(F32)
    base = (2 * 256 * y).astype(F32)
    for q in range(NY):
        wanted = jnp.broadcast_to(map_row(2 * q + core), (LANES, LANES)).astype(F32).T
        for t in range(4):
            rowhot[pl.ds(LANES * q, LANES), pl.ds(LANES * t, LANES)] = (
                wanted == lane + (base + 128.0 * t)
            ).astype(F32).astype(BF16)
    fill(onehot_a, order[2])
    columns(1)
    rows_of(0)
    fill(onehot_b, order[3])
    columns(2)
    count_copy.wait_recv()
    mask[0] = (rows < cnt[1, pl.ds(0, 1)]).astype(F32)
    outer(0, residual, parts=(0,))
    rows_of(1)
    columns(3)
    outer(0, residual, parts=(1,))
    rows_of(2)
    rows_of(3)

    loads[5].wait()
    loads[4].wait()
    cpl_right.wait_recv()
    cpl_left.wait_recv()
    for j in range(SUBS):
        for a, b in ((0, 1), (1, 0)):
            sc[j, block(a), block(b)] = -sc[j, block(a), block(b)]
        for half in range(2):
            part = cext[j + 1, :, block(half)]
            high, low = split(part if half else -part)
            sc[j, pl.ds(PS, NC), block(half)] = high
            sc[j, pl.ds(PS + NC, NC), block(half)] = low

    inner(1, image_in(0, u))
    outer(1, image_in(0, u))
    for i in range(PAIRS):
        both = jnp.concatenate([cext[i, :, block(1)], -cext[i + 1, :, block(0)]], axis=0)
        high = both.astype(BF16).astype(F32)
        low = both - high
        ext[i] = jnp.concatenate([high, high, low, low], axis=0).T.astype(BF16)
    chunks(lambda k: gather(0, k))
    chunks(scatter)
    for q in order:
        ring(0, q).start()
        ring(1, q).start()
    chunks(collect)

    inner(2, image_in(1, w))
    outer(2, image_in(1, w))
    chunks(lambda k: put_sums(0, k, [product(r, u, k), product(u, w, k)]))
    send_sums(0)
    inner(3, image_in(2, m0))
    pass_sums(0)
    for q in order:
        add_row(q)
    outer(3, image_in(2, m0))
    for q in range(NY):
        ring(1, q).wait_recv()
        ring(2, q).wait_recv()
        high, low = split(g_part[y, q] + ring_b[0, q] + ring_b[1, q])
        gs[pl.ds(0, OWN), pl.ds(256 * q, 256)] = high
        gs[pl.ds(OWN, OWN), pl.ds(256 * q, 256)] = low
    all_coarse(1)
    rz0, den0, alpha0 = [], [], []
    for rz, uw, _ in get_sums(0):
        rz0.append(rz)
        den0.append(uw)
        alpha0.append(rz / uw)

    def lowered(k, i):
        here = (k, block(i))
        s[here] = w[here]
        n0[here] = image(3, k, i)
        w[here] = w[here] - alpha0[k] * n0[here]
        return w[here]

    inner(4, lowered)
    outer(4, lowered)

    def fifth(k):
        for i in range(PAIRS):
            here = (k, block(i))
            p[here] = u[here]
            x[here] = alpha0[k] * u[here]
            r[here] = r[here] - alpha0[k] * s[here]
            u[here] = u[here] - alpha0[k] * m0[here]
        put_sums(1, k, [product(r, u, k), product(u, w, k), product(u, s, k)])

    chunks(fifth)
    send_sums(1)
    inner(5, image_in(4, m1))
    pass_sums(1)
    outer(5, image_in(4, m1), last=True)
    rz1, den1, alpha1 = [], [], []
    beta1 = []
    for k, (rz, uw, us) in enumerate(get_sums(1)):
        beta = rz / rz0[k]
        den = uw + beta * (us + us) + beta * beta * den0[k]
        rz1.append(rz)
        den1.append(den)
        beta1.append(beta)
        alpha1.append(rz / den)

    partial = []

    def seventh(k):
        alpha, beta = alpha1[k], beta1[k]
        for i in range(PAIRS):
            here = (k, block(i))
            p[here] = u[here] + beta * p[here]
            s[here] = w[here] + beta * s[here]
            x[here] = x[here] + alpha * p[here]
            r[here] = r[here] - alpha * s[here]
            u[here] = u[here] - alpha * (m1[here] + beta * m0[here])
            w[here] = w[here] - (alpha * beta) * n0[here]
        faces = jnp.zeros((1, LANES), F32)
        for j in range(SUBS):
            faces = faces + colsum(u[k, pl.ds(H * j, PS)] * wb[1, k, j])
        partial.append([product(r, u, k), product(u, w, k), product(u, s, k), faces])

    chunks(seventh)
    all_coarse(2, last=True)
    for k in range(CHUNKS):
        corner = cown[0, k] - alpha0[k] * cown[1, k] - alpha1[k] * (cown[2, k] + beta1[k] * cown[1, k])
        ru, uw, us, faces = partial[k]
        faces = faces + colsum(corner * bext[2, k, pl.ds(NC, OWN)])
        put_sums(2, k, [ru, uw - alpha1[k] * faces, us])
    send_sums(2)

    for i in range(1, NGRP):
        map_copy(i).wait_send()
    for copy in (count_copy, cpl_right, cpl_left):
        copy.wait_send()
    for q in range(NY):
        mate_copy(q).wait_send()
        for stage in range(3):
            ring(stage, q).wait_send()
    for t in range(2):
        for i in range(1, NGRP):
            sum_a(t, i).wait_send()
    pass_sums(2)

    def under(k):
        arrive(5, k, last=True)
        for i in range(1, PAIRS):
            here = (k, block(i))
            w[here] = w[here] - alpha1[k] * image(5, k, i)

    chunks(under)

    def drain(k):
        halo_copy(k).wait_send()
        for step in range(1, NY):
            share_copy(k, step).wait_send()
        face_left(4, k).wait_send()
        face_right(4, k).wait_send()
        face_left(5, k).wait_send()
        for f in range(3):
            back_left(f, k).wait_send()
            if f < 2:
                back_right(f, k).wait_send()
            for i in range(NY):
                corner_copy(f, k, i).wait_send()
            for i in range(1, NY):
                corner_forward(f, k, i).wait_send()

    chunks(drain)
    for t in range(2):
        for i in range(1, NSUB):
            sum_b(t, i).wait_send()
    for i in range(1, NGRP):
        sum_a(2, i).wait_send()

    stores = []
    for k, (rz, uw, us) in enumerate(get_sums(2)):
        beta = rz / rz1[k]
        den = uw + beta * (us + us) + beta * beta * den1[k]
        alpha = rz / den
        for i in range(1, PAIRS):
            here = (k, block(i))
            x[here] = x[here] + alpha * (u[here] + beta * p[here])
            r[here] = r[here] - alpha * (w[here] + beta * s[here])
        own = (k, pl.ds(H, SUBS * H))
        stores.append(pltpu.make_async_copy(x.at[own], x_h.at[k], load_sem.at[6 + 2 * k]))
        stores.append(pltpu.make_async_copy(r.at[own], res_h.at[k], load_sem.at[7 + 2 * k]))
        stores[-2].start()
        stores[-1].start()
    for i in range(1, NSUB):
        sum_b(2, i).wait_send()
    for copy in stores:
        copy.wait()


def turn(x_h, r_h, x_out, r_out, taken, given, load_sem, store_sem):
    def load(side, c):
        source = (x_h, r_h)[side].at[:, block(c)]
        return pltpu.make_async_copy(source, taken.at[side, c], load_sem.at[side, c])

    def store(side, c):
        target = (x_out, r_out)[side].at[0, c]
        return pltpu.make_async_copy(given.at[side, c], target, store_sem.at[side, c])

    parts = [(side, c) for c in range(SUBS) for side in range(2)]
    for part in parts:
        load(*part).start()
    for side, c in parts:
        load(side, c).wait()
        for k in range(CHUNKS):
            given[side, c, pl.ds(LANES * k, LANES)] = taken[side, c, k].T
        store(side, c).start()
    for part in parts:
        store(*part).wait()


def local(rhs, counts, solve_panel, dirichlet_panel, coupling, corner_map, coarse_inverse):
    vector = pltpu.VMEM((CHUNKS, PAIRS * H, LANES), F32)
    dma = pltpu.SemaphoreType.DMA
    anywhere = pl.BlockSpec(memory_space=pl.ANY)
    shape = jax.ShapeDtypeStruct((CHUNKS, SUBS * H, LANES), F32)
    x_turned, r_turned = pl.pallas_call(
        kernel,
        out_shape=(shape, shape),
        in_specs=[anywhere, pl.BlockSpec(memory_space=pltpu.SMEM)] + [anywhere] * 5,
        out_specs=(anywhere, anywhere),
        scratch_shapes=[
            pltpu.VMEM((PAIRS, 256, H), F32),
            pltpu.VMEM((SUBS, PS + 2 * NC, PS), BF16),
            pltpu.VMEM((SUBS, PS, PS), BF16),
            pltpu.VMEM((SUBS + 2, NC, PS), F32),
            pltpu.VMEM((256, NCO), F32),
            pltpu.VMEM((512, NCO), BF16),
            pltpu.VMEM((NGRP, SUBS, NC), I32),
            pltpu.VMEM((2, 8, LANES), I32),
            pltpu.VMEM((NCO, 256), BF16),
            pltpu.VMEM((NCO, 256), BF16),
            pltpu.VMEM((512, 512), BF16),
            pltpu.VMEM((2, NY, 256, 256), F32),
            pltpu.VMEM((NY, 512, 512), BF16),
            pltpu.VMEM((NY, NY, OWN, 256), F32),
            pltpu.VMEM((NY, OWN, 256), F32),
            pltpu.VMEM((2, NY, OWN, 256), F32),
            pltpu.VMEM((2 * OWN, NGRP * OWN), BF16),
            pltpu.VMEM((NY, 2 * OWN, NGRP * OWN), BF16),
            pltpu.VMEM((CHUNKS, NY, OWN, LANES), F32),
            pltpu.VMEM((CHUNKS, NY, OWN, LANES), F32),
            pltpu.VMEM((PAIRS, H, 8 * NC), BF16),
            pltpu.VMEM((PAIRS, H, LANES), F32),
            vector, vector, vector, vector, vector, vector, vector, vector, vector,
            pltpu.VMEM((CHUNKS, PAIRS * H, 2 * LANES), BF16),
            pltpu.VMEM((2, CHUNKS, SUBS, PS, LANES), F32),
            pltpu.VMEM((6, CHUNKS, H, LANES), F32),
            pltpu.VMEM((6, CHUNKS, H, LANES), F32),
            pltpu.VMEM((3, CHUNKS, NGRP, OWN, LANES), F32),
            pltpu.VMEM((3, CHUNKS, OWN, LANES), F32),
            pltpu.VMEM((3, CHUNKS, OWN + 2 * NC, LANES), F32),
            pltpu.VMEM((3, NGRP, 8, LANES), F32),
            pltpu.VMEM((3, NSUB, 8, LANES), F32),
            dma((10,)), dma((NGRP,)), dma((NGRP,)), dma((7,)), dma((7,)), dma((CHUNKS,)), dma((CHUNKS,)),
            dma((6, 2, CHUNKS)), dma((6, 2, CHUNKS)), dma((3, 2, CHUNKS)), dma((3, 2, CHUNKS)),
            dma((3, CHUNKS, 7)), dma((3, CHUNKS, 7)),
            dma((3, NGRP)), dma((3, NGRP)), dma((3, NSUB)), dma((3, NSUB)), dma((3, NY)), dma((3, NY)),
            dma((CHUNKS, NY)), dma((CHUNKS, NY)),
        ],
        compiler_params=pltpu.CompilerParams(
            collective_id=0, has_side_effects=True, vmem_limit_bytes=66_000_000
        ),
    )(rhs, counts, solve_panel, dirichlet_panel, coupling, corner_map, coarse_inverse)
    out = jax.ShapeDtypeStruct(rhs.shape, F32)
    return pl.pallas_call(
        turn,
        out_shape=(out, out),
        in_specs=[anywhere, anywhere],
        out_specs=(anywhere, anywhere),
        scratch_shapes=[
            pltpu.VMEM((2, SUBS, CHUNKS, H, LANES), F32),
            pltpu.VMEM((2, SUBS, CHUNKS * LANES, H), F32),
            dma((2, SUBS)), dma((2, SUBS)),
        ],
    )(x_turned, r_turned)


def solution(mesh):
    return jax.shard_map(
        local,
        mesh=mesh,
        in_specs=(
            P("grp", "sub", None, None),
            P("grp", "sub"),
            P("grp", "sub", None, None),
            P("grp", "sub", None, None),
            P("grp", "sub", None, None),
            P("grp", "sub", None),
            P("sub", "grp", None),
        ),
        out_specs=(P("grp", "sub", None, None), P("grp", "sub", None, None)),
        check_vma=False,
    )
```

```python
import jax
import jax.numpy as jnp
from jax import lax
from jax.experimental import pallas as pl
from jax.experimental.pallas import tpu as pltpu
from jax.sharding import PartitionSpec as P

MESH = pl.DeviceIdType.MESH
F32, BF16, I32 = jnp.float32, jnp.bfloat16, jnp.int32
NSUB, NGRP, NY = 16, 8, 4
SUBS, H, PS, NC, NCO = 4, 256, 512, 32, 2048
LANES, CHUNKS, PAIRS = 128, 2, 5
OWN = SUBS * NC
LEFT, RIGHT = 0, 1


def remote(src, dst, send_sem, recv_sem, device):
    return pltpu.make_async_remote_copy(
        src_ref=src,
        dst_ref=dst,
        send_sem=send_sem,
        recv_sem=recv_sem,
        device_id=device,
        device_id_type=MESH,
    )


def split(value):
    high = value.astype(BF16)
    low = (value - high.astype(F32)).astype(BF16)
    return high, low


def colsum(value):
    return jnp.sum(value, axis=0, keepdims=True)


def chunks(body):
    for k in range(CHUNKS):
        body(k)


def block(i):
    return pl.ds(H * i, H)


def kernel(
    rhs_h, counts_s, solve_h, dirichlet_h, coupling_h, map_h, coarse_h, x_h, res_h,
    rhs_v, sc, dm, cext, ci, cis, cmt, cnt, onehot_a, onehot_b, rowhot, a_part, a_split, g_part, ring_a, ring_b,
    gs, ext, mask, r, u, w, m0, n0, m1, p, s, x, vs, wb, from_left, from_right, corners, cown, bext, red_a, red_b,
    load_sem, cm_send, cm_recv, misc_send, misc_recv, halo_send, halo_recv, ex_send, ex_recv,
    bk_send, bk_recv, ag_send, ag_recv, ra_send, ra_recv, rb_send, rb_recv, ring_send, ring_recv,
):
    sub, grp = lax.axis_index("sub"), lax.axis_index("grp")
    right, left = lax.rem(sub + 1, NSUB), lax.rem(sub + NSUB - 1, NSUB)
    y, core = lax.div(grp, 2), lax.rem(grp, 2)
    mate = 2 * y + 1 - core
    up, down, far = lax.rem(y + 1, NY), lax.rem(y + 3, NY), lax.rem(y + 2, NY)
    to_right, to_left, to_mate = {"sub": right}, {"sub": left}, {"grp": mate}
    to_up, to_down = {"grp": 2 * up + core}, {"grp": 2 * down + core}

    barrier = pltpu.get_barrier_semaphore()
    for i in range(1, NGRP):
        pl.semaphore_signal(barrier, inc=1, device_id={"grp": lax.rem(grp + i, NGRP)}, device_id_type=MESH)
    for i in range(1, NSUB):
        pl.semaphore_signal(barrier, inc=1, device_id={"sub": lax.rem(sub + i, NSUB)}, device_id_type=MESH)

    loads = [
        pltpu.make_async_copy(map_h.at[0], cmt.at[grp], load_sem.at[0]),
        pltpu.make_async_copy(rhs_h.at[0], rhs_v.at[pl.ds(1, SUBS)], load_sem.at[1]),
        pltpu.make_async_copy(coarse_h.at[0], ci, load_sem.at[2]),
        pltpu.make_async_copy(dirichlet_h.at[0], dm, load_sem.at[3]),
        pltpu.make_async_copy(coupling_h.at[0], cext.at[pl.ds(1, SUBS)], load_sem.at[4]),
        pltpu.make_async_copy(solve_h.at[0], sc.at[:, pl.ds(0, PS)], load_sem.at[5]),
    ]
    for load in loads:
        load.start()

    def map_copy(i):
        peer = lax.rem(grp + i, NGRP)
        return remote(map_h.at[0], cmt.at[grp], cm_send.at[i], cm_recv.at[i], {"grp": peer})

    def map_arrival(i):
        slot = lax.rem(grp + NGRP - i, NGRP)
        return remote(map_h.at[0], cmt.at[slot], cm_send.at[i], cm_recv.at[i], to_mate)

    count_copy = remote(cnt.at[0], cnt.at[1], misc_send.at[0], misc_recv.at[0], to_right)
    cpl_right = remote(
        coupling_h.at[0, SUBS - 1, :, pl.ds(H, H)], cext.at[0, :, pl.ds(H, H)],
        misc_send.at[1], misc_recv.at[1], to_right,
    )
    cpl_left = remote(
        coupling_h.at[0, 0, :, pl.ds(0, H)], cext.at[SUBS + 1, :, pl.ds(0, H)],
        misc_send.at[2], misc_recv.at[2], to_left,
    )

    def mate_copy(q, mine=True):
        part = a_part.at[core if mine else 1 - core, q]
        return remote(part, part, misc_send.at[3 + q], misc_recv.at[3 + q], to_mate)

    def ring(stage, q):
        upward = (q < 2) == (stage != 1)
        if stage == 0:
            source, target = g_part.at[far, q], ring_a.at[q]
        else:
            source, target = g_part.at[up if upward else down, q], ring_b.at[0 if upward else 1, q]
        return remote(
            source, target, ring_send.at[stage, q], ring_recv.at[stage, q], to_up if upward else to_down
        )

    def halo_copy(k):
        part = pl.ds(LANES * k, LANES)
        return remote(
            rhs_h.at[0, SUBS - 1, part], rhs_v.at[0, part], halo_send.at[k], halo_recv.at[k], to_right
        )

    def face_left(op, k):
        return remote(
            wb.at[op % 2, k, 0, pl.ds(0, H)], from_right.at[op, k],
            ex_send.at[op, LEFT, k], ex_recv.at[op, LEFT, k], to_left,
        )

    def face_right(op, k):
        return remote(
            wb.at[op % 2, k, SUBS - 1, pl.ds(H, H)], from_left.at[op, k],
            ex_send.at[op, RIGHT, k], ex_recv.at[op, RIGHT, k], to_right,
        )

    def back_left(f, k):
        return remote(
            bext.at[f, k, pl.ds(NC, NC)], bext.at[f, k, pl.ds(NC + OWN, NC)],
            bk_send.at[f, LEFT, k], bk_recv.at[f, LEFT, k], to_left,
        )

    def back_right(f, k):
        return remote(
            bext.at[f, k, pl.ds(OWN, NC)], bext.at[f, k, pl.ds(0, NC)],
            bk_send.at[f, RIGHT, k], bk_recv.at[f, RIGHT, k], to_right,
        )

    def corner_link(f, k, i, part, device):
        return remote(part, part, ag_send.at[f, k, i], ag_recv.at[f, k, i], device)

    def corner_slot(f, k, chip, mine=True):
        return corners.at[f, k, 2 * chip + (core if mine else 1 - core)]

    def corner_copy(f, k, i):
        device = to_mate if i == 0 else {"grp": 2 * lax.rem(y + i, NY) + core}
        return corner_link(f, k, i, corner_slot(f, k, y), device)

    def corner_arrival(f, k, i):
        return corner_link(f, k, i, corner_slot(f, k, lax.rem(y + NY - i, NY), i > 0), to_mate)

    def corner_forward(f, k, i, mine=True):
        return corner_link(f, k, NY - 1 + i, corner_slot(f, k, lax.rem(y + NY - i, NY), mine), to_mate)

    def sum_a(t, i):
        mine = red_a.at[t, grp]
        return remote(mine, mine, ra_send.at[t, i], ra_recv.at[t, i], {"grp": lax.rem(grp + i, NGRP)})

    def sum_a_arrival(t, i):
        there = red_a.at[t, lax.rem(grp + NGRP - i, NGRP)]
        return remote(there, there, ra_send.at[t, i], ra_recv.at[t, i], to_mate)

    def sum_b(t, i):
        mine = red_b.at[t, sub]
        return remote(mine, mine, rb_send.at[t, i], rb_recv.at[t, i], {"sub": lax.rem(sub + i, NSUB)})

    def sum_b_arrival(t, i):
        there = red_b.at[t, lax.rem(sub + NSUB - i, NSUB)]
        return remote(there, there, rb_send.at[t, i], rb_recv.at[t, i], to_right)


    def panel_rows(op, k, j, first, count):
        panel = (sc if op % 2 == 1 else dm)[j, pl.ds(first, count)]
        both = jnp.dot(panel, vs[k, pl.ds(H * j, PS), :], preferred_element_type=F32)
        return both[:, :LANES] + both[:, LANES:]

    def put_corner(op, k, j, both):
        f = op // 2
        values = both[:NC] + both[NC:]
        cown[f, k, pl.ds(NC * j, NC)] = values
        corners[f, k, grp, pl.ds(NC * j, NC)] = values

    def apply_panel(op, k, j):
        both = panel_rows(op, k, j, 0, PS + (2 * NC if op % 2 == 1 else 0))
        wb[op % 2, k, j] = both[:PS]
        if op % 2 == 1:
            put_corner(op, k, j, both[PS:])

    def apply_half(op, k, j, half):
        wb[op % 2, k, j, block(half)] = panel_rows(op, k, j, H * half, H)

    def put_faces(k, pairs, value):
        for i in pairs:
            high, low = split(value(k, i))
            vs[k, block(i), pl.ds(0, LANES)] = high
            vs[k, block(i), pl.ds(LANES, LANES)] = low

    def inner(op, value):
        for k in range(CHUNKS):
            put_faces(k, range(1, SUBS), value)
            apply_panel(op, k, 1)
            apply_panel(op, k, 2)

    def outer(op, value, last=False, parts=range(CHUNKS)):
        for k in parts:
            if op > 0:
                arrive(op - 1, k)
            if op >= 2:
                face_left(op - 2, k).wait_send()
                face_right(op - 2, k).wait_send()
            put_faces(k, (0, SUBS), value)
            if op % 2 == 1:
                for j in (0, SUBS - 1):
                    put_corner(op, k, j, panel_rows(op, k, j, PS, 2 * NC))
                for i in (2, 1, 3, 0):
                    corner_copy(op // 2, k, i).start()
            apply_half(op, k, 0, 0)
            face_left(op, k).start()
            apply_half(op, k, SUBS - 1, 1)
            if not last:
                face_right(op, k).start()
            apply_half(op, k, 0, 1)
            apply_half(op, k, SUBS - 1, 0)

    def gather(f, k):
        for i in (1, 3, 2):
            corner_arrival(f, k, i).wait_recv()
            corner_forward(f, k, i).start()

    def coarse(f, k, last=False):
        corner_arrival(f, k, 0).wait_recv()
        for i in range(1, NY):
            corner_forward(f, k, i, False).wait_recv()
        high, low = split(corners[f, k].reshape(NGRP * OWN, LANES))
        both = jnp.dot(gs[...], jnp.concatenate([high, low], axis=1), preferred_element_type=F32)
        both = both[:, :LANES] + both[:, LANES:]
        bext[f, k, pl.ds(NC, OWN)] = both[:OWN] + both[OWN:]
        back_left(f, k).start()
        if not last:
            back_right(f, k).start()

    def all_coarse(f, last=False):
        for k in range(CHUNKS):
            gather(f, k)
        for k in range(CHUNKS):
            coarse(f, k, last)

    def image(op, k, i):
        before = from_left[op, k] if i == 0 else wb[op % 2, k, i - 1, pl.ds(H, H)]
        after = from_right[op, k] if i == SUBS else wb[op % 2, k, i, pl.ds(0, H)]
        value = before + after
        if op % 2 == 1:
            high, low = split(bext[op // 2, k, pl.ds(NC * i, 2 * NC)])
            faces = jnp.concatenate([high, low, high, low], axis=0)
            value = value + jnp.dot(ext[i], faces, preferred_element_type=F32)
        else:
            value = 0.25 * value
        return jnp.where(mask[i] > 0.0, value, 0.0)

    def arrive(op, k, last=False):
        face_left(op, k).wait_recv()
        if op % 2 == 1:
            back_left(op // 2, k).wait_recv()
        if not last:
            face_right(op, k).wait_recv()
            if op % 2 == 1:
                back_right(op // 2, k).wait_recv()

    def image_in(op, out):
        def value(k, i):
            result = image(op, k, i)
            out[k, block(i)] = result
            return result

        return value

    def product(first, second, k):
        return colsum(first[k, pl.ds(H, SUBS * H)] * second[k, pl.ds(H, SUBS * H)])

    def put_sums(t, k, values):
        for i, value in enumerate(values):
            red_a[t, grp, pl.ds(3 * k + i, 1)] = value

    def send_sums(t):
        for i in range(1, NGRP):
            sum_a(t, i).start()

    def pass_sums(t):
        for i in range(1, NGRP):
            sum_a_arrival(t, i).wait_recv()
        red_b[t, sub] = jnp.sum(red_a[t], axis=0)
        for i in range(1, NSUB):
            sum_b(t, i).start()

    def get_sums(t):
        for i in range(1, NSUB):
            sum_b_arrival(t, i).wait_recv()
        total = jnp.sum(red_b[t], axis=0)
        return [[total[3 * k + i : 3 * k + i + 1] for i in range(3)] for k in range(CHUNKS)]

    live = [counts_s[0, c] for c in range(SUBS)]
    live[SUBS - 1] = jnp.where(sub == NSUB - 1, 0, live[SUBS - 1])
    cnt[0] = jnp.full((8, LANES), live[SUBS - 1], I32)
    red_a[...] = jnp.zeros_like(red_a)
    pl.semaphore_wait(barrier, NGRP + NSUB - 2)
    for i in range(1, NGRP):
        map_copy(i).start()
    count_copy.start()
    chunks(lambda k: halo_copy(k).start())
    cpl_right.start()
    cpl_left.start()

    loads[2].wait()
    for i in range(4):
        high, low = split(ci[pl.ds(64 * i, 64)])
        cis[pl.ds(64 * i, 64)] = high
        cis[pl.ds(256 + 64 * i, 64)] = low
    rows = lax.broadcasted_iota(I32, (H, LANES), 0)
    for c in range(SUBS):
        mask[c + 1] = (rows < live[c]).astype(F32)
    loads[1].wait()
    for c in range(SUBS):
        turned = rhs_v[c + 1].T
        for k in range(CHUNKS):
            r[k, block(c + 1)] = jnp.where(
                mask[c + 1] > 0.0, turned[:, LANES * k : LANES * (k + 1)], 0.0
            )

    loads[3].wait()
    for j in range(SUBS):
        for a, b in ((0, 1), (1, 0)):
            dm[j, block(a), block(b)] = -dm[j, block(a), block(b)]

    def residual(k, i):
        if i == 0:
            halo_copy(k).wait_recv()
            turned = rhs_v[0, pl.ds(LANES * k, LANES)].T
            r[k, block(0)] = jnp.where(mask[0] > 0.0, turned, 0.0)
        return r[k, block(i)]

    inner(0, residual)

    loads[0].wait()
    for i in range(1, NGRP):
        map_arrival(i).wait_recv()

    def map_row(g):
        return jnp.concatenate([cmt[g, pl.ds(c, 1)] for c in range(SUBS)], axis=1)

    def fill(onehot, q):
        for c in range(2):
            wanted = map_row(2 * q + c)
            for t in range(NCO // 256):
                hit = rows + 256 * t == wanted
                onehot[pl.ds(256 * t, 256), pl.ds(LANES * c, LANES)] = hit.astype(F32).astype(BF16)

    slots = (onehot_a, onehot_b)
    order = (0, 2, 1, 3)

    def columns(n):
        q, onehot = order[n], slots[n % 2]
        both = jnp.dot(cis[...], onehot[...], preferred_element_type=F32)
        a_part[core, q] = both[:256] + both[256:]
        mate_copy(q).start()

    def rows_of(n):
        q = order[n]
        mate_copy(q, False).wait_recv()
        for c in range(2):
            high, low = split(a_part[c, q])
            a_split[q, block(c), pl.ds(0, 256)] = high
            a_split[q, block(c), pl.ds(256, 256)] = low
        both = jnp.dot(rowhot[...], a_split[q], preferred_element_type=F32)
        both = both[:, :256] + both[:, 256:]
        for chip in range(NY):
            g_part[chip, q] = both[LANES * chip : LANES * (chip + 1)]
        ring(0, q).start()
        ring(1, q).start()

    def add_row(q):
        ring(0, q).wait_recv()
        there = (up if q < 2 else down, q)
        g_part[there] = g_part[there] + ring_a[q]
        ring(2, q).start()

    fill(onehot_a, order[0])
    fill(onehot_b, order[1])
    columns(0)
    lane = lax.broadcasted_iota(I32, (LANES, LANES), 1).astype(F32)
    base = (2 * 256 * y).astype(F32)
    for q in range(NY):
        wanted = jnp.broadcast_to(map_row(2 * q + core), (LANES, LANES)).astype(F32).T
        for t in range(4):
            rowhot[pl.ds(LANES * q, LANES), pl.ds(LANES * t, LANES)] = (
                wanted == lane + (base + 128.0 * t)
            ).astype(F32).astype(BF16)
    fill(onehot_a, order[2])
    columns(1)
    rows_of(0)
    fill(onehot_b, order[3])
    columns(2)
    count_copy.wait_recv()
    mask[0] = (rows < cnt[1, pl.ds(0, 1)]).astype(F32)
    outer(0, residual, parts=(0,))
    rows_of(1)
    columns(3)
    outer(0, residual, parts=(1,))
    rows_of(2)
    rows_of(3)

    loads[5].wait()
    loads[4].wait()
    cpl_right.wait_recv()
    cpl_left.wait_recv()
    for j in range(SUBS):
        for a, b in ((0, 1), (1, 0)):
            sc[j, block(a), block(b)] = -sc[j, block(a), block(b)]
        for half in range(2):
            part = cext[j + 1, :, block(half)]
            high, low = split(part if half else -part)
            sc[j, pl.ds(PS, NC), block(half)] = high
            sc[j, pl.ds(PS + NC, NC), block(half)] = low

    inner(1, image_in(0, u))
    add_row(0)
    add_row(2)
    outer(1, image_in(0, u))
    add_row(1)
    add_row(3)
    for i in range(PAIRS):
        both = jnp.concatenate([cext[i, :, block(1)], -cext[i + 1, :, block(0)]], axis=0)
        high = both.astype(BF16).astype(F32)
        low = both - high
        ext[i] = jnp.concatenate([high, high, low, low], axis=0).T.astype(BF16)
    chunks(lambda k: gather(0, k))
    for q in range(NY):
        ring(1, q).wait_recv()
        ring(2, q).wait_recv()
        high, low = split(g_part[y, q] + ring_b[0, q] + ring_b[1, q])
        gs[pl.ds(0, OWN), pl.ds(256 * q, 256)] = high
        gs[pl.ds(OWN, OWN), pl.ds(256 * q, 256)] = low

    chunks(lambda k: coarse(0, k))

    inner(2, image_in(1, w))
    outer(2, image_in(1, w))
    chunks(lambda k: put_sums(0, k, [product(r, u, k), product(u, w, k)]))
    send_sums(0)
    inner(3, image_in(2, m0))
    pass_sums(0)
    outer(3, image_in(2, m0))
    all_coarse(1)
    rz0, den0, alpha0 = [], [], []
    for rz, uw, _ in get_sums(0):
        rz0.append(rz)
        den0.append(uw)
        alpha0.append(rz / uw)

    def lowered(k, i):
        here = (k, block(i))
        s[here] = w[here]
        n0[here] = image(3, k, i)
        w[here] = w[here] - alpha0[k] * n0[here]
        return w[here]

    inner(4, lowered)
    outer(4, lowered)

    def fifth(k):
        for i in range(PAIRS):
            here = (k, block(i))
            p[here] = u[here]
            x[here] = alpha0[k] * u[here]
            r[here] = r[here] - alpha0[k] * s[here]
            u[here] = u[here] - alpha0[k] * m0[here]
        put_sums(1, k, [product(r, u, k), product(u, w, k), product(u, s, k)])

    chunks(fifth)
    send_sums(1)
    inner(5, image_in(4, m1))
    pass_sums(1)
    outer(5, image_in(4, m1), last=True)
    rz1, den1, alpha1 = [], [], []
    beta1 = []
    for k, (rz, uw, us) in enumerate(get_sums(1)):
        beta = rz / rz0[k]
        den = uw + beta * (us + us) + beta * beta * den0[k]
        rz1.append(rz)
        den1.append(den)
        beta1.append(beta)
        alpha1.append(rz / den)

    partial = []

    def seventh(k):
        alpha, beta = alpha1[k], beta1[k]
        for i in range(PAIRS):
            here = (k, block(i))
            p[here] = u[here] + beta * p[here]
            s[here] = w[here] + beta * s[here]
            x[here] = x[here] + alpha * p[here]
            r[here] = r[here] - alpha * s[here]
            u[here] = u[here] - alpha * (m1[here] + beta * m0[here])
            w[here] = w[here] - (alpha * beta) * n0[here]
        faces = jnp.zeros((1, LANES), F32)
        for j in range(SUBS):
            faces = faces + colsum(u[k, pl.ds(H * j, PS)] * wb[1, k, j])
        partial.append([product(r, u, k), product(u, w, k), product(u, s, k), faces])

    chunks(seventh)
    all_coarse(2, last=True)
    for k in range(CHUNKS):
        corner = cown[0, k] - alpha0[k] * cown[1, k] - alpha1[k] * (cown[2, k] + beta1[k] * cown[1, k])
        ru, uw, us, faces = partial[k]
        faces = faces + colsum(corner * bext[2, k, pl.ds(NC, OWN)])
        put_sums(2, k, [ru, uw - alpha1[k] * faces, us])
    send_sums(2)

    for i in range(1, NGRP):
        map_copy(i).wait_send()
    for copy in (count_copy, cpl_right, cpl_left):
        copy.wait_send()
    for q in range(NY):
        mate_copy(q).wait_send()
        for stage in range(3):
            ring(stage, q).wait_send()
    for t in range(2):
        for i in range(1, NGRP):
            sum_a(t, i).wait_send()
    pass_sums(2)

    def under(k):
        arrive(5, k, last=True)
        for i in range(1, PAIRS):
            here = (k, block(i))
            w[here] = w[here] - alpha1[k] * image(5, k, i)

    chunks(under)

    def drain(k):
        halo_copy(k).wait_send()
        face_left(4, k).wait_send()
        face_right(4, k).wait_send()
        face_left(5, k).wait_send()
        for f in range(3):
            back_left(f, k).wait_send()
            if f < 2:
                back_right(f, k).wait_send()
            for i in range(NY):
                corner_copy(f, k, i).wait_send()
            for i in range(1, NY):
                corner_forward(f, k, i).wait_send()

    chunks(drain)
    for t in range(2):
        for i in range(1, NSUB):
            sum_b(t, i).wait_send()
    for i in range(1, NGRP):
        sum_a(2, i).wait_send()

    stores = []
    for k, (rz, uw, us) in enumerate(get_sums(2)):
        beta = rz / rz1[k]
        den = uw + beta * (us + us) + beta * beta * den1[k]
        alpha = rz / den
        for i in range(1, PAIRS):
            here = (k, block(i))
            x[here] = x[here] + alpha * (u[here] + beta * p[here])
            r[here] = r[here] - alpha * (w[here] + beta * s[here])
        own = (k, pl.ds(H, SUBS * H))
        stores.append(pltpu.make_async_copy(x.at[own], x_h.at[k], load_sem.at[6 + 2 * k]))
        stores.append(pltpu.make_async_copy(r.at[own], res_h.at[k], load_sem.at[7 + 2 * k]))
        stores[-2].start()
        stores[-1].start()
    for i in range(1, NSUB):
        sum_b(2, i).wait_send()
    for copy in stores:
        copy.wait()


def turn(x_h, r_h, x_out, r_out, taken, given, load_sem, store_sem):
    def load(side, c):
        source = (x_h, r_h)[side].at[:, block(c)]
        return pltpu.make_async_copy(source, taken.at[side, c], load_sem.at[side, c])

    def store(side, c):
        target = (x_out, r_out)[side].at[0, c]
        return pltpu.make_async_copy(given.at[side, c], target, store_sem.at[side, c])

    parts = [(side, c) for c in range(SUBS) for side in range(2)]
    for part in parts:
        load(*part).start()
    for side, c in parts:
        load(side, c).wait()
        for k in range(CHUNKS):
            given[side, c, pl.ds(LANES * k, LANES)] = taken[side, c, k].T
        store(side, c).start()
    for part in parts:
        store(*part).wait()


def local(rhs, counts, solve_panel, dirichlet_panel, coupling, corner_map, coarse_inverse):
    vector = pltpu.VMEM((CHUNKS, PAIRS * H, LANES), F32)
    dma = pltpu.SemaphoreType.DMA
    anywhere = pl.BlockSpec(memory_space=pl.ANY)
    shape = jax.ShapeDtypeStruct((CHUNKS, SUBS * H, LANES), F32)
    x_turned, r_turned = pl.pallas_call(
        kernel,
        out_shape=(shape, shape),
        in_specs=[anywhere, pl.BlockSpec(memory_space=pltpu.SMEM)] + [anywhere] * 5,
        out_specs=(anywhere, anywhere),
        scratch_shapes=[
            pltpu.VMEM((PAIRS, 256, H), F32),
            pltpu.VMEM((SUBS, PS + 2 * NC, PS), BF16),
            pltpu.VMEM((SUBS, PS, PS), BF16),
            pltpu.VMEM((SUBS + 2, NC, PS), F32),
            pltpu.VMEM((256, NCO), F32),
            pltpu.VMEM((512, NCO), BF16),
            pltpu.VMEM((NGRP, SUBS, NC), I32),
            pltpu.VMEM((2, 8, LANES), I32),
            pltpu.VMEM((NCO, 256), BF16),
            pltpu.VMEM((NCO, 256), BF16),
            pltpu.VMEM((512, 512), BF16),
            pltpu.VMEM((2, NY, 256, 256), F32),
            pltpu.VMEM((NY, 512, 512), BF16),
            pltpu.VMEM((NY, NY, OWN, 256), F32),
            pltpu.VMEM((NY, OWN, 256), F32),
            pltpu.VMEM((2, NY, OWN, 256), F32),
            pltpu.VMEM((2 * OWN, NGRP * OWN), BF16),
            pltpu.VMEM((PAIRS, H, 8 * NC), BF16),
            pltpu.VMEM((PAIRS, H, LANES), F32),
            vector, vector, vector, vector, vector, vector, vector, vector, vector,
            pltpu.VMEM((CHUNKS, PAIRS * H, 2 * LANES), BF16),
            pltpu.VMEM((2, CHUNKS, SUBS, PS, LANES), F32),
            pltpu.VMEM((6, CHUNKS, H, LANES), F32),
            pltpu.VMEM((6, CHUNKS, H, LANES), F32),
            pltpu.VMEM((3, CHUNKS, NGRP, OWN, LANES), F32),
            pltpu.VMEM((3, CHUNKS, OWN, LANES), F32),
            pltpu.VMEM((3, CHUNKS, OWN + 2 * NC, LANES), F32),
            pltpu.VMEM((3, NGRP, 8, LANES), F32),
            pltpu.VMEM((3, NSUB, 8, LANES), F32),
            dma((10,)), dma((NGRP,)), dma((NGRP,)), dma((7,)), dma((7,)), dma((CHUNKS,)), dma((CHUNKS,)),
            dma((6, 2, CHUNKS)), dma((6, 2, CHUNKS)), dma((3, 2, CHUNKS)), dma((3, 2, CHUNKS)),
            dma((3, CHUNKS, 7)), dma((3, CHUNKS, 7)),
            dma((3, NGRP)), dma((3, NGRP)), dma((3, NSUB)), dma((3, NSUB)), dma((3, NY)), dma((3, NY)),
        ],
        compiler_params=pltpu.CompilerParams(
            collective_id=0, has_side_effects=True, vmem_limit_bytes=66_000_000
        ),
    )(rhs, counts, solve_panel, dirichlet_panel, coupling, corner_map, coarse_inverse)
    out = jax.ShapeDtypeStruct(rhs.shape, F32)
    return pl.pallas_call(
        turn,
        out_shape=(out, out),
        in_specs=[anywhere, anywhere],
        out_specs=(anywhere, anywhere),
        scratch_shapes=[
            pltpu.VMEM((2, SUBS, CHUNKS, H, LANES), F32),
            pltpu.VMEM((2, SUBS, CHUNKS * LANES, H), F32),
            dma((2, SUBS)), dma((2, SUBS)),
        ],
    )(x_turned, r_turned)


def solution(mesh):
    return jax.shard_map(
        local,
        mesh=mesh,
        in_specs=(
            P("grp", "sub", None, None),
            P("grp", "sub"),
            P("grp", "sub", None, None),
            P("grp", "sub", None, None),
            P("grp", "sub", None, None),
            P("grp", "sub", None),
            P("sub", "grp", None),
        ),
        out_specs=(P("grp", "sub", None, None), P("grp", "sub", None, None)),
        check_vma=False,
    )
```
